32 devices in a mesh: row: 2 (over core), col: 16 (over z, y, x).
Axes of the slice: x: 2, y: 2, z: 4, core: 2. Of those that a mesh axis runs over, the one named last changes fastest.
Arguments:
- object_field: float32 [2, 2, 512, 4096], P(None, None, 'row', 'col'), may hold values from -5 to 5
- probe: float32 [2, 256, 256], replicated, may hold values from -5 to 5
- phase: float32 [256, 256], replicated, may hold values from -3.140625 to 3.140625
- amplitudes: float32 [2, 16, 1, 256, 256], P('row', 'col'), may hold values from 0.2 to 3
- offsets: int32 [2, 16, 1, 2], P('row', 'col'), may hold values from 0 to 128, as said below
Outputs:
- object_grad: float32 [2, 2, 512, 4096], P(None, None, 'row', 'col')
- probe_grad: float32 [2, 256, 256], replicated
The draws below stay inside these ranges and needn't reach their ends.
Inputs may be any that keep to these rules, and one draw needn't show every extreme that they name: `offsets`: every offset lies between 0 and 128; in every draw some offset is 0 and some offset is 128.
All inputs are finite; a program needn't handle non-finite values.
Results may differ from the reference program's by a relative error of at most 0.0003.
Values sent between devices are 32-bit elements; how exact they have to be, the bound alone decides.
No kernel may reach another device: no remote copies, remote signals or barrier semaphores. Data moves between devices by JAX's collectives and lax.ppermute only.
A program may use at most 64 MiB of HBM per device.

```python
import math
import jax
import jax.numpy as jnp
from jax import lax

N = 256
POS = 1
HALO = 64
GRID_R = 2
GRID_C = 16
HEIGHT = 512
WIDTH = 4096


def draw_offsets(key, part):
    total = GRID_R * GRID_C * POS * 2
    values = jax.random.randint(key, (total,), 0, 2 * HALO + 1, dtype=jnp.int32)
    order = jax.random.permutation(jax.random.fold_in(key, 7), total)
    values = values.at[order[0]].set(0)
    values = values.at[order[1]].set(2 * HALO)
    return values.reshape(GRID_R, GRID_C, POS, 2).astype(jnp.int32)


def level_of(stream_key, shape, split, smallest, largest):
    factor_of, own = 1.0, jax.random.fold_in(stream_key, 6)
    for dim, parts in split:
        draws = jnp.exp(jax.random.uniform(jax.random.fold_in(own, dim), (parts,), jnp.float32, smallest / len(split), largest / len(split)))
        factor_of = factor_of * jnp.repeat(draws, shape[dim] // parts).reshape([-1 if axis == dim else 1 for axis in range(len(shape))])
    return factor_of


def noise(stream_key, dims, deviation, bound, cuts=(), kind=jnp.bfloat16):
    entries = deviation * jax.random.normal(stream_key, dims, jnp.float32)
    if cuts:
        entries = entries * level_of(stream_key, dims, cuts, -0.22, 0.18)
    return jnp.clip(entries, -bound, bound).astype(kind)


def setup_inputs(seed: int = 0) -> dict:
    splits = jax.random.split(jax.random.key(seed), 6)
    object_field = noise(splits[0], (2, 2, HEIGHT, WIDTH), 0.7, 5.0, ((2, 2), (3, 16)), jnp.float32)
    probe = noise(splits[1], (2, N, N), 0.7, 5.0, (), jnp.float32)
    phase = jnp.clip(jax.random.uniform(splits[2], (N, N), jnp.float32, -3.140625, 3.140625), -3.140625, 3.140625)
    amplitudes = jnp.clip(jnp.exp(math.log(3.0) - 2.7080502 * jax.random.uniform(splits[3], (GRID_R, GRID_C, POS, N, N), jnp.float32) ** level_of(splits[3], (GRID_R, GRID_C, POS, N, N), ((0, 2), (1, 16)), -0.2, 0.2)), 0.2, 3.0)
    offsets = draw_offsets(jax.random.fold_in(splits[5], 71), 0)
    return {"object_field": object_field, "probe": probe, "phase": phase, "amplitudes": amplitudes, "offsets": offsets}


EPS_AMP = 0.5

def dft_tables(count):
    counter = jnp.arange(count, dtype=jnp.int32)
    product_idx = counter[:, None] * counter[None, :] % count
    angles = product_idx.astype(jnp.float32) * (2.0 * jnp.pi / count)
    scale = 1.0 / jnp.sqrt(jnp.asarray(count, jnp.float32))
    return (jnp.cos(angles) * scale, -jnp.sin(angles) * scale)

def left_mult(table, field):
    return jnp.einsum('jk,...kl->...jl', table, field, precision=lax.Precision.HIGHEST)

def right_mult(field, table):
    return jnp.einsum('...jk,kl->...jl', field, table, precision=lax.Precision.HIGHEST)

def transform(real_part, imag_part, table_re, table_im):
    mid_re = left_mult(table_re, real_part) - left_mult(table_im, imag_part)
    mid_im = left_mult(table_re, imag_part) + left_mult(table_im, real_part)
    out_re = right_mult(mid_re, table_re) - right_mult(mid_im, table_im)
    out_im = right_mult(mid_im, table_re) + right_mult(mid_re, table_im)
    return (out_re, out_im)

def product(first_re, first_im, second_re, second_im):
    return (first_re * second_re - first_im * second_im, first_re * second_im + first_im * second_re)

def conj_product(first_re, first_im, second_re, second_im):
    return (first_re * second_re + first_im * second_im, first_re * second_im - first_im * second_re)

def position_grads(first_re, first_im, second_re, second_im, probe_re, probe_im, kernel_re, kernel_im, measured, table_re, table_im):
    entry = product(probe_re, probe_im, first_re, first_im)
    spectrum = transform(entry[0], entry[1], table_re, table_im)
    moved = product(kernel_re, kernel_im, spectrum[0], spectrum[1])
    arrive = transform(moved[0], moved[1], table_re, -table_im)
    leaving = product(arrive[0], arrive[1], second_re, second_im)
    far = transform(leaving[0], leaving[1], table_re, table_im)
    modulus = jnp.sqrt(far[0] * far[0] + far[1] * far[1] + EPS_AMP)
    factor = 2.0 * (1.0 - measured / modulus)
    back_far = transform(factor * far[0], factor * far[1], table_re, -table_im)
    grad_second = conj_product(arrive[0], arrive[1], back_far[0], back_far[1])
    back_arrive = conj_product(second_re, second_im, back_far[0], back_far[1])
    back_spec = transform(back_arrive[0], back_arrive[1], table_re, table_im)
    back_moved = conj_product(kernel_re, kernel_im, back_spec[0], back_spec[1])
    back_entry = transform(back_moved[0], back_moved[1], table_re, -table_im)
    grad_probe = conj_product(first_re, first_im, back_entry[0], back_entry[1])
    grad_first = conj_product(probe_re, probe_im, back_entry[0], back_entry[1])
    return (grad_first, grad_second, grad_probe)

def reference(object_field, probe, phase, amplitudes, offsets):
    table_re, table_im = dft_tables(N)
    kernel_re = jnp.cos(phase)
    kernel_im = jnp.sin(phase)
    height = object_field.shape[2]
    width = object_field.shape[3]
    padded = jnp.pad(object_field.reshape(4, height, width), ((0, 0), (HALO, HALO), (HALO, HALO)))
    flat_offsets = offsets.reshape(-1, 2)
    flat_amps = amplitudes.reshape(-1, N, N)
    total = flat_offsets.shape[0]

    def step(carry, index):
        grad_pad, grad_probe = carry
        tile_row = index // (GRID_C * POS)
        tile_col = index // POS % GRID_C
        start_y = (tile_row * N + flat_offsets[index, 0]).astype(jnp.int32)
        start_x = (tile_col * N + flat_offsets[index, 1]).astype(jnp.int32)
        zero = jnp.zeros((), jnp.int32)
        window = lax.dynamic_slice(padded, (zero, start_y, start_x), (4, N, N))
        measured = lax.dynamic_index_in_dim(flat_amps, index, 0, keepdims=False)
        grad_first, grad_second, grad_pr = position_grads(window[0], window[1], window[2], window[3], probe[0], probe[1], kernel_re, kernel_im, measured, table_re, table_im)
        piece = jnp.stack([grad_first[0], grad_first[1], grad_second[0], grad_second[1]])
        current = lax.dynamic_slice(grad_pad, (zero, start_y, start_x), (4, N, N))
        grad_pad = lax.dynamic_update_slice(grad_pad, current + piece, (zero, start_y, start_x))
        grad_probe = grad_probe + jnp.stack([grad_pr[0], grad_pr[1]])
        return ((grad_pad, grad_probe), None)
    init = (jnp.zeros(padded.shape, jnp.float32), jnp.zeros((2, N, N), jnp.float32))
    (grad_pad, grad_probe), leftover = lax.scan(step, init, jnp.arange(total, dtype=jnp.int32))
    object_grad = grad_pad[:, HALO:HALO + height, HALO:HALO + width].reshape(2, 2, height, width)
    return (object_grad, grad_probe)
```

```python
import functools

import jax
import jax.numpy as jnp
import numpy as np
from jax import lax
from jax.experimental import pallas as pl
from jax.experimental.pallas import tpu as pltpu
from jax.sharding import PartitionSpec as P

EPS_AMP = 0.5
F32 = jnp.float32
BF16 = jnp.bfloat16
VMEM = pl.BlockSpec(memory_space=pltpu.VMEM)
SMEM = pl.BlockSpec(memory_space=pltpu.SMEM)


def split_np(table):
    high = table.astype(BF16)
    low = (table - high.astype(np.float64)).astype(BF16)
    return [high, low]


def dft_constants(n):
    h = n // 2
    k = np.arange(h)
    angle = 2.0 * np.pi * ((k[:, None] * k[None, :]) % h) / h
    scale = 1.0 / np.sqrt(n)
    c, s = np.cos(angle) * scale, np.sin(angle) * scale
    d = np.block([[c, s], [-s, c]])
    mats = np.stack(split_np(d) + split_np(d.T))
    w = np.exp(-2j * np.pi * k / n)
    tw_left = np.stack([np.tile(w.real[:, None], (1, h)), np.tile(w.imag[:, None], (1, h))])
    tw_right = np.stack([np.tile(w.real[None], (8, 1)), np.tile(w.imag[None], (8, 1))])
    order = np.zeros((n, n))
    order[2 * k, k] = 1.0
    order[2 * k + 1, h + k] = 1.0
    return (
        mats,
        tw_left.astype(np.float32),
        tw_right.astype(np.float32),
        np.stack([order.T, order]).astype(BF16),
    )


def split(x):
    high = x.astype(BF16)
    return high, (x - high.astype(F32)).astype(BF16)


def dot(a, b):
    return jnp.dot(a, b, preferred_element_type=F32)


def left_dot(mats, which, x):
    high, low = split(x)
    return dot(mats[which], high) + (dot(mats[which], low) + dot(mats[which + 1], high))


def right_dot(x, mats, which):
    high, low = split(x)
    return dot(high, mats[which]) + (dot(low, mats[which]) + dot(high, mats[which + 1]))


def cat(parts, axis):
    return jnp.concatenate(parts, axis=axis)


def product(a, b):
    return (a[0] * b[0] - a[1] * b[1], a[0] * b[1] + a[1] * b[0])


def conj_product(a, b):
    return (a[0] * b[0] + a[1] * b[1], a[0] * b[1] - a[1] * b[0])


class Dft:
    def __init__(self, mats, tw_left, tw_right, n):
        self.mats, self.n, self.h = mats, n, n // 2
        self.wl = [cat([tw_left[i], tw_left[i]], 1) for i in range(2)]
        self.wr = [tw_right[i, 0:1] for i in range(2)]

    def forward(self, x):
        n, h = self.n, self.h
        total = [p[:h] + p[h:] for p in x]
        odd = product([p[:h] - p[h:] for p in x], self.wl)
        y = left_dot(self.mats, 0, cat([cat(total, 0), cat(odd, 0)], 1))
        x = [cat([y[:h, :n], y[:h, n:]], 0), cat([y[h:, :n], y[h:, n:]], 0)]
        total = [p[:, :h] + p[:, h:] for p in x]
        odd = product([p[:, :h] - p[:, h:] for p in x], self.wr)
        y = right_dot(cat([cat(total, 1), cat(odd, 1)], 0), self.mats, 2)
        return [cat([y[:n, :h], y[n:, :h]], 1), cat([y[:n, h:], y[n:, h:]], 1)]

    def inverse(self, x):
        n, h = self.n, self.h
        y = cat([cat([p[:, :h] for p in x], 1), cat([p[:, h:] for p in x], 1)], 0)
        y = right_dot(y, self.mats, 0)
        even = [y[:n, :h], y[:n, h:]]
        odd = conj_product(self.wr, [y[n:, :h], y[n:, h:]])
        x = [cat([e + o, e - o], 1) for e, o in zip(even, odd)]
        y = cat([cat([p[:h] for p in x], 0), cat([p[h:] for p in x], 0)], 1)
        y = left_dot(self.mats, 2, y)
        even = [y[:h, :n], y[h:, :n]]
        odd = conj_product(self.wl, [y[:h, n:], y[h:, n:]])
        return [cat([e + o, e - o], 0) for e, o in zip(even, odd)]


def iota(shape, dim):
    return lax.broadcasted_iota(jnp.int32, shape, dim)


def half_roll(x):
    return pltpu.roll(x, x.shape[-1] // 2, axis=x.ndim - 1)


def pack_cols(re, im):
    h = re.shape[1] // 2
    front = iota((re.shape[0], h), 1) < h // 2
    low = jnp.where(front, re[:, :h], half_roll(im[:, :h]))
    high = jnp.where(front, half_roll(im[:, h:]), re[:, h:])
    return low, high


def pack_kernel(n_row, obj, *refs):
    halos, outs = refs[:n_row], refs[n_row:]
    even = lax.axis_index("col") % 2 == 0
    for s in range(2):
        sources = [obj] + list(halos)
        at = 0
        for source in sources:
            rows = source.shape[1]
            low, high = pack_cols(source[2 * s], source[2 * s + 1])
            outs[2 * s][at : at + rows] = jnp.where(even, high, low)
            outs[2 * s + 1][at : at + rows] = jnp.where(even, low, high)
            at += rows


def dyn_roll(x, shift, axis):
    return pltpu.roll(x, shift, axis=axis)


def prep_kernel(margin, phase, amps, probe, offs, order, kr, ki, am, pr):
    n = phase.shape[0]

    def thirds(x):
        a = x.astype(BF16)
        rest = x - a.astype(F32)
        return (a,) + split(rest)

    def reorder(ref):
        a, b, c = thirds(ref[...])
        rows = dot(order[0], a) + (dot(order[0], b) + dot(order[0], c))
        a, b, c = thirds(rows)
        return dot(a, order[1]) + (dot(b, order[1]) + dot(c, order[1]))

    angle = reorder(phase)
    kr[...] = jnp.cos(angle)
    ki[...] = jnp.sin(angle)
    am[...] = reorder(amps)
    sy = (offs[0, 0] - margin + n) % n
    sx = (offs[0, 1] - margin + n) % n
    for i in range(2):
        pr[i] = dyn_roll(dyn_roll(probe[i], sy, 0), sx, 1)


def merge_cols(own, low, high, ox, margin):
    n = own[0].shape[1]
    h = n // 2
    lane = iota((own[0].shape[0], h), 1)
    from_high = lane < ox - margin
    from_low = lane + h >= ox + n - margin
    out = []
    for i in range(2):
        strip_high = high if i == 0 else half_roll(high)
        strip_low = low if i == 0 else half_roll(low)
        out.append(
            cat(
                [
                    jnp.where(from_high, strip_high, own[i][:, :h]),
                    jnp.where(from_low, strip_low, own[i][:, h:]),
                ],
                1,
            )
        )
    return out


def window_of(obj, s, halos, strip_e, strip_o, offs, margin):
    n = obj.shape[1]
    oy, ox = offs[0, 0], offs[0, 1]
    col_even = lax.axis_index("col") % 2 == 0
    row_even = lax.axis_index("row") % 2 == 0
    blocks = []
    at = 0
    for source in [obj] + list(halos):
        rows = source.shape[1]
        e, o = strip_e[at : at + rows], strip_o[at : at + rows]
        high, low = jnp.where(col_even, e, o), jnp.where(col_even, o, e)
        blocks.append(merge_cols([source[2 * s], source[2 * s + 1]], low, high, ox, margin))
        at += rows
    row = iota((margin, n), 0)
    take_high = row < oy - margin
    take_low = row + n - margin >= oy + n - margin
    out = []
    for i in range(2):
        main = blocks[0][i]
        if len(blocks) == 3:
            e, o = blocks[1][i], blocks[2][i]
            high, low = jnp.where(row_even, e, o), jnp.where(row_even, o, e)
        else:
            e = blocks[1][i]
            zero = jnp.zeros_like(e)
            high, low = jnp.where(row_even, e, zero), jnp.where(row_even, zero, e)
        out.append(
            cat(
                [
                    jnp.where(take_high, high, main[:margin]),
                    main[margin : n - margin],
                    jnp.where(take_low, low, main[n - margin :]),
                ],
                0,
            )
        )
    return out


def arrive_kernel(n_row, margin, *refs):
    obj, halos = refs[0], refs[1 : 1 + n_row]
    e1, o1, offs, pr, kr, ki, mats, twl, twr, w1, arrive = refs[1 + n_row :]
    n = obj.shape[1]
    dft = Dft(mats, twl[...], twr[...], n)
    win = window_of(obj, 0, halos, e1, o1, offs, margin)
    w1[0], w1[1] = win
    x = dft.forward(product([pr[0], pr[1]], win))
    x = dft.inverse(product([kr[...], ki[...]], x))
    arrive[0], arrive[1] = x


def split_grad(grad, offs, margin, own, strip, sends):
    n = grad[0].shape[0]
    h = n // 2
    oy, ox = offs[0, 0], offs[0, 1]
    row_even = lax.axis_index("row") % 2 == 0
    lane = iota((1, h), 1)
    to_high, to_low = lane < ox - margin, lane + h >= ox + n - margin
    front = lane < h // 2
    spill = jnp.where(front, to_high.astype(jnp.int32), to_low.astype(jnp.int32)) != 0
    for i in range(2):
        g = grad[i]
        row = iota((n, h), 0)
        high_rows = row < oy - margin
        low_rows = row >= oy + n - margin
        inner = jnp.logical_not(jnp.logical_or(high_rows, low_rows))
        left = jnp.where(to_high, 0.0, g[:, :h])
        right = jnp.where(to_low, 0.0, g[:, h:])
        side = jnp.where(spill, jnp.where(front, g[:, :h], g[:, h:]), 0.0)
        pieces = [left, right, side]
        own[i, :, :h] = jnp.where(inner, left, 0.0)
        own[i, :, h:] = jnp.where(inner, right, 0.0)
        strip[i] = jnp.where(inner, side, 0.0)
        for j, piece in enumerate(pieces):
            top = jnp.where(high_rows[:margin], piece[:margin], 0.0)
            bottom = jnp.where(low_rows[n - margin :], piece[n - margin :], 0.0)
            for which, send in enumerate(sends):
                first = row_even if which == 0 else jnp.logical_not(row_even)
                send[i, :, j * h : (j + 1) * h] = jnp.where(first, top, bottom)


def back_kernel(n_row, margin, *refs):
    obj, halos = refs[0], refs[1 : 1 + n_row]
    e2, o2, offs, pr, kr, ki, am, w1, arrive, mats, twl, twr = refs[1 + n_row : 13 + n_row]
    outs = refs[13 + n_row :]
    keep, give = outs[:2]
    n = obj.shape[1]
    dft = Dft(mats, twl[...], twr[...], n)
    win = window_of(obj, 1, halos, e2, o2, offs, margin)
    arr = [arrive[0], arrive[1]]
    far = dft.forward(product(arr, win))
    modulus = jnp.sqrt(far[0] * far[0] + far[1] * far[1] + EPS_AMP)
    factor = 2.0 * (1.0 - am[...] / modulus)
    back_far = dft.inverse([factor * far[0], factor * far[1]])
    rest = outs[2:]
    split_grad(conj_product(arr, back_far), offs, margin, rest[0], rest[1], rest[2 : 2 + n_row])
    x = dft.forward(conj_product(win, back_far))
    x = dft.inverse(conj_product([kr[...], ki[...]], x))
    rest = rest[2 + n_row :]
    split_grad(
        conj_product([pr[0], pr[1]], x), offs, margin, rest[0], rest[1], rest[2 : 2 + n_row]
    )
    grad = conj_product([w1[0], w1[1]], x)
    sy = (margin - offs[0, 0] + n) % n
    sx = (margin - offs[0, 1] + n) % n
    grad = [dyn_roll(dyn_roll(g, sy, 0), sx, 1) for g in grad]
    even = lax.axis_index("row") % 2 == 0
    keep[...] = jnp.where(even, grad[0], grad[1])
    give[...] = jnp.where(even, grad[1], grad[0])


def fold_rows_kernel(n_row, margin, *refs):
    ins, outs = refs[: 2 * (2 + n_row)], refs[2 * (2 + n_row) :]
    row_even = lax.axis_index("row") % 2 == 0
    col_even = lax.axis_index("col") % 2 == 0
    for s in range(2):
        own, strip = ins[s * (2 + n_row) : s * (2 + n_row) + 2]
        got = ins[s * (2 + n_row) + 2 : (s + 1) * (2 + n_row)]
        total, send_e, send_o = outs[3 * s : 3 * s + 3]
        n = own.shape[1]
        h = n // 2
        strips = []
        for i in range(2):
            total[i] = own[i]
            r = got[0][i]
            if n_row == 2:
                q = got[1][i]
            else:
                q = jnp.zeros_like(r)
            top, bottom = jnp.where(row_even, q, r), jnp.where(row_even, r, q)
            total[i, :margin] += top[:, :n]
            total[i, n - margin :] += bottom[:, :n]
            st = strip[i]
            strips.append(
                cat(
                    [
                        st[:margin] + top[:, n:],
                        st[margin : n - margin],
                        st[n - margin :] + bottom[:, n:],
                    ],
                    0,
                )
            )
        front = iota((n, h), 1) < h // 2
        moved = half_roll(strips[1])
        to_high = jnp.where(front, strips[0], moved)
        to_low = jnp.where(front, moved, strips[0])
        send_e[...] = jnp.where(col_even, to_high, to_low)
        send_o[...] = jnp.where(col_even, to_low, to_high)


def fold_cols_kernel(t1, e1, o1, t2, e2, o2, out):
    col_even = lax.axis_index("col") % 2 == 0
    for s, (t, e, o) in enumerate(((t1, e1, o1), (t2, e2, o2))):
        n = t.shape[1]
        h = n // 2
        front = iota((n, h), 1) < h // 2
        high = jnp.where(col_even, e[...], o[...])
        low = jnp.where(col_even, o[...], e[...])
        for i in range(2):
            a = low if i == 0 else half_roll(low)
            b = high if i == 0 else half_roll(high)
            out[2 * s + i, :, :h] = t[i, :, :h] + jnp.where(front, a, 0.0)
            out[2 * s + i, :, h:] = t[i, :, h:] + jnp.where(front, 0.0, b)


def call(kernel, shapes, in_specs, *args):
    return pl.pallas_call(
        kernel,
        out_shape=[jax.ShapeDtypeStruct(s, F32) for s in shapes],
        in_specs=in_specs,
        out_specs=[VMEM] * len(shapes),
        compiler_params=pltpu.CompilerParams(vmem_limit_bytes=48 * 1024 * 1024),
    )(*args)


def edges(axis):
    count = lax.axis_size(axis)
    rounds = []
    for first in (0, 1):
        pairs = [(i, i + 1) for i in range(first, count - 1, 2)]
        pairs += [(b, a) for a, b in pairs]
        if pairs:
            rounds.append(pairs)
    return rounds


def swap(value, axis, distance):
    count = lax.axis_size(axis)
    return lax.ppermute(value, axis, [(i, i ^ distance) for i in range(count)])


def stages(axis, start):
    count = lax.axis_size(axis)
    out = []
    stride = start
    while stride < count:
        width = min(4, count // stride)
        out.append((axis, stride, width))
        stride *= width
    return out


def pair_sum(parts):
    while len(parts) > 1:
        parts = [parts[i] + parts[i + 1] for i in range(0, len(parts), 2)]
    return parts[0]


def reduce_probe(keep, give):
    rows = lax.axis_size("row")
    cols = lax.axis_size("col")
    n = keep.shape[0]
    mine = keep + swap(give, "row", 1)
    quad = min(4, cols)
    place = lax.axis_index("col") % quad
    chunk = n // quad
    parts = [
        lax.dynamic_slice_in_dim(mine, (place ^ j) * chunk, chunk, 0) for j in range(quad)
    ]
    total = pair_sum([parts[0]] + [swap(parts[j], "col", j) for j in range(1, quad)])
    for axis, stride, width in stages("col", quad) + stages("row", 2):
        total = pair_sum([total] + [swap(total, axis, stride * j) for j in range(1, width)])
    full = jnp.zeros((quad, chunk, n), F32)
    for j in range(quad):
        part = total if j == 0 else swap(total, "col", j)
        full = lax.dynamic_update_slice(full, part[None], (place ^ j, 0, 0))
    full = full.reshape(n, n)
    other = swap(full, "row", 1)
    even = lax.axis_index("row") % 2 == 0
    return jnp.stack([jnp.where(even, full, other), jnp.where(even, other, full)])


def body(object_field, probe, phase, amplitudes, offsets):
    tile = object_field.shape[2]
    n = probe.shape[1]
    h = n // 2
    margin = n // 4
    obj = object_field.reshape(4, tile, tile)
    offs = offsets.reshape(1, 2)
    amps = amplitudes.reshape(n, n)
    mats, tw_left, tw_right, order = [jnp.asarray(t) for t in dft_constants(n)]

    row_rounds, col_rounds = edges("row"), edges("col")
    n_row = len(row_rounds)
    row_even = lax.axis_index("row") % 2 == 0
    halos = []
    for which, pairs in enumerate(row_rounds):
        last = row_even if which == 0 else jnp.logical_not(row_even)
        strip = lax.dynamic_slice_in_dim(obj, jnp.where(last, tile - margin, 0), margin, 1)
        halos.append(lax.ppermute(strip, "row", pairs))
    length = tile + margin * n_row

    packed = call(
        functools.partial(pack_kernel, n_row),
        [(length, h)] * 4,
        [VMEM] * (1 + n_row),
        obj,
        *halos,
    )
    strips = [lax.ppermute(packed[i], "col", col_rounds[i % 2]) for i in range(4)]
    kr, ki, am, pr = call(
        functools.partial(prep_kernel, margin),
        [(n, n), (n, n), (n, n), (2, n, n)],
        [VMEM, VMEM, VMEM, SMEM, VMEM],
        phase,
        amps,
        probe,
        offs,
        order,
    )
    w1, arrive = call(
        functools.partial(arrive_kernel, n_row, margin),
        [(2, n, n), (2, n, n)],
        [VMEM] * (1 + n_row) + [VMEM, VMEM, SMEM] + [VMEM] * 6,
        obj,
        *halos,
        strips[0],
        strips[1],
        offs,
        pr,
        kr,
        ki,
        mats,
        tw_left,
        tw_right,
    )
    per_slice = [(2, n, n), (2, n, h)] + [(2, margin, n + h)] * n_row
    outs = call(
        functools.partial(back_kernel, n_row, margin),
        [(n, n), (n, n)] + per_slice * 2,
        [VMEM] * (1 + n_row) + [VMEM, VMEM, SMEM] + [VMEM] * 9,
        obj,
        *halos,
        strips[2],
        strips[3],
        offs,
        pr,
        kr,
        ki,
        am,
        w1,
        arrive,
        mats,
        tw_left,
        tw_right,
    )
    keep, give = outs[:2]
    probe_grad = reduce_probe(keep, give)
    second, first = outs[2 : 4 + n_row], outs[4 + n_row :]
    ins = []
    for part in (first, second):
        ins += list(part[:2])
        ins += [lax.ppermute(part[2 + i], "row", row_rounds[i]) for i in range(n_row)]
    folded = call(
        functools.partial(fold_rows_kernel, n_row, margin),
        [(2, n, n), (n, h), (n, h)] * 2,
        [VMEM] * len(ins),
        *ins,
    )
    folded = [
        f if i % 3 == 0 else lax.ppermute(f, "col", col_rounds[i % 3 - 1])
        for i, f in enumerate(folded)
    ]
    (grad,) = call(fold_cols_kernel, [(4, n, n)], [VMEM] * 6, *folded)
    return (grad.reshape(2, 2, tile, tile), probe_grad)


def solution(mesh):
    placed = (
        P(None, None, "row", "col"),
        P(),
        P(),
        P("row", "col", None, None, None),
        P("row", "col", None, None),
    )
    return jax.shard_map(
        body,
        mesh=mesh,
        in_specs=placed,
        out_specs=(P(None, None, "row", "col"), P()),
        check_vma=False,
    )
```

```python
import functools

import jax
import jax.numpy as jnp
import numpy as np
from jax import lax
from jax.experimental import pallas as pl
from jax.experimental.pallas import tpu as pltpu
from jax.sharding import PartitionSpec as P


EPS_AMP = 0.5
F32 = jnp.float32
BF16 = jnp.bfloat16
VMEM = pl.BlockSpec(memory_space=pltpu.VMEM)
SMEM = pl.BlockSpec(memory_space=pltpu.SMEM)
HBM = pl.BlockSpec(memory_space=pltpu.HBM)


def split_np(table):
    high = table.astype(BF16)
    low = (table - high.astype(np.float64)).astype(BF16)
    return [high, low]


def dft_constants(n):
    h = n // 2
    k = np.arange(h)
    angle = 2.0 * np.pi * ((k[:, None] * k[None, :]) % h) / h
    scale = 1.0 / np.sqrt(n)
    c, s = np.cos(angle) * scale, np.sin(angle) * scale
    d = np.block([[c, s], [-s, c]])
    mats = np.stack(split_np(d) + split_np(d.T))
    w = np.exp(-2j * np.pi * k / n)
    tw_left = np.stack([np.tile(w.real[:, None], (1, h)), np.tile(w.imag[:, None], (1, h))])
    tw_right = np.stack([np.tile(w.real[None], (8, 1)), np.tile(w.imag[None], (8, 1))])
    order = np.zeros((n, n))
    order[2 * k, k] = 1.0
    order[2 * k + 1, h + k] = 1.0
    return (
        mats,
        tw_left.astype(np.float32),
        tw_right.astype(np.float32),
        np.stack([order.T, order]).astype(BF16),
    )


def split(x):
    high = x.astype(BF16)
    return high, (x - high.astype(F32)).astype(BF16)


def dot(a, b):
    return jnp.dot(a, b, preferred_element_type=F32)


def left_dot(mats, which, x):
    high, low = split(x)
    return dot(mats[which], high) + (dot(mats[which], low) + dot(mats[which + 1], high))


def right_dot(x, mats, which):
    high, low = split(x)
    return dot(high, mats[which]) + (dot(low, mats[which]) + dot(high, mats[which + 1]))


def cat(parts, axis):
    return jnp.concatenate(parts, axis=axis)


def product(a, b):
    return (a[0] * b[0] - a[1] * b[1], a[0] * b[1] + a[1] * b[0])


def conj_product(a, b):
    return (a[0] * b[0] + a[1] * b[1], a[0] * b[1] - a[1] * b[0])


class Dft:
    def __init__(self, mats, tw_left, tw_right, n):
        self.mats, self.n, self.h = mats, n, n // 2
        self.wl = [cat([tw_left[i], tw_left[i]], 1) for i in range(2)]
        self.wr = [tw_right[i, 0:1] for i in range(2)]

    def forward(self, x):
        n, h = self.n, self.h
        total = [p[:h] + p[h:] for p in x]
        odd = product([p[:h] - p[h:] for p in x], self.wl)
        y = left_dot(self.mats, 0, cat([cat(total, 0), cat(odd, 0)], 1))
        x = [cat([y[:h, :n], y[:h, n:]], 0), cat([y[h:, :n], y[h:, n:]], 0)]
        total = [p[:, :h] + p[:, h:] for p in x]
        odd = product([p[:, :h] - p[:, h:] for p in x], self.wr)
        y = right_dot(cat([cat(total, 1), cat(odd, 1)], 0), self.mats, 2)
        return [cat([y[:n, :h], y[n:, :h]], 1), cat([y[:n, h:], y[n:, h:]], 1)]

    def inverse(self, x):
        n, h = self.n, self.h
        y = cat([cat([p[:, :h] for p in x], 1), cat([p[:, h:] for p in x], 1)], 0)
        y = right_dot(y, self.mats, 0)
        even = [y[:n, :h], y[:n, h:]]
        odd = conj_product(self.wr, [y[n:, :h], y[n:, h:]])
        x = [cat([e + o, e - o], 1) for e, o in zip(even, odd)]
        y = cat([cat([p[:h] for p in x], 0), cat([p[h:] for p in x], 0)], 1)
        y = left_dot(self.mats, 2, y)
        even = [y[:h, :n], y[h:, :n]]
        odd = conj_product(self.wl, [y[:h, n:], y[h:, n:]])
        return [cat([e + o, e - o], 0) for e, o in zip(even, odd)]


def iota(shape, dim):
    return lax.broadcasted_iota(jnp.int32, shape, dim)


def half_roll(x):
    return pltpu.roll(x, x.shape[-1] // 2, axis=x.ndim - 1)


def pack_cols(re, im):
    h = re.shape[1] // 2
    front = iota((re.shape[0], h), 1) < h // 2
    low = jnp.where(front, re[:, :h], half_roll(im[:, :h]))
    high = jnp.where(front, half_roll(im[:, h:]), re[:, h:])
    return low, high


def load_kernel(n_row, margin, obj_hbm, offs_hbm, *refs):
    strips, (obj, offs, sems) = refs[:n_row], refs[n_row:]
    n = obj.shape[1]
    even = lax.axis_index("row") % 2 == 0
    copies = []
    for which, strip in enumerate(strips):
        last = even if which == 0 else jnp.logical_not(even)
        start = pl.multiple_of(jnp.where(last, n - margin, 0), 8)
        copies.append(
            pltpu.make_async_copy(
                obj_hbm.at[:, pl.ds(start, margin), :], strip, sems.at[which + 1]
            )
        )
    copies.append(pltpu.make_async_copy(obj_hbm, obj, sems.at[0]))
    copies.append(pltpu.make_async_copy(offs_hbm, offs, sems.at[n_row + 1]))
    for copy in copies:
        copy.start()
    for copy in copies:
        copy.wait()


def pack_kernel(n_row, obj, *refs):
    halos, outs = refs[:n_row], refs[n_row:]
    even = lax.axis_index("col") % 2 == 0
    for s in range(2):
        sources = [obj] + list(halos)
        at = 0
        for source in sources:
            rows = source.shape[1]
            low, high = pack_cols(source[2 * s], source[2 * s + 1])
            outs[2 * s][at : at + rows] = jnp.where(even, high, low)
            outs[2 * s + 1][at : at + rows] = jnp.where(even, low, high)
            at += rows


def dyn_roll(x, shift, axis):
    return pltpu.roll(x, shift, axis=axis)


def prep_kernel(margin, offs, *refs):
    hbm, outs, scratch, sems = refs[:7], refs[7:14], refs[14:18], refs[18]
    kr, ki, am, pr = outs[:4]
    phase, amps, probe, order = scratch
    n = phase.shape[0]
    places = list(scratch) + list(outs[4:])
    copies = [pltpu.make_async_copy(a, b, sems.at[i]) for i, (a, b) in enumerate(zip(hbm, places))]
    for copy in copies:
        copy.start()

    def thirds(x):
        a = x.astype(BF16)
        rest = x - a.astype(F32)
        return (a,) + split(rest)

    def reorder(ref):
        a, b, c = thirds(ref[...])
        rows = dot(order[0], a) + (dot(order[0], b) + dot(order[0], c))
        a, b, c = thirds(rows)
        return dot(a, order[1]) + (dot(b, order[1]) + dot(c, order[1]))

    copies[0].wait()
    copies[3].wait()
    angle = reorder(phase)
    kr[...] = jnp.cos(angle)
    ki[...] = jnp.sin(angle)
    copies[1].wait()
    am[...] = reorder(amps)
    sy = (offs[0, 0] - margin + n) % n
    sx = (offs[0, 1] - margin + n) % n
    copies[2].wait()
    for i in range(2):
        pr[i] = dyn_roll(dyn_roll(probe[i], sy, 0), sx, 1)
    for copy in copies[4:]:
        copy.wait()


def merge_cols(own, low, high, ox, margin):
    n = own[0].shape[1]
    h = n // 2
    lane = iota((own[0].shape[0], h), 1)
    from_high = lane < ox - margin
    from_low = lane + h >= ox + n - margin
    out = []
    for i in range(2):
        strip_high = high if i == 0 else half_roll(high)
        strip_low = low if i == 0 else half_roll(low)
        out.append(
            cat(
                [
                    jnp.where(from_high, strip_high, own[i][:, :h]),
                    jnp.where(from_low, strip_low, own[i][:, h:]),
                ],
                1,
            )
        )
    return out


def window_of(obj, s, halos, strip_e, strip_o, offs, margin):
    n = obj.shape[1]
    oy, ox = offs[0, 0], offs[0, 1]
    col_even = lax.axis_index("col") % 2 == 0
    row_even = lax.axis_index("row") % 2 == 0
    blocks = []
    at = 0
    for source in [obj] + list(halos):
        rows = source.shape[1]
        e, o = strip_e[at : at + rows], strip_o[at : at + rows]
        high, low = jnp.where(col_even, e, o), jnp.where(col_even, o, e)
        blocks.append(merge_cols([source[2 * s], source[2 * s + 1]], low, high, ox, margin))
        at += rows
    row = iota((margin, n), 0)
    take_high = row < oy - margin
    take_low = row + n - margin >= oy + n - margin
    out = []
    for i in range(2):
        main = blocks[0][i]
        if len(blocks) == 3:
            e, o = blocks[1][i], blocks[2][i]
            high, low = jnp.where(row_even, e, o), jnp.where(row_even, o, e)
        else:
            e = blocks[1][i]
            zero = jnp.zeros_like(e)
            high, low = jnp.where(row_even, e, zero), jnp.where(row_even, zero, e)
        out.append(
            cat(
                [
                    jnp.where(take_high, high, main[:margin]),
                    main[margin : n - margin],
                    jnp.where(take_low, low, main[n - margin :]),
                ],
                0,
            )
        )
    return out


def arrive_kernel(n_row, margin, *refs):
    obj, halos = refs[0], refs[1 : 1 + n_row]
    e1, o1, offs, pr, kr, ki, mats, twl, twr, w1, arrive = refs[1 + n_row :]
    n = obj.shape[1]
    dft = Dft(mats, twl[...], twr[...], n)
    win = window_of(obj, 0, halos, e1, o1, offs, margin)
    w1[0], w1[1] = win
    x = dft.forward(product([pr[0], pr[1]], win))
    x = dft.inverse(product([kr[...], ki[...]], x))
    arrive[0], arrive[1] = x


def split_grad(grad, s, offs, margin, own, strip, sends):
    n = grad[0].shape[0]
    h = n // 2
    oy, ox = offs[0, 0], offs[0, 1]
    row_even = lax.axis_index("row") % 2 == 0
    lane = iota((1, h), 1)
    to_high, to_low = lane < ox - margin, lane + h >= ox + n - margin
    front = lane < h // 2
    spill = jnp.where(front, to_high.astype(jnp.int32), to_low.astype(jnp.int32)) != 0
    for i in range(2):
        g = grad[i]
        row = iota((n, h), 0)
        high_rows = row < oy - margin
        low_rows = row >= oy + n - margin
        inner = jnp.logical_not(jnp.logical_or(high_rows, low_rows))
        left = jnp.where(to_high, 0.0, g[:, :h])
        right = jnp.where(to_low, 0.0, g[:, h:])
        side = jnp.where(spill, jnp.where(front, g[:, :h], g[:, h:]), 0.0)
        pieces = [left, right, side]
        own[2 * s + i, :, :h] = jnp.where(inner, left, 0.0)
        own[2 * s + i, :, h:] = jnp.where(inner, right, 0.0)
        strip[2 * s + i] = jnp.where(inner, side, 0.0)
        for j, piece in enumerate(pieces):
            top = jnp.where(high_rows[:margin], piece[:margin], 0.0)
            bottom = jnp.where(low_rows[n - margin :], piece[n - margin :], 0.0)
            for which, send in enumerate(sends):
                first = row_even if which == 0 else jnp.logical_not(row_even)
                send[2 * s + i, :, j * h : (j + 1) * h] = jnp.where(first, top, bottom)


def back_kernel(n_row, margin, *refs):
    obj, halos = refs[0], refs[1 : 1 + n_row]
    e2, o2, offs, pr, kr, ki, am, w1, arrive, mats, twl, twr = refs[1 + n_row : 13 + n_row]
    outs = refs[13 + n_row :]
    keep, give = outs[:2]
    n = obj.shape[1]
    dft = Dft(mats, twl[...], twr[...], n)
    win = window_of(obj, 1, halos, e2, o2, offs, margin)
    arr = [arrive[0], arrive[1]]
    far = dft.forward(product(arr, win))
    modulus = jnp.sqrt(far[0] * far[0] + far[1] * far[1] + EPS_AMP)
    factor = 2.0 * (1.0 - am[...] / modulus)
    back_far = dft.inverse([factor * far[0], factor * far[1]])
    own, strip, sends = outs[2], outs[3], outs[4:]
    split_grad(conj_product(arr, back_far), 1, offs, margin, own, strip, sends)
    x = dft.forward(conj_product(win, back_far))
    x = dft.inverse(conj_product([kr[...], ki[...]], x))
    split_grad(conj_product([pr[0], pr[1]], x), 0, offs, margin, own, strip, sends)
    grad = conj_product([w1[0], w1[1]], x)
    sy = (margin - offs[0, 0] + n) % n
    sx = (margin - offs[0, 1] + n) % n
    grad = [dyn_roll(dyn_roll(g, sy, 0), sx, 1) for g in grad]
    even = lax.axis_index("row") % 2 == 0
    keep[...] = jnp.where(even, grad[0], grad[1])
    give[...] = jnp.where(even, grad[1], grad[0])


def fold_rows_kernel(n_row, margin, own, strip, *refs):
    got, (total, send_e, send_o) = refs[:n_row], refs[n_row:]
    row_even = lax.axis_index("row") % 2 == 0
    col_even = lax.axis_index("col") % 2 == 0
    n = own.shape[1]
    h = n // 2
    front = iota((n, h), 1) < h // 2
    for s in range(2):
        strips = []
        for i in range(2 * s, 2 * s + 2):
            total[i] = own[i]
            r = got[0][i]
            q = got[1][i] if n_row == 2 else jnp.zeros_like(r)
            top, bottom = jnp.where(row_even, q, r), jnp.where(row_even, r, q)
            total[i, :margin] += top[:, :n]
            total[i, n - margin :] += bottom[:, :n]
            st = strip[i]
            strips.append(
                cat(
                    [
                        st[:margin] + top[:, n:],
                        st[margin : n - margin],
                        st[n - margin :] + bottom[:, n:],
                    ],
                    0,
                )
            )
        moved = half_roll(strips[1])
        to_high = jnp.where(front, strips[0], moved)
        to_low = jnp.where(front, moved, strips[0])
        send_e[s] = jnp.where(col_even, to_high, to_low)
        send_o[s] = jnp.where(col_even, to_low, to_high)


def fold_cols_kernel(total, e, o, out):
    col_even = lax.axis_index("col") % 2 == 0
    n = total.shape[1]
    h = n // 2
    front = iota((n, h), 1) < h // 2
    for s in range(2):
        high = jnp.where(col_even, e[s], o[s])
        low = jnp.where(col_even, o[s], e[s])
        for i in range(2):
            a = low if i == 0 else half_roll(low)
            b = high if i == 0 else half_roll(high)
            at = 2 * s + i
            out[at, :, :h] = total[at, :, :h] + jnp.where(front, a, 0.0)
            out[at, :, h:] = total[at, :, h:] + jnp.where(front, 0.0, b)


def in_hbm(x):
    return pltpu.with_memory_space_constraint(x, pltpu.HBM)


def call(kernel, shapes, in_specs, *args, scratch=(), mib=16):
    shapes = [s if isinstance(s, jax.ShapeDtypeStruct) else jax.ShapeDtypeStruct(s, F32) for s in shapes]
    return pl.pallas_call(
        kernel,
        out_shape=shapes,
        in_specs=in_specs,
        out_specs=[VMEM if s.dtype != jnp.int32 else SMEM for s in shapes],
        scratch_shapes=list(scratch),
        compiler_params=pltpu.CompilerParams(vmem_limit_bytes=mib << 20),
    )(*args)


def edges(axis):
    count = lax.axis_size(axis)
    rounds = []
    for first in (0, 1):
        pairs = [(i, i + 1) for i in range(first, count - 1, 2)]
        pairs += [(b, a) for a, b in pairs]
        if pairs:
            rounds.append(pairs)
    return rounds


def swap(value, axis, distance):
    count = lax.axis_size(axis)
    return lax.ppermute(value, axis, [(i, i ^ distance) for i in range(count)])


def stages(axis, start):
    count = lax.axis_size(axis)
    out = []
    stride = start
    while stride < count:
        width = min(4, count // stride)
        out.append((axis, stride, width))
        stride *= width
    return out


def pair_sum(parts):
    while len(parts) > 1:
        parts = [parts[i] + parts[i + 1] for i in range(0, len(parts), 2)]
    return parts[0]


def reduce_probe(keep, give):
    cols = lax.axis_size("col")
    n = keep.shape[0]
    other = swap(give, "row", 1)
    mine = keep + other
    quad = min(4, cols)
    place = lax.axis_index("col") % quad
    chunk = n // quad
    parts = [
        lax.dynamic_slice_in_dim(mine, (place ^ j) * chunk, chunk, 0) for j in range(quad)
    ]
    sums = [parts[0]]
    for j in range(1, quad):
        sums.append(swap(parts[j], "col", j))
    total = pair_sum(sums)
    for axis, stride, width in stages("col", quad) + stages("row", 2):
        sums = [total]
        for j in range(1, width):
            sums.append(swap(total, axis, stride * j))
        total = pair_sum(sums)
    full = jnp.zeros((quad, chunk, n), F32)
    for j in range(quad):
        part = total if j == 0 else swap(total, "col", j)
        full = lax.dynamic_update_slice(full, part[None], (place ^ j, 0, 0))
    full = full.reshape(n, n)
    other = swap(full, "row", 1)
    even = lax.axis_index("row") % 2 == 0
    return jnp.stack([jnp.where(even, full, other), jnp.where(even, other, full)])


def whole(object_field, probe, phase, amplitudes, offsets):
    tile = object_field.shape[2]
    n = probe.shape[1]
    h = n // 2
    margin = n // 4
    tables = [jnp.asarray(t) for t in dft_constants(n)]
    mats, tw_left, tw_right, order = tables

    row_rounds, col_rounds = edges("row"), edges("col")
    n_row = len(row_rounds)
    *halos, obj, offs = call(
        functools.partial(load_kernel, n_row, margin),
        [(4, margin, n)] * n_row + [(4, n, n), jax.ShapeDtypeStruct((1, 2), jnp.int32)],
        [HBM, HBM],
        in_hbm(object_field.reshape(4, tile, tile)),
        in_hbm(offsets.reshape(1, 2)),
        scratch=[pltpu.SemaphoreType.DMA((n_row + 2,))],
    )
    halos = [lax.ppermute(x, "row", pairs) for x, pairs in zip(halos, row_rounds)]
    length = tile + margin * n_row
    packed = call(
        functools.partial(pack_kernel, n_row),
        [(length, h)] * 4,
        [VMEM] * (1 + n_row),
        obj,
        *halos,
    )
    strips = []
    for i in range(4):
        strips.append(lax.ppermute(packed[i], "col", col_rounds[i % 2]))
    kr, ki, am, pr, mats, tw_left, tw_right = call(
        functools.partial(prep_kernel, margin),
        [(n, n), (n, n), (n, n), (2, n, n)]
        + [jax.ShapeDtypeStruct(t.shape, t.dtype) for t in tables[:3]],
        [SMEM] + [HBM] * 7,
        offs,
        *[in_hbm(x) for x in (phase, amplitudes.reshape(n, n), probe, order)],
        *[in_hbm(x) for x in (mats, tw_left, tw_right)],
        scratch=[
            pltpu.VMEM((n, n), F32),
            pltpu.VMEM((n, n), F32),
            pltpu.VMEM((2, n, n), F32),
            pltpu.VMEM((2, n, n), BF16),
            pltpu.SemaphoreType.DMA((7,)),
        ],
    )
    w1, arrive = call(
        functools.partial(arrive_kernel, n_row, margin),
        [(2, n, n), (2, n, n)],
        [VMEM] * (1 + n_row) + [VMEM, VMEM, SMEM] + [VMEM] * 6,
        obj,
        *halos,
        strips[0],
        strips[1],
        offs,
        pr,
        kr,
        ki,
        mats,
        tw_left,
        tw_right,
    )
    keep, give, own, strip, *sends = call(
        functools.partial(back_kernel, n_row, margin),
        [(n, n), (n, n), (4, n, n), (4, n, h)] + [(4, margin, n + h)] * n_row,
        [VMEM] * (1 + n_row) + [VMEM, VMEM, SMEM] + [VMEM] * 9,
        obj,
        *halos,
        strips[2],
        strips[3],
        offs,
        pr,
        kr,
        ki,
        am,
        w1,
        arrive,
        mats,
        tw_left,
        tw_right,
        mib=40,
    )
    probe_grad = reduce_probe(keep, give)
    got = []
    for i, pairs in enumerate(row_rounds):
        got.append(lax.ppermute(sends[i], "row", pairs))
    total, send_e, send_o = call(
        functools.partial(fold_rows_kernel, n_row, margin),
        [(4, n, n), (2, n, h), (2, n, h)],
        [VMEM] * (2 + n_row),
        own,
        strip,
        *got,
    )
    send_e = lax.ppermute(send_e, "col", col_rounds[0])
    send_o = lax.ppermute(send_o, "col", col_rounds[1])
    (grad,) = call(fold_cols_kernel, [(4, n, n)], [VMEM] * 3, total, send_e, send_o)
    return (grad.reshape(2, 2, tile, tile), probe_grad)


def solution(mesh):
    placed = (
        P(None, None, "row", "col"),
        P(),
        P(),
        P("row", "col", None, None, None),
        P("row", "col", None, None),
    )
    return jax.shard_map(
        whole,
        mesh=mesh,
        in_specs=placed,
        out_specs=(P(None, None, "row", "col"), P()),
        check_vma=False,
    )
```

```python
import functools

import jax
import jax.numpy as jnp
import numpy as np
from jax import lax
from jax.experimental import pallas as pl
from jax.experimental.pallas import tpu as pltpu
from jax.sharding import PartitionSpec as P


EPS_AMP = 0.5
F32 = jnp.float32
BF16 = jnp.bfloat16
VMEM = pl.BlockSpec(memory_space=pltpu.VMEM)
SMEM = pl.BlockSpec(memory_space=pltpu.SMEM)
HBM = pl.BlockSpec(memory_space=pltpu.HBM)


def split_np(table):
    high = table.astype(BF16)
    low = (table - high.astype(np.float64)).astype(BF16)
    return [high, low]


def dft_constants(n):
    h = n // 2
    k = np.arange(h)
    angle = 2.0 * np.pi * ((k[:, None] * k[None, :]) % h) / h
    scale = 1.0 / np.sqrt(n)
    c, s = np.cos(angle) * scale, np.sin(angle) * scale
    d = np.block([[c, s], [-s, c]])
    mats = np.stack(split_np(d) + split_np(d.T))
    w = np.exp(-2j * np.pi * k / n)
    tw_left = np.stack([np.tile(w.real[:, None], (1, h)), np.tile(w.imag[:, None], (1, h))])
    tw_right = np.stack([np.tile(w.real[None], (8, 1)), np.tile(w.imag[None], (8, 1))])
    order = np.zeros((n, n))
    order[2 * k, k] = 1.0
    order[2 * k + 1, h + k] = 1.0
    return (
        mats,
        tw_left.astype(np.float32),
        tw_right.astype(np.float32),
        np.stack([order.T, order]).astype(BF16),
    )


def split(x):
    high = x.astype(BF16)
    return high, (x - high.astype(F32)).astype(BF16)


def dot(a, b):
    return jnp.dot(a, b, preferred_element_type=F32)


def left_dot(mats, which, x):
    high, low = split(x)
    return dot(mats[which], high) + (dot(mats[which], low) + dot(mats[which + 1], high))


def right_dot(x, mats, which):
    high, low = split(x)
    return dot(high, mats[which]) + (dot(low, mats[which]) + dot(high, mats[which + 1]))


def cat(parts, axis):
    return jnp.concatenate(parts, axis=axis)


def product(a, b):
    return (a[0] * b[0] - a[1] * b[1], a[0] * b[1] + a[1] * b[0])


def conj_product(a, b):
    return (a[0] * b[0] + a[1] * b[1], a[0] * b[1] - a[1] * b[0])


class Dft:
    def __init__(self, mats, tw_left, tw_right, n):
        self.mats, self.n, self.h = mats, n, n // 2
        self.wl = [cat([tw_left[i], tw_left[i]], 1) for i in range(2)]
        self.wr = [tw_right[i, 0:1] for i in range(2)]

    def forward(self, x):
        n, h = self.n, self.h
        total = [p[:h] + p[h:] for p in x]
        odd = product([p[:h] - p[h:] for p in x], self.wl)
        y = left_dot(self.mats, 0, cat([cat(total, 0), cat(odd, 0)], 1))
        x = [cat([y[:h, :n], y[:h, n:]], 0), cat([y[h:, :n], y[h:, n:]], 0)]
        total = [p[:, :h] + p[:, h:] for p in x]
        odd = product([p[:, :h] - p[:, h:] for p in x], self.wr)
        y = right_dot(cat([cat(total, 1), cat(odd, 1)], 0), self.mats, 2)
        return [cat([y[:n, :h], y[n:, :h]], 1), cat([y[:n, h:], y[n:, h:]], 1)]

    def inverse(self, x):
        n, h = self.n, self.h
        y = cat([cat([p[:, :h] for p in x], 1), cat([p[:, h:] for p in x], 1)], 0)
        y = right_dot(y, self.mats, 0)
        even = [y[:n, :h], y[:n, h:]]
        odd = conj_product(self.wr, [y[n:, :h], y[n:, h:]])
        x = [cat([e + o, e - o], 1) for e, o in zip(even, odd)]
        y = cat([cat([p[:h] for p in x], 0), cat([p[h:] for p in x], 0)], 1)
        y = left_dot(self.mats, 2, y)
        even = [y[:h, :n], y[h:, :n]]
        odd = conj_product(self.wl, [y[:h, n:], y[h:, n:]])
        return [cat([e + o, e - o], 0) for e, o in zip(even, odd)]


def iota(shape, dim):
    return lax.broadcasted_iota(jnp.int32, shape, dim)


def half_roll(x):
    return pltpu.roll(x, x.shape[-1] // 2, axis=x.ndim - 1)


def pack_cols(re, im):
    h = re.shape[1] // 2
    front = iota((re.shape[0], h), 1) < h // 2
    low = jnp.where(front, re[:, :h], half_roll(im[:, :h]))
    high = jnp.where(front, half_roll(im[:, h:]), re[:, h:])
    return low, high


def copy_all(sources, places, sems):
    copies = [
        pltpu.make_async_copy(a, b, sems.at[i]) for i, (a, b) in enumerate(zip(sources, places))
    ]
    for copy in copies:
        copy.start()
    return copies


def strips_kernel(margin, obj, offs_hbm, *refs):
    offs, strips, sems = refs[0], refs[1:-1], refs[-1]
    n = obj.shape[1]
    even = lax.axis_index("row") % 2 == 0
    sources = [offs_hbm]
    for which in range(len(strips)):
        last = even if which == 0 else jnp.logical_not(even)
        start = pl.multiple_of(jnp.where(last, n - margin, 0), 8)
        sources.append(obj.at[:, pl.ds(start, margin), :])
    for copy in copy_all(sources, [offs, *strips], sems):
        copy.wait()


def load_kernel(*refs):
    half = len(refs) // 2
    for copy in copy_all(refs[:half], refs[half:-1], refs[-1]):
        copy.wait()


def pack_kernel(n_row, obj, *refs):
    halos, outs = refs[:n_row], refs[n_row:]
    even = lax.axis_index("col") % 2 == 0
    for s in range(2):
        sources = [obj] + list(halos)
        at = 0
        for source in sources:
            rows = source.shape[1]
            low, high = pack_cols(source[2 * s], source[2 * s + 1])
            outs[2 * s][at : at + rows] = jnp.where(even, high, low)
            outs[2 * s + 1][at : at + rows] = jnp.where(even, low, high)
            at += rows


def dyn_roll(x, shift, axis):
    return pltpu.roll(x, shift, axis=axis)


def reorder(x, order):
    def thirds(y):
        a = y.astype(BF16)
        return (a,) + split(y - a.astype(F32))

    a, b, c = thirds(x)
    a, b, c = thirds(dot(order[0], a) + (dot(order[0], b) + dot(order[0], c)))
    return dot(a, order[1]) + (dot(b, order[1]) + dot(c, order[1]))


def prep_kernel(margin, phase, probe, order, offs, amps_hbm, mats_hbm, twl_hbm, twr_hbm, *refs):
    kr, ki, pr, amps, mats, twl, twr, sems = refs
    n = phase.shape[0]
    copies = copy_all((mats_hbm, twl_hbm, twr_hbm, amps_hbm), (mats, twl, twr, amps), sems)
    angle = reorder(phase[...], order)
    kr[...] = jnp.cos(angle)
    ki[...] = jnp.sin(angle)
    sy = (offs[0, 0] - margin + n) % n
    sx = (offs[0, 1] - margin + n) % n
    for i in range(2):
        pr[i] = dyn_roll(dyn_roll(probe[i], sy, 0), sx, 1)
    for copy in copies:
        copy.wait()


def reorder_kernel(x, order, after, out):
    out[...] = reorder(x[...], order)


def merge_cols(own, low, high, ox, margin):
    n = own[0].shape[1]
    h = n // 2
    lane = iota((own[0].shape[0], h), 1)
    from_high = lane < ox - margin
    from_low = lane + h >= ox + n - margin
    out = []
    for i in range(2):
        strip_high = high if i == 0 else half_roll(high)
        strip_low = low if i == 0 else half_roll(low)
        out.append(
            cat(
                [
                    jnp.where(from_high, strip_high, own[i][:, :h]),
                    jnp.where(from_low, strip_low, own[i][:, h:]),
                ],
                1,
            )
        )
    return out


def window_of(obj, s, halos, strip_e, strip_o, offs, margin):
    n = obj.shape[1]
    oy, ox = offs[0, 0], offs[0, 1]
    col_even = lax.axis_index("col") % 2 == 0
    row_even = lax.axis_index("row") % 2 == 0
    blocks = []
    at = 0
    for source in [obj] + list(halos):
        rows = source.shape[1]
        e, o = strip_e[at : at + rows], strip_o[at : at + rows]
        high, low = jnp.where(col_even, e, o), jnp.where(col_even, o, e)
        blocks.append(merge_cols([source[2 * s], source[2 * s + 1]], low, high, ox, margin))
        at += rows
    row = iota((margin, n), 0)
    take_high = row < oy - margin
    take_low = row + n - margin >= oy + n - margin
    out = []
    for i in range(2):
        main = blocks[0][i]
        if len(blocks) == 3:
            e, o = blocks[1][i], blocks[2][i]
            high, low = jnp.where(row_even, e, o), jnp.where(row_even, o, e)
        else:
            e = blocks[1][i]
            zero = jnp.zeros_like(e)
            high, low = jnp.where(row_even, e, zero), jnp.where(row_even, zero, e)
        out.append(
            cat(
                [
                    jnp.where(take_high, high, main[:margin]),
                    main[margin : n - margin],
                    jnp.where(take_low, low, main[n - margin :]),
                ],
                0,
            )
        )
    return out


def arrive_kernel(n_row, margin, *refs):
    obj, halos = refs[0], refs[1 : 1 + n_row]
    e1, o1, offs, pr, kr, ki, mats, twl, twr, w1, arrive = refs[1 + n_row :]
    n = obj.shape[1]
    dft = Dft(mats, twl[...], twr[...], n)
    win = window_of(obj, 0, halos, e1, o1, offs, margin)
    w1[0], w1[1] = win
    x = dft.forward(product([pr[0], pr[1]], win))
    x = dft.inverse(product([kr[...], ki[...]], x))
    arrive[0], arrive[1] = x


def split_grad(grad, s, offs, margin, own, strip, sends):
    n = grad[0].shape[0]
    h = n // 2
    oy, ox = offs[0, 0], offs[0, 1]
    row_even = lax.axis_index("row") % 2 == 0
    lane = iota((1, h), 1)
    to_high, to_low = lane < ox - margin, lane + h >= ox + n - margin
    front = lane < h // 2
    spill = jnp.where(front, to_high.astype(jnp.int32), to_low.astype(jnp.int32)) != 0
    for i in range(2):
        g = grad[i]
        row = iota((n, h), 0)
        high_rows = row < oy - margin
        low_rows = row >= oy + n - margin
        inner = jnp.logical_not(jnp.logical_or(high_rows, low_rows))
        left = jnp.where(to_high, 0.0, g[:, :h])
        right = jnp.where(to_low, 0.0, g[:, h:])
        side = jnp.where(spill, jnp.where(front, g[:, :h], g[:, h:]), 0.0)
        pieces = [left, right, side]
        own[2 * s + i, :, :h] = jnp.where(inner, left, 0.0)
        own[2 * s + i, :, h:] = jnp.where(inner, right, 0.0)
        strip[2 * s + i] = jnp.where(inner, side, 0.0)
        for j, piece in enumerate(pieces):
            top = jnp.where(high_rows[:margin], piece[:margin], 0.0)
            bottom = jnp.where(low_rows[n - margin :], piece[n - margin :], 0.0)
            for which, send in enumerate(sends):
                first = row_even if which == 0 else jnp.logical_not(row_even)
                send[2 * s + i, :, j * h : (j + 1) * h] = jnp.where(first, top, bottom)


def back_kernel(n_row, margin, *refs):
    obj, halos = refs[0], refs[1 : 1 + n_row]
    e2, o2, offs, pr, kr, ki, am, w1, arrive, mats, twl, twr = refs[1 + n_row : 13 + n_row]
    outs = refs[13 + n_row :]
    keep, give = outs[:2]
    n = obj.shape[1]
    dft = Dft(mats, twl[...], twr[...], n)
    win = window_of(obj, 1, halos, e2, o2, offs, margin)
    arr = [arrive[0], arrive[1]]
    far = dft.forward(product(arr, win))
    modulus = jnp.sqrt(far[0] * far[0] + far[1] * far[1] + EPS_AMP)
    factor = 2.0 * (1.0 - am[...] / modulus)
    back_far = dft.inverse([factor * far[0], factor * far[1]])
    own, strip, sends = outs[2], outs[3], outs[4:]
    split_grad(conj_product(arr, back_far), 1, offs, margin, own, strip, sends)
    x = dft.forward(conj_product(win, back_far))
    x = dft.inverse(conj_product([kr[...], ki[...]], x))
    split_grad(conj_product([pr[0], pr[1]], x), 0, offs, margin, own, strip, sends)
    grad = conj_product([w1[0], w1[1]], x)
    sy = (margin - offs[0, 0] + n) % n
    sx = (margin - offs[0, 1] + n) % n
    grad = [dyn_roll(dyn_roll(g, sy, 0), sx, 1) for g in grad]
    even = lax.axis_index("row") % 2 == 0
    keep[...] = jnp.where(even, grad[0], grad[1])
    give[...] = jnp.where(even, grad[1], grad[0])


def fold_rows_kernel(n_row, margin, own, strip, *refs):
    got, (total, send_e, send_o) = refs[:n_row], refs[n_row:]
    row_even = lax.axis_index("row") % 2 == 0
    col_even = lax.axis_index("col") % 2 == 0
    n = own.shape[1]
    h = n // 2
    front = iota((n, h), 1) < h // 2
    for s in range(2):
        strips = []
        for i in range(2 * s, 2 * s + 2):
            total[i] = own[i]
            r = got[0][i]
            q = got[1][i] if n_row == 2 else jnp.zeros_like(r)
            top, bottom = jnp.where(row_even, q, r), jnp.where(row_even, r, q)
            total[i, :margin] += top[:, :n]
            total[i, n - margin :] += bottom[:, :n]
            st = strip[i]
            strips.append(
                cat(
                    [
                        st[:margin] + top[:, n:],
                        st[margin : n - margin],
                        st[n - margin :] + bottom[:, n:],
                    ],
                    0,
                )
            )
        moved = half_roll(strips[1])
        to_high = jnp.where(front, strips[0], moved)
        to_low = jnp.where(front, moved, strips[0])
        send_e[s] = jnp.where(col_even, to_high, to_low)
        send_o[s] = jnp.where(col_even, to_low, to_high)


def fold_cols_kernel(total, e, o, out):
    col_even = lax.axis_index("col") % 2 == 0
    n = total.shape[1]
    h = n // 2
    front = iota((n, h), 1) < h // 2
    for s in range(2):
        high = jnp.where(col_even, e[s], o[s])
        low = jnp.where(col_even, o[s], e[s])
        for i in range(2):
            a = low if i == 0 else half_roll(low)
            b = high if i == 0 else half_roll(high)
            at = 2 * s + i
            out[at, :, :h] = total[at, :, :h] + jnp.where(front, a, 0.0)
            out[at, :, h:] = total[at, :, h:] + jnp.where(front, 0.0, b)


def in_hbm(x):
    return pltpu.with_memory_space_constraint(x, pltpu.HBM)


def call(kernel, shapes, in_specs, *args, scratch=(), mib=16):
    shapes = [s if isinstance(s, jax.ShapeDtypeStruct) else jax.ShapeDtypeStruct(s, F32) for s in shapes]
    return pl.pallas_call(
        kernel,
        out_shape=shapes,
        in_specs=in_specs,
        out_specs=[VMEM if s.dtype != jnp.int32 else SMEM for s in shapes],
        scratch_shapes=list(scratch),
        compiler_params=pltpu.CompilerParams(vmem_limit_bytes=mib << 20),
    )(*args)


def edges(axis):
    count = lax.axis_size(axis)
    rounds = []
    for first in (0, 1):
        pairs = [(i, i + 1) for i in range(first, count - 1, 2)]
        pairs += [(b, a) for a, b in pairs]
        if pairs:
            rounds.append(pairs)
    return rounds


def swap(value, axis, distance):
    count = lax.axis_size(axis)
    return lax.ppermute(value, axis, [(i, i ^ distance) for i in range(count)])


def stages(axis, start):
    count = lax.axis_size(axis)
    out = []
    stride = start
    while stride < count:
        width = min(4, count // stride)
        out.append((axis, stride, width))
        stride *= width
    return out


def pair_sum(parts):
    while len(parts) > 1:
        parts = [parts[i] + parts[i + 1] for i in range(0, len(parts), 2)]
    return parts[0]


def share_kernel(quad, keep, other, *parts):
    place = lax.axis_index("col") % quad
    chunk = keep.shape[0] // quad
    for j, part in enumerate(parts):
        rows = pl.ds(pl.multiple_of((place ^ j) * chunk, 8), chunk)
        part[...] = keep[rows, :] + other[rows, :]


def sum_kernel(*refs):
    refs[-1][...] = pair_sum([r[...] for r in refs[:-1]])


def join_kernel(*refs):
    parts, full = refs[:-1], refs[-1]
    quad, chunk = len(parts), parts[0].shape[0]
    place = lax.axis_index("col") % quad
    for j, part in enumerate(parts):
        full[pl.ds(pl.multiple_of((place ^ j) * chunk, 8), chunk), :] = part[...]


def both_kernel(full, other, out):
    even = lax.axis_index("row") % 2 == 0
    out[0] = jnp.where(even, full[...], other[...])
    out[1] = jnp.where(even, other[...], full[...])


def reduce_probe(keep, give):
    cols = lax.axis_size("col")
    n = keep.shape[0]
    other = swap(give, "row", 1)
    quad = min(4, cols)
    chunk = n // quad
    parts = call(
        functools.partial(share_kernel, quad), [(chunk, n)] * quad, [VMEM] * 2, keep, other
    )
    sums = [parts[0]]
    for j in range(1, quad):
        sums.append(swap(parts[j], "col", j))
    (total,) = call(sum_kernel, [(chunk, n)], [VMEM] * quad, *sums)
    for axis, stride, width in stages("col", quad) + stages("row", 2):
        sums = [total]
        for j in range(1, width):
            sums.append(swap(total, axis, stride * j))
        (total,) = call(sum_kernel, [(chunk, n)], [VMEM] * width, *sums)
    parts = [total]
    for j in range(1, quad):
        parts.append(swap(total, "col", j))
    (full,) = call(join_kernel, [(n, n)], [VMEM] * quad, *parts)
    other = swap(full, "row", 1)
    (grad,) = call(both_kernel, [(2, n, n)], [VMEM] * 2, full, other)
    return grad


def whole(object_field, probe, phase, amplitudes, offsets):
    tile = object_field.shape[2]
    n = probe.shape[1]
    h = n // 2
    margin = n // 4
    tables = [jnp.asarray(t) for t in dft_constants(n)]
    mats, tw_left, tw_right, order = tables

    row_rounds, col_rounds = edges("row"), edges("col")
    n_row = len(row_rounds)
    whole_tile = in_hbm(object_field.reshape(4, tile, tile))
    offs, *halos = call(
        functools.partial(strips_kernel, margin),
        [jax.ShapeDtypeStruct((1, 2), jnp.int32)] + [(4, margin, n)] * n_row,
        [HBM, HBM],
        whole_tile,
        in_hbm(offsets.reshape(1, 2)),
        scratch=[pltpu.SemaphoreType.DMA((n_row + 1,))],
    )
    halos = [lax.ppermute(x, "row", pairs) for x, pairs in zip(halos, row_rounds)]
    first = [whole_tile] + [in_hbm(x) for x in (phase, probe, order)]
    obj, phase, probe, order = call(
        load_kernel,
        [jax.ShapeDtypeStruct(x.shape, x.dtype) for x in first],
        [HBM] * len(first),
        *first,
        scratch=[pltpu.SemaphoreType.DMA((len(first),))],
    )
    length = tile + margin * n_row
    packed = call(
        functools.partial(pack_kernel, n_row),
        [(length, h)] * 4,
        [VMEM] * (1 + n_row),
        obj,
        *halos,
    )
    strips = []
    for i in range(4):
        strips.append(lax.ppermute(packed[i], "col", col_rounds[i % 2]))
    later = [in_hbm(x) for x in (amplitudes.reshape(n, n), mats, tw_left, tw_right)]
    kr, ki, pr, am, mats, tw_left, tw_right = call(
        functools.partial(prep_kernel, margin),
        [(n, n), (n, n), (2, n, n)]
        + [jax.ShapeDtypeStruct(x.shape, x.dtype) for x in later],
        [VMEM, VMEM, VMEM, SMEM] + [HBM] * 4,
        phase,
        probe,
        order,
        offs,
        *later,
        scratch=[pltpu.SemaphoreType.DMA((4,))],
    )
    w1, arrive = call(
        functools.partial(arrive_kernel, n_row, margin),
        [(2, n, n), (2, n, n)],
        [VMEM] * (1 + n_row) + [VMEM, VMEM, SMEM] + [VMEM] * 6,
        obj,
        *halos,
        strips[0],
        strips[1],
        offs,
        pr,
        kr,
        ki,
        mats,
        tw_left,
        tw_right,
    )
    (am,) = call(reorder_kernel, [(n, n)], [VMEM] * 3, am, order, arrive)
    keep, give, own, strip, *sends = call(
        functools.partial(back_kernel, n_row, margin),
        [(n, n), (n, n), (4, n, n), (4, n, h)] + [(4, margin, n + h)] * n_row,
        [VMEM] * (1 + n_row) + [VMEM, VMEM, SMEM] + [VMEM] * 9,
        obj,
        *halos,
        strips[2],
        strips[3],
        offs,
        pr,
        kr,
        ki,
        am,
        w1,
        arrive,
        mats,
        tw_left,
        tw_right,
        mib=40,
    )
    probe_grad = reduce_probe(keep, give)
    got = []
    for i, pairs in enumerate(row_rounds):
        got.append(lax.ppermute(sends[i], "row", pairs))
    total, send_e, send_o = call(
        functools.partial(fold_rows_kernel, n_row, margin),
        [(4, n, n), (2, n, h), (2, n, h)],
        [VMEM] * (2 + n_row),
        own,
        strip,
        *got,
    )
    send_e = lax.ppermute(send_e, "col", col_rounds[0])
    send_o = lax.ppermute(send_o, "col", col_rounds[1])
    (grad,) = call(fold_cols_kernel, [(4, n, n)], [VMEM] * 3, total, send_e, send_o)
    return (grad.reshape(2, 2, tile, tile), probe_grad)


def solution(mesh):
    placed = (
        P(None, None, "row", "col"),
        P(),
        P(),
        P("row", "col", None, None, None),
        P("row", "col", None, None),
    )
    return jax.shard_map(
        whole,
        mesh=mesh,
        in_specs=placed,
        out_specs=(P(None, None, "row", "col"), P()),
        check_vma=False,
    )
```

```python
import functools

import jax
import jax.numpy as jnp
import numpy as np
from jax import lax
from jax.experimental import pallas as pl
from jax.experimental.pallas import tpu as pltpu
from jax.sharding import PartitionSpec as P


EPS_AMP = 0.5
F32 = jnp.float32
BF16 = jnp.bfloat16
VMEM = pl.BlockSpec(memory_space=pltpu.VMEM)
SMEM = pl.BlockSpec(memory_space=pltpu.SMEM)
HBM = pl.BlockSpec(memory_space=pltpu.HBM)


def split_np(table):
    high = table.astype(BF16)
    low = (table - high.astype(np.float64)).astype(BF16)
    return [high, low]


def dft_constants(n):
    h = n // 2
    k = np.arange(h)
    angle = 2.0 * np.pi * ((k[:, None] * k[None, :]) % h) / h
    scale = 1.0 / np.sqrt(n)
    c, s = np.cos(angle) * scale, np.sin(angle) * scale
    d = np.block([[c, s], [-s, c]])
    mats = np.stack(split_np(d) + split_np(d.T))
    w = np.exp(-2j * np.pi * k / n)
    tw_left = np.stack([np.tile(w.real[:, None], (1, h)), np.tile(w.imag[:, None], (1, h))])
    tw_right = np.stack([np.tile(w.real[None], (8, 1)), np.tile(w.imag[None], (8, 1))])
    order = np.zeros((n, n))
    order[2 * k, k] = 1.0
    order[2 * k + 1, h + k] = 1.0
    return (
        mats,
        tw_left.astype(np.float32),
        tw_right.astype(np.float32),
        np.stack([order.T, order]).astype(BF16),
    )


def split(x):
    high = x.astype(BF16)
    return high, (x - high.astype(F32)).astype(BF16)


def dot(a, b):
    return jnp.dot(a, b, preferred_element_type=F32)


def left_dot(mats, which, x):
    high, low = split(x)
    return dot(mats[which], high) + (dot(mats[which], low) + dot(mats[which + 1], high))


def right_dot(x, mats, which):
    high, low = split(x)
    return dot(high, mats[which]) + (dot(low, mats[which]) + dot(high, mats[which + 1]))


def cat(parts, axis):
    return jnp.concatenate(parts, axis=axis)


def product(a, b):
    return (a[0] * b[0] - a[1] * b[1], a[0] * b[1] + a[1] * b[0])


def conj_product(a, b):
    return (a[0] * b[0] + a[1] * b[1], a[0] * b[1] - a[1] * b[0])


class Dft:
    def __init__(self, mats, tw_left, tw_right, n):
        self.mats, self.n, self.h = mats, n, n // 2
        self.wl = [cat([tw_left[i], tw_left[i]], 1) for i in range(2)]
        self.wr = [tw_right[i, 0:1] for i in range(2)]

    def forward(self, x):
        n, h = self.n, self.h
        total = [p[:h] + p[h:] for p in x]
        odd = product([p[:h] - p[h:] for p in x], self.wl)
        y = left_dot(self.mats, 0, cat([cat(total, 0), cat(odd, 0)], 1))
        x = [cat([y[:h, :n], y[:h, n:]], 0), cat([y[h:, :n], y[h:, n:]], 0)]
        total = [p[:, :h] + p[:, h:] for p in x]
        odd = product([p[:, :h] - p[:, h:] for p in x], self.wr)
        y = right_dot(cat([cat(total, 1), cat(odd, 1)], 0), self.mats, 2)
        return [cat([y[:n, :h], y[n:, :h]], 1), cat([y[:n, h:], y[n:, h:]], 1)]

    def inverse(self, x):
        n, h = self.n, self.h
        y = cat([cat([p[:, :h] for p in x], 1), cat([p[:, h:] for p in x], 1)], 0)
        y = right_dot(y, self.mats, 0)
        even = [y[:n, :h], y[:n, h:]]
        odd = conj_product(self.wr, [y[n:, :h], y[n:, h:]])
        x = [cat([e + o, e - o], 1) for e, o in zip(even, odd)]
        y = cat([cat([p[:h] for p in x], 0), cat([p[h:] for p in x], 0)], 1)
        y = left_dot(self.mats, 2, y)
        even = [y[:h, :n], y[h:, :n]]
        odd = conj_product(self.wl, [y[:h, n:], y[h:, n:]])
        return [cat([e + o, e - o], 0) for e, o in zip(even, odd)]


def iota(shape, dim):
    return lax.broadcasted_iota(jnp.int32, shape, dim)


def dyn_roll(x, shift, axis):
    return pltpu.roll(x, shift, axis=axis)


def half_roll(x):
    return pltpu.roll(x, x.shape[-1] // 2, axis=x.ndim - 1)


def pack_cols(re, im):
    h = re.shape[1] // 2
    front = iota((re.shape[0], h), 1) < h // 2
    low = jnp.where(front, re[:, :h], half_roll(im[:, :h]))
    high = jnp.where(front, half_roll(im[:, h:]), re[:, h:])
    return low, high


def copy_all(sources, places, sems):
    copies = [
        pltpu.make_async_copy(a, b, sems.at[i]) for i, (a, b) in enumerate(zip(sources, places))
    ]
    for copy in copies:
        copy.start()
    return copies


def row_start(which, n, margin):
    even = lax.axis_index("row") % 2 == 0
    last = even if which == 0 else jnp.logical_not(even)
    return pl.multiple_of(jnp.where(last, n - margin, 0), 8)


def pack_kernel(margin, obj_hbm, offs_hbm, obj, offs, *refs):
    strips, rows, sems = refs[:4], refs[4:-1], refs[-1]
    n = obj.shape[1]
    copies = copy_all(
        (obj_hbm.at[0:2], obj_hbm.at[2:4], offs_hbm), (obj.at[0:2], obj.at[2:4], offs), sems
    )
    even = lax.axis_index("col") % 2 == 0
    for s in range(2):
        copies[s].wait()
        low, high = pack_cols(obj[2 * s], obj[2 * s + 1])
        strips[2 * s][...] = jnp.where(even, high, low)
        strips[2 * s + 1][...] = jnp.where(even, low, high)
    for which, out in enumerate(rows):
        out[...] = obj[:, pl.ds(row_start(which, n, margin), margin), :]
    copies[2].wait()


def corner_kernel(margin, e, o, after, *outs):
    for which, out in enumerate(outs):
        rows = pl.ds(row_start(which, e.shape[0], margin), margin)
        out[0] = e[rows, :]
        out[1] = o[rows, :]


def reorder(x, order):
    def thirds(y):
        a = y.astype(BF16)
        return (a,) + split(y - a.astype(F32))

    a, b, c = thirds(x)
    a, b, c = thirds(dot(order[0], a) + (dot(order[0], b) + dot(order[0], c)))
    return dot(a, order[1]) + (dot(b, order[1]) + dot(c, order[1]))


def prep_kernel(*refs):
    hbm, (kr, ki), loaded = refs[:7], refs[7:9], refs[9:15]
    phase, sems = refs[15:]
    copies = copy_all(hbm, (phase,) + loaded, sems)
    copies[0].wait()
    copies[1].wait()
    angle = reorder(phase[...], loaded[0])
    kr[...] = jnp.cos(angle)
    ki[...] = jnp.sin(angle)
    for copy in copies[2:]:
        copy.wait()


def roll_kernel(margin, offs, probe, pr):
    n = probe.shape[1]
    sy = (offs[0, 0] - margin + n) % n
    sx = (offs[0, 1] - margin + n) % n
    for i in range(2):
        pr[i] = dyn_roll(dyn_roll(probe[i], sy, 0), sx, 1)


def reorder_kernel(x, order, after, out):
    out[...] = reorder(x[...], order)


def merge_cols(own, low, high, ox, margin):
    n = own[0].shape[1]
    h = n // 2
    lane = iota((own[0].shape[0], h), 1)
    from_high = lane < ox - margin
    from_low = lane + h >= ox + n - margin
    out = []
    for i in range(2):
        strip_high = high if i == 0 else half_roll(high)
        strip_low = low if i == 0 else half_roll(low)
        out.append(
            cat(
                [
                    jnp.where(from_high, strip_high, own[i][:, :h]),
                    jnp.where(from_low, strip_low, own[i][:, h:]),
                ],
                1,
            )
        )
    return out


def window_of(obj, s, halos, corners, strip_e, strip_o, offs, margin):
    n = obj.shape[1]
    oy, ox = offs[0, 0], offs[0, 1]
    col_even = lax.axis_index("col") % 2 == 0
    row_even = lax.axis_index("row") % 2 == 0
    blocks = []
    sides = [(strip_e, strip_o)] + [(c.at[0], c.at[1]) for c in corners]
    for source, (e, o) in zip([obj] + list(halos), sides):
        e, o = e[...], o[...]
        high, low = jnp.where(col_even, e, o), jnp.where(col_even, o, e)
        blocks.append(merge_cols([source[2 * s], source[2 * s + 1]], low, high, ox, margin))
    row = iota((margin, n), 0)
    take_high = row < oy - margin
    take_low = row + n - margin >= oy + n - margin
    out = []
    for i in range(2):
        main = blocks[0][i]
        if len(blocks) == 3:
            e, o = blocks[1][i], blocks[2][i]
            high, low = jnp.where(row_even, e, o), jnp.where(row_even, o, e)
        else:
            e = blocks[1][i]
            zero = jnp.zeros_like(e)
            high, low = jnp.where(row_even, e, zero), jnp.where(row_even, zero, e)
        out.append(
            cat(
                [
                    jnp.where(take_high, high, main[:margin]),
                    main[margin : n - margin],
                    jnp.where(take_low, low, main[n - margin :]),
                ],
                0,
            )
        )
    return out


def unpack(n_row, refs):
    return refs[0], refs[1 : 1 + n_row], refs[1 + n_row : 1 + 2 * n_row], refs[1 + 2 * n_row :]


def arrive_kernel(n_row, margin, *refs):
    obj, halos, corners, refs = unpack(n_row, refs)
    e1, o1, offs, pr, kr, ki, mats, twl, twr, w1, arrive = refs
    n = obj.shape[1]
    dft = Dft(mats, twl[...], twr[...], n)
    win = window_of(obj, 0, halos, corners, e1, o1, offs, margin)
    w1[0], w1[1] = win
    x = dft.forward(product([pr[0], pr[1]], win))
    x = dft.inverse(product([kr[...], ki[...]], x))
    arrive[0], arrive[1] = x


def split_grad(grad, s, offs, margin, own, strip, sends):
    n = grad[0].shape[0]
    h = n // 2
    oy, ox = offs[0, 0], offs[0, 1]
    row_even = lax.axis_index("row") % 2 == 0
    lane = iota((1, h), 1)
    to_high, to_low = lane < ox - margin, lane + h >= ox + n - margin
    front = lane < h // 2
    spill = jnp.where(front, to_high.astype(jnp.int32), to_low.astype(jnp.int32)) != 0
    for i in range(2):
        g = grad[i]
        row = iota((n, h), 0)
        high_rows = row < oy - margin
        low_rows = row >= oy + n - margin
        inner = jnp.logical_not(jnp.logical_or(high_rows, low_rows))
        left = jnp.where(to_high, 0.0, g[:, :h])
        right = jnp.where(to_low, 0.0, g[:, h:])
        side = jnp.where(spill, jnp.where(front, g[:, :h], g[:, h:]), 0.0)
        pieces = [left, right, side]
        own[2 * s + i, :, :h] = jnp.where(inner, left, 0.0)
        own[2 * s + i, :, h:] = jnp.where(inner, right, 0.0)
        strip[2 * s + i] = jnp.where(inner, side, 0.0)
        for j, piece in enumerate(pieces):
            top = jnp.where(high_rows[:margin], piece[:margin], 0.0)
            bottom = jnp.where(low_rows[n - margin :], piece[n - margin :], 0.0)
            for which, send in enumerate(sends):
                first = row_even if which == 0 else jnp.logical_not(row_even)
                send[2 * s + i, :, j * h : (j + 1) * h] = jnp.where(first, top, bottom)


def back_kernel(n_row, margin, *refs):
    obj, halos, corners, refs = unpack(n_row, refs)
    e2, o2, offs, pr, kr, ki, am, w1, arrive, mats, twl, twr = refs[:12]
    outs = refs[12:]
    keep, give = outs[:2]
    n = obj.shape[1]
    dft = Dft(mats, twl[...], twr[...], n)
    win = window_of(obj, 1, halos, corners, e2, o2, offs, margin)
    arr = [arrive[0], arrive[1]]
    far = dft.forward(product(arr, win))
    modulus = jnp.sqrt(far[0] * far[0] + far[1] * far[1] + EPS_AMP)
    factor = 2.0 * (1.0 - am[...] / modulus)
    back_far = dft.inverse([factor * far[0], factor * far[1]])
    own, strip, sends = outs[2], outs[3], outs[4:]
    split_grad(conj_product(arr, back_far), 1, offs, margin, own, strip, sends)
    x = dft.forward(conj_product(win, back_far))
    x = dft.inverse(conj_product([kr[...], ki[...]], x))
    split_grad(conj_product([pr[0], pr[1]], x), 0, offs, margin, own, strip, sends)
    grad = conj_product([w1[0], w1[1]], x)
    sy = (margin - offs[0, 0] + n) % n
    sx = (margin - offs[0, 1] + n) % n
    grad = [dyn_roll(dyn_roll(g, sy, 0), sx, 1) for g in grad]
    even = lax.axis_index("row") % 2 == 0
    keep[...] = jnp.where(even, grad[0], grad[1])
    give[...] = jnp.where(even, grad[1], grad[0])


def fold_rows_kernel(n_row, margin, own, strip, *refs):
    got, (total, send_e, send_o) = refs[:n_row], refs[n_row:]
    row_even = lax.axis_index("row") % 2 == 0
    col_even = lax.axis_index("col") % 2 == 0
    n = own.shape[1]
    h = n // 2
    front = iota((n, h), 1) < h // 2
    for s in range(2):
        strips = []
        for i in range(2 * s, 2 * s + 2):
            total[i] = own[i]
            r = got[0][i]
            q = got[1][i] if n_row == 2 else jnp.zeros_like(r)
            top, bottom = jnp.where(row_even, q, r), jnp.where(row_even, r, q)
            total[i, :margin] += top[:, :n]
            total[i, n - margin :] += bottom[:, :n]
            st = strip[i]
            strips.append(
                cat(
                    [
                        st[:margin] + top[:, n:],
                        st[margin : n - margin],
                        st[n - margin :] + bottom[:, n:],
                    ],
                    0,
                )
            )
        moved = half_roll(strips[1])
        to_high = jnp.where(front, strips[0], moved)
        to_low = jnp.where(front, moved, strips[0])
        send_e[s] = jnp.where(col_even, to_high, to_low)
        send_o[s] = jnp.where(col_even, to_low, to_high)


def fold_cols_kernel(total, e, o, out):
    col_even = lax.axis_index("col") % 2 == 0
    n = total.shape[1]
    h = n // 2
    front = iota((n, h), 1) < h // 2
    for s in range(2):
        high = jnp.where(col_even, e[s], o[s])
        low = jnp.where(col_even, o[s], e[s])
        for i in range(2):
            a = low if i == 0 else half_roll(low)
            b = high if i == 0 else half_roll(high)
            at = 2 * s + i
            out[at, :, :h] = total[at, :, :h] + jnp.where(front, a, 0.0)
            out[at, :, h:] = total[at, :, h:] + jnp.where(front, 0.0, b)


def in_hbm(x):
    return pltpu.with_memory_space_constraint(x, pltpu.HBM)


def call(kernel, shapes, in_specs, *args, scratch=(), mib=16):
    shapes = [s if isinstance(s, jax.ShapeDtypeStruct) else jax.ShapeDtypeStruct(s, F32) for s in shapes]
    return pl.pallas_call(
        kernel,
        out_shape=shapes,
        in_specs=in_specs,
        out_specs=[VMEM if s.dtype != jnp.int32 else SMEM for s in shapes],
        scratch_shapes=list(scratch),
        compiler_params=pltpu.CompilerParams(vmem_limit_bytes=mib << 20),
    )(*args)


def edges(axis):
    count = lax.axis_size(axis)
    rounds = []
    for first in (0, 1):
        pairs = [(i, i + 1) for i in range(first, count - 1, 2)]
        pairs += [(b, a) for a, b in pairs]
        if pairs:
            rounds.append(pairs)
    return rounds


def swap(value, axis, distance):
    count = lax.axis_size(axis)
    return lax.ppermute(value, axis, [(i, i ^ distance) for i in range(count)])


def groups():
    cols = [("col", 1 << b) for b in range(lax.axis_size("col").bit_length() - 1)]
    rows = [("row", 1 << b) for b in range(1, lax.axis_size("row").bit_length() - 1)]
    first, rest = cols[:2], cols[2:]
    pairs = [first]
    for bits in (rest, rows):
        pairs += [bits[i : i + 2] for i in range(0, len(bits), 2)]
    out = []
    for pair in pairs:
        axis, masks = pair[0][0], [m for _, m in pair]
        out.append((axis, [0] + masks + ([sum(masks)] if len(masks) == 2 else [])))
    return out


def pair_sum(parts):
    while len(parts) > 1:
        parts = [parts[i] + parts[i + 1] for i in range(0, len(parts), 2)]
    return parts[0]


def share_kernel(quad, stride, keep, other, *parts):
    place = lax.axis_index("col") // stride % quad
    chunk = keep.shape[0] // quad
    for j, part in enumerate(parts):
        rows = pl.ds(pl.multiple_of((place ^ j) * chunk, 8), chunk)
        part[...] = keep[rows, :] + other[rows, :]


def sum_kernel(*refs):
    refs[-1][...] = pair_sum([r[...] for r in refs[:-1]])


def join_kernel(stride, *refs):
    parts, full = refs[:-1], refs[-1]
    quad, chunk = len(parts), parts[0].shape[0]
    place = lax.axis_index("col") // stride % quad
    for j, part in enumerate(parts):
        full[pl.ds(pl.multiple_of((place ^ j) * chunk, 8), chunk), :] = part[...]


def both_kernel(full, other, out):
    even = lax.axis_index("row") % 2 == 0
    out[0] = jnp.where(even, full[...], other[...])
    out[1] = jnp.where(even, other[...], full[...])


def reduce_probe(keep, give):
    n = keep.shape[0]
    (_, offsets), *rest = groups()
    quad, stride = len(offsets), offsets[1]
    chunk = n // quad
    other = swap(give, "row", 1)
    parts = call(
        functools.partial(share_kernel, quad, stride),
        [(chunk, n)] * quad,
        [VMEM] * 2,
        keep,
        other,
    )
    sums = [parts[0]]
    for j in range(1, quad):
        sums.append(swap(parts[j], "col", offsets[j]))
    (total,) = call(sum_kernel, [(chunk, n)], [VMEM] * quad, *sums)
    for axis, masks in rest:
        sums = [total]
        for mask in masks[1:]:
            sums.append(swap(total, axis, mask))
        (total,) = call(sum_kernel, [(chunk, n)], [VMEM] * len(sums), *sums)
    parts = [total]
    for j in range(1, quad):
        parts.append(swap(total, "col", offsets[j]))
    (full,) = call(
        functools.partial(join_kernel, stride), [(n, n)], [VMEM] * quad, *parts
    )
    other = swap(full, "row", 1)
    (grad,) = call(both_kernel, [(2, n, n)], [VMEM] * 2, full, other)
    return grad


def whole(object_field, probe, phase, amplitudes, offsets):
    tile = object_field.shape[2]
    n = probe.shape[1]
    h = n // 2
    margin = n // 4
    tables = [jnp.asarray(t) for t in dft_constants(n)]
    mats, tw_left, tw_right, order = tables

    row_rounds, col_rounds = edges("row"), edges("col")
    n_row = len(row_rounds)
    obj, offs, *packed = call(
        functools.partial(pack_kernel, margin),
        [(4, n, n), jax.ShapeDtypeStruct((1, 2), jnp.int32)]
        + [(n, h)] * 4
        + [(4, margin, n)] * n_row,
        [HBM, HBM],
        in_hbm(object_field.reshape(4, tile, tile)),
        in_hbm(offsets.reshape(1, 2)),
        scratch=[pltpu.SemaphoreType.DMA((3,))],
    )
    strips, halos, corners = [], [], [[], []]
    for i in range(4):
        strips.append(lax.ppermute(packed[i], "col", col_rounds[i % 2]))
    for i, pairs in enumerate(row_rounds):
        halos.append(lax.ppermute(packed[4 + i], "row", pairs))

    def cut(s, after):
        parts = call(
            functools.partial(corner_kernel, margin),
            [(2, margin, h)] * n_row,
            [VMEM] * 3,
            *strips[2 * s : 2 * s + 2],
            after,
        )
        for i, pairs in enumerate(row_rounds):
            corners[s].append(lax.ppermute(parts[i], "row", pairs))

    loads = (phase, order, mats, tw_left, tw_right, probe, amplitudes.reshape(n, n))
    kr, ki, order, mats, tw_left, tw_right, pr, am = call(
        prep_kernel,
        [(n, n), (n, n)] + [jax.ShapeDtypeStruct(x.shape, x.dtype) for x in loads[1:]],
        [HBM] * len(loads),
        *[in_hbm(x) for x in loads],
        scratch=[pltpu.VMEM((n, n), F32), pltpu.SemaphoreType.DMA((len(loads),))],
    )
    cut(0, kr)
    (pr,) = call(functools.partial(roll_kernel, margin), [(2, n, n)], [SMEM, VMEM], offs, pr)
    w1, arrive = call(
        functools.partial(arrive_kernel, n_row, margin),
        [(2, n, n), (2, n, n)],
        [VMEM] * (3 + 2 * n_row) + [SMEM] + [VMEM] * 6,
        obj,
        *halos,
        *corners[0],
        strips[0],
        strips[1],
        offs,
        pr,
        kr,
        ki,
        mats,
        tw_left,
        tw_right,
    )
    cut(1, arrive)
    (am,) = call(reorder_kernel, [(n, n)], [VMEM] * 3, am, order, arrive)
    keep, give, own, strip, *sends = call(
        functools.partial(back_kernel, n_row, margin),
        [(n, n), (n, n), (4, n, n), (4, n, h)] + [(4, margin, n + h)] * n_row,
        [VMEM] * (3 + 2 * n_row) + [SMEM] + [VMEM] * 9,
        obj,
        *halos,
        *corners[1],
        strips[2],
        strips[3],
        offs,
        pr,
        kr,
        ki,
        am,
        w1,
        arrive,
        mats,
        tw_left,
        tw_right,
        mib=40,
    )
    probe_grad = reduce_probe(keep, give)
    got = []
    for i, pairs in enumerate(row_rounds):
        got.append(lax.ppermute(sends[i], "row", pairs))
    total, send_e, send_o = call(
        functools.partial(fold_rows_kernel, n_row, margin),
        [(4, n, n), (2, n, h), (2, n, h)],
        [VMEM] * (2 + n_row),
        own,
        strip,
        *got,
    )
    send_e = lax.ppermute(send_e, "col", col_rounds[0])
    send_o = lax.ppermute(send_o, "col", col_rounds[1])
    (grad,) = call(fold_cols_kernel, [(4, n, n)], [VMEM] * 3, total, send_e, send_o)
    return (grad.reshape(2, 2, tile, tile), probe_grad)


def solution(mesh):
    placed = (
        P(None, None, "row", "col"),
        P(),
        P(),
        P("row", "col", None, None, None),
        P("row", "col", None, None),
    )
    return jax.shard_map(
        whole,
        mesh=mesh,
        in_specs=placed,
        out_specs=(P(None, None, "row", "col"), P()),
        check_vma=False,
    )
```

```python
import functools
import math

import jax
import jax.numpy as jnp
import numpy as np
from jax import lax
from jax.experimental import pallas as pl
from jax.experimental.pallas import tpu as pltpu
from jax.sharding import PartitionSpec as P


EPS_AMP = 0.5
F32 = jnp.float32
BF16 = jnp.bfloat16
VMEM = pl.BlockSpec(memory_space=pltpu.VMEM)
SMEM = pl.BlockSpec(memory_space=pltpu.SMEM)
HBM = pl.BlockSpec(memory_space=pltpu.HBM)


def split_np(table):
    high = table.astype(BF16)
    low = (table - high.astype(np.float64)).astype(BF16)
    return [high, low]


def dft_constants(n):
    h = n // 2
    k = np.arange(h)
    angle = 2.0 * np.pi * ((k[:, None] * k[None, :]) % h) / h
    scale = 1.0 / np.sqrt(n)
    c, s = np.cos(angle) * scale, np.sin(angle) * scale
    d = np.block([[c, s], [-s, c]])
    mats = np.stack(split_np(d) + split_np(d.T))
    w = np.exp(-2j * np.pi * k / n)
    tw_left = np.stack([np.tile(w.real[:, None], (1, h)), np.tile(w.imag[:, None], (1, h))])
    tw_right = np.stack([np.tile(w.real[None], (8, 1)), np.tile(w.imag[None], (8, 1))])
    order = np.zeros((n, n))
    order[2 * k, k] = 1.0
    order[2 * k + 1, h + k] = 1.0
    return (
        mats,
        tw_left.astype(np.float32),
        tw_right.astype(np.float32),
        np.stack([order.T, order]).astype(BF16),
    )


def split(x):
    high = x.astype(BF16)
    return high, (x - high.astype(F32)).astype(BF16)


def dot(a, b):
    return jnp.dot(a, b, preferred_element_type=F32)


def left_dot(mats, which, x):
    high, low = split(x)
    return dot(mats[which], high) + (dot(mats[which], low) + dot(mats[which + 1], high))


def right_dot(x, mats, which):
    high, low = split(x)
    return dot(high, mats[which]) + (dot(low, mats[which]) + dot(high, mats[which + 1]))


def cat(parts, axis):
    return jnp.concatenate(parts, axis=axis)


def product(a, b):
    return (a[0] * b[0] - a[1] * b[1], a[0] * b[1] + a[1] * b[0])


def conj_product(a, b):
    return (a[0] * b[0] + a[1] * b[1], a[0] * b[1] - a[1] * b[0])


class Dft:
    def __init__(self, mats, tw_left, tw_right, n):
        self.mats, self.n, self.h = mats, n, n // 2
        self.wl = [cat([tw_left[i], tw_left[i]], 1) for i in range(2)]
        self.wr = [tw_right[i, 0:1] for i in range(2)]

    def forward(self, x):
        n, h = self.n, self.h
        total = [p[:h] + p[h:] for p in x]
        odd = product([p[:h] - p[h:] for p in x], self.wl)
        y = left_dot(self.mats, 0, cat([cat(total, 0), cat(odd, 0)], 1))
        x = [cat([y[:h, :n], y[:h, n:]], 0), cat([y[h:, :n], y[h:, n:]], 0)]
        total = [p[:, :h] + p[:, h:] for p in x]
        odd = product([p[:, :h] - p[:, h:] for p in x], self.wr)
        y = right_dot(cat([cat(total, 1), cat(odd, 1)], 0), self.mats, 2)
        return [cat([y[:n, :h], y[n:, :h]], 1), cat([y[:n, h:], y[n:, h:]], 1)]

    def inverse(self, x):
        n, h = self.n, self.h
        y = cat([cat([p[:, :h] for p in x], 1), cat([p[:, h:] for p in x], 1)], 0)
        y = right_dot(y, self.mats, 0)
        even = [y[:n, :h], y[:n, h:]]
        odd = conj_product(self.wr, [y[n:, :h], y[n:, h:]])
        x = [cat([e + o, e - o], 1) for e, o in zip(even, odd)]
        y = cat([cat([p[:h] for p in x], 0), cat([p[h:] for p in x], 0)], 1)
        y = left_dot(self.mats, 2, y)
        even = [y[:h, :n], y[h:, :n]]
        odd = conj_product(self.wl, [y[:h, n:], y[h:, n:]])
        return [cat([e + o, e - o], 0) for e, o in zip(even, odd)]


SIN = [(-1.0) ** i / math.factorial(2 * i + 1) for i in range(7)]
COS = [(-1.0) ** i / math.factorial(2 * i) for i in range(7)]


def series(coefficients, z):
    total = coefficients[-1]
    for c in coefficients[-2::-1]:
        total = total * z + c
    return total


def cos_sin(x):
    y = 0.5 * x
    z = y * y
    s, c = y * series(SIN, z), series(COS, z)
    return 1.0 - 2.0 * (s * s), 2.0 * (s * c)


def iota(shape, dim):
    return lax.broadcasted_iota(jnp.int32, shape, dim)


def dyn_roll(x, shift, axis):
    return pltpu.roll(x, shift, axis=axis)


def half_roll(x):
    return pltpu.roll(x, x.shape[-1] // 2, axis=x.ndim - 1)


def pack_cols(re, im):
    h = re.shape[1] // 2
    front = iota((re.shape[0], h), 1) < h // 2
    low = jnp.where(front, re[:, :h], half_roll(im[:, :h]))
    high = jnp.where(front, half_roll(im[:, h:]), re[:, h:])
    return low, high


def copy_all(sources, places, sems):
    copies = [
        pltpu.make_async_copy(a, b, sems.at[i]) for i, (a, b) in enumerate(zip(sources, places))
    ]
    for copy in copies:
        copy.start()
    return copies


def row_start(which, n, margin):
    even = lax.axis_index("row") % 2 == 0
    last = even if which == 0 else jnp.logical_not(even)
    return pl.multiple_of(jnp.where(last, n - margin, 0), 8)


def pack_kernel(margin, obj_hbm, offs_hbm, obj, offs, *refs):
    strips, rows, sems = refs[:4], refs[4:-1], refs[-1]
    n = obj.shape[1]
    copies = copy_all(
        (obj_hbm.at[0:2], obj_hbm.at[2:4], offs_hbm), (obj.at[0:2], obj.at[2:4], offs), sems
    )
    even = lax.axis_index("col") % 2 == 0
    for s in range(2):
        copies[s].wait()
        low, high = pack_cols(obj[2 * s], obj[2 * s + 1])
        strips[2 * s][...] = jnp.where(even, high, low)
        strips[2 * s + 1][...] = jnp.where(even, low, high)
    for which, out in enumerate(rows):
        out[...] = obj[:, pl.ds(row_start(which, n, margin), margin), :]
    copies[2].wait()


def corner_kernel(margin, e, o, after, *outs):
    for which, out in enumerate(outs):
        rows = pl.ds(row_start(which, e.shape[0], margin), margin)
        out[0] = e[rows, :]
        out[1] = o[rows, :]


def reorder(x, order):
    def thirds(y):
        a = y.astype(BF16)
        return (a,) + split(y - a.astype(F32))

    a, b, c = thirds(x)
    a, b, c = thirds(dot(order[0], a) + (dot(order[0], b) + dot(order[0], c)))
    return dot(a, order[1]) + (dot(b, order[1]) + dot(c, order[1]))


def prep_kernel(*refs):
    hbm, (kr, ki), loaded = refs[:7], refs[7:9], refs[9:15]
    phase, sems = refs[15:]
    copies = copy_all(hbm, (phase,) + loaded, sems)
    copies[0].wait()
    copies[1].wait()
    angle = reorder(phase[...], loaded[0])
    kr[...], ki[...] = cos_sin(angle)
    for copy in copies[2:]:
        copy.wait()


def roll_kernel(margin, offs, probe, pr):
    n = probe.shape[1]
    sy = (offs[0, 0] - margin + n) % n
    sx = (offs[0, 1] - margin + n) % n
    for i in range(2):
        pr[i] = dyn_roll(dyn_roll(probe[i], sy, 0), sx, 1)


def reorder_kernel(x, order, after, out):
    out[...] = reorder(x[...], order)


def merge_cols(own, low, high, ox, margin):
    n = own[0].shape[1]
    h = n // 2
    lane = iota((own[0].shape[0], h), 1)
    from_high = lane < ox - margin
    from_low = lane + h >= ox + n - margin
    out = []
    for i in range(2):
        strip_high = high if i == 0 else half_roll(high)
        strip_low = low if i == 0 else half_roll(low)
        out.append(
            cat(
                [
                    jnp.where(from_high, strip_high, own[i][:, :h]),
                    jnp.where(from_low, strip_low, own[i][:, h:]),
                ],
                1,
            )
        )
    return out


def window_of(obj, s, halos, corners, strip_e, strip_o, offs, margin):
    n = obj.shape[1]
    oy, ox = offs[0, 0], offs[0, 1]
    col_even = lax.axis_index("col") % 2 == 0
    row_even = lax.axis_index("row") % 2 == 0
    blocks = []
    sides = [(strip_e, strip_o)] + [(c.at[0], c.at[1]) for c in corners]
    for source, (e, o) in zip([obj] + list(halos), sides):
        e, o = e[...], o[...]
        high, low = jnp.where(col_even, e, o), jnp.where(col_even, o, e)
        blocks.append(merge_cols([source[2 * s], source[2 * s + 1]], low, high, ox, margin))
    row = iota((margin, n), 0)
    take_high = row < oy - margin
    take_low = row + n - margin >= oy + n - margin
    out = []
    for i in range(2):
        main = blocks[0][i]
        if len(blocks) == 3:
            e, o = blocks[1][i], blocks[2][i]
            high, low = jnp.where(row_even, e, o), jnp.where(row_even, o, e)
        else:
            e = blocks[1][i]
            zero = jnp.zeros_like(e)
            high, low = jnp.where(row_even, e, zero), jnp.where(row_even, zero, e)
        out.append(
            cat(
                [
                    jnp.where(take_high, high, main[:margin]),
                    main[margin : n - margin],
                    jnp.where(take_low, low, main[n - margin :]),
                ],
                0,
            )
        )
    return out


def unpack(n_row, refs):
    return refs[0], refs[1 : 1 + n_row], refs[1 + n_row : 1 + 2 * n_row], refs[1 + 2 * n_row :]


def arrive_kernel(n_row, margin, *refs):
    obj, halos, corners, refs = unpack(n_row, refs)
    e1, o1, offs, pr, kr, ki, mats, twl, twr, w1, arrive = refs
    n = obj.shape[1]
    dft = Dft(mats, twl[...], twr[...], n)
    win = window_of(obj, 0, halos, corners, e1, o1, offs, margin)
    w1[0], w1[1] = win
    x = dft.forward(product([pr[0], pr[1]], win))
    x = dft.inverse(product([kr[...], ki[...]], x))
    arrive[0], arrive[1] = x


def divide_kernel(margin, grads, offs, own, strip, *sends):
    for s in range(2):
        split_grad([grads[2 * s], grads[2 * s + 1]], s, offs, margin, own, strip, sends)


def split_grad(grad, s, offs, margin, own, strip, sends):
    n = grad[0].shape[0]
    h = n // 2
    oy, ox = offs[0, 0], offs[0, 1]
    row_even = lax.axis_index("row") % 2 == 0
    lane = iota((1, h), 1)
    to_high, to_low = lane < ox - margin, lane + h >= ox + n - margin
    front = lane < h // 2
    spill = jnp.where(front, to_high.astype(jnp.int32), to_low.astype(jnp.int32)) != 0
    for i in range(2):
        g = grad[i]
        row = iota((n, h), 0)
        high_rows = row < oy - margin
        low_rows = row >= oy + n - margin
        inner = jnp.logical_not(jnp.logical_or(high_rows, low_rows))
        left = jnp.where(to_high, 0.0, g[:, :h])
        right = jnp.where(to_low, 0.0, g[:, h:])
        side = jnp.where(spill, jnp.where(front, g[:, :h], g[:, h:]), 0.0)
        pieces = [left, right, side]
        own[2 * s + i, :, :h] = jnp.where(inner, left, 0.0)
        own[2 * s + i, :, h:] = jnp.where(inner, right, 0.0)
        strip[2 * s + i] = jnp.where(inner, side, 0.0)
        for j, piece in enumerate(pieces):
            top = jnp.where(high_rows[:margin], piece[:margin], 0.0)
            bottom = jnp.where(low_rows[n - margin :], piece[n - margin :], 0.0)
            for which, send in enumerate(sends):
                first = row_even if which == 0 else jnp.logical_not(row_even)
                send[2 * s + i, :, j * h : (j + 1) * h] = jnp.where(first, top, bottom)


def back_kernel(n_row, margin, *refs):
    obj, halos, corners, refs = unpack(n_row, refs)
    e2, o2, offs, pr, kr, ki, am, w1, arrive, mats, twl, twr = refs[:12]
    outs = refs[12:]
    keep, give, grads = outs
    n = obj.shape[1]
    dft = Dft(mats, twl[...], twr[...], n)
    win = window_of(obj, 1, halos, corners, e2, o2, offs, margin)
    arr = [arrive[0], arrive[1]]
    far = dft.forward(product(arr, win))
    modulus = jnp.sqrt(far[0] * far[0] + far[1] * far[1] + EPS_AMP)
    factor = 2.0 * (1.0 - am[...] / modulus)
    back_far = dft.inverse([factor * far[0], factor * far[1]])
    grads[2], grads[3] = conj_product(arr, back_far)
    x = dft.forward(conj_product(win, back_far))
    x = dft.inverse(conj_product([kr[...], ki[...]], x))
    grads[0], grads[1] = conj_product([pr[0], pr[1]], x)
    grad = conj_product([w1[0], w1[1]], x)
    sy = (margin - offs[0, 0] + n) % n
    sx = (margin - offs[0, 1] + n) % n
    grad = [dyn_roll(dyn_roll(g, sy, 0), sx, 1) for g in grad]
    even = lax.axis_index("row") % 2 == 0
    keep[...] = jnp.where(even, grad[0], grad[1])
    give[...] = jnp.where(even, grad[1], grad[0])


def fold_rows_kernel(n_row, margin, own, strip, *refs):
    got, (total, send_e, send_o) = refs[:n_row], refs[n_row:]
    row_even = lax.axis_index("row") % 2 == 0
    col_even = lax.axis_index("col") % 2 == 0
    n = own.shape[1]
    h = n // 2
    front = iota((n, h), 1) < h // 2
    for s in range(2):
        strips = []
        for i in range(2 * s, 2 * s + 2):
            total[i] = own[i]
            r = got[0][i]
            q = got[1][i] if n_row == 2 else jnp.zeros_like(r)
            top, bottom = jnp.where(row_even, q, r), jnp.where(row_even, r, q)
            total[i, :margin] += top[:, :n]
            total[i, n - margin :] += bottom[:, :n]
            st = strip[i]
            strips.append(
                cat(
                    [
                        st[:margin] + top[:, n:],
                        st[margin : n - margin],
                        st[n - margin :] + bottom[:, n:],
                    ],
                    0,
                )
            )
        moved = half_roll(strips[1])
        to_high = jnp.where(front, strips[0], moved)
        to_low = jnp.where(front, moved, strips[0])
        send_e[s] = jnp.where(col_even, to_high, to_low)
        send_o[s] = jnp.where(col_even, to_low, to_high)


def fold_cols_kernel(total, e, o, out):
    col_even = lax.axis_index("col") % 2 == 0
    n = total.shape[1]
    h = n // 2
    front = iota((n, h), 1) < h // 2
    for s in range(2):
        high = jnp.where(col_even, e[s], o[s])
        low = jnp.where(col_even, o[s], e[s])
        for i in range(2):
            a = low if i == 0 else half_roll(low)
            b = high if i == 0 else half_roll(high)
            at = 2 * s + i
            out[at, :, :h] = total[at, :, :h] + jnp.where(front, a, 0.0)
            out[at, :, h:] = total[at, :, h:] + jnp.where(front, 0.0, b)


def in_hbm(x):
    return pltpu.with_memory_space_constraint(x, pltpu.HBM)


def call(kernel, shapes, in_specs, *args, scratch=(), mib=16):
    shapes = [s if isinstance(s, jax.ShapeDtypeStruct) else jax.ShapeDtypeStruct(s, F32) for s in shapes]
    return pl.pallas_call(
        kernel,
        out_shape=shapes,
        in_specs=in_specs,
        out_specs=[VMEM if s.dtype != jnp.int32 else SMEM for s in shapes],
        scratch_shapes=list(scratch),
        compiler_params=pltpu.CompilerParams(vmem_limit_bytes=mib << 20),
    )(*args)


def edges(axis):
    count = lax.axis_size(axis)
    rounds = []
    for first in (0, 1):
        pairs = [(i, i + 1) for i in range(first, count - 1, 2)]
        pairs += [(b, a) for a, b in pairs]
        if pairs:
            rounds.append(pairs)
    return rounds


def swap(value, axis, distance):
    count = lax.axis_size(axis)
    return lax.ppermute(value, axis, [(i, i ^ distance) for i in range(count)])


def groups():
    cols = [("col", 1 << b) for b in range(lax.axis_size("col").bit_length() - 1)]
    rows = [("row", 1 << b) for b in range(1, lax.axis_size("row").bit_length() - 1)]
    first, rest = cols[:2], cols[2:]
    pairs = [first]
    for bits in (rest, rows):
        pairs += [bits[i : i + 2] for i in range(0, len(bits), 2)]
    out = []
    for pair in pairs:
        axis, masks = pair[0][0], [m for _, m in pair]
        out.append((axis, [0] + masks + ([sum(masks)] if len(masks) == 2 else [])))
    return out


def pair_sum(parts):
    while len(parts) > 1:
        parts = [parts[i] + parts[i + 1] for i in range(0, len(parts), 2)]
    return parts[0]


def share_kernel(quad, stride, keep, other, *parts):
    place = lax.axis_index("col") // stride % quad
    chunk = keep.shape[0] // quad
    for j, part in enumerate(parts):
        rows = pl.ds(pl.multiple_of((place ^ j) * chunk, 8), chunk)
        part[...] = keep[rows, :] + other[rows, :]


def sum_kernel(*refs):
    refs[-1][...] = pair_sum([r[...] for r in refs[:-1]])


def join_kernel(stride, *refs):
    parts, full = refs[:-1], refs[-1]
    quad, chunk = len(parts), parts[0].shape[0]
    place = lax.axis_index("col") // stride % quad
    for j, part in enumerate(parts):
        full[pl.ds(pl.multiple_of((place ^ j) * chunk, 8), chunk), :] = part[...]


def both_kernel(full, other, out):
    even = lax.axis_index("row") % 2 == 0
    out[0] = jnp.where(even, full[...], other[...])
    out[1] = jnp.where(even, other[...], full[...])


def reduce_probe(keep, give):
    n = keep.shape[0]
    (_, offsets), *rest = groups()
    quad, stride = len(offsets), offsets[1]
    chunk = n // quad
    other = swap(give, "row", 1)
    parts = call(
        functools.partial(share_kernel, quad, stride),
        [(chunk, n)] * quad,
        [VMEM] * 2,
        keep,
        other,
    )
    sums = [parts[0]]
    for j in range(1, quad):
        sums.append(swap(parts[j], "col", offsets[j]))
    (total,) = call(sum_kernel, [(chunk, n)], [VMEM] * quad, *sums)
    for axis, masks in rest:
        sums = [total]
        for mask in masks[1:]:
            sums.append(swap(total, axis, mask))
        (total,) = call(sum_kernel, [(chunk, n)], [VMEM] * len(sums), *sums)
    parts = [total]
    for j in range(1, quad):
        parts.append(swap(total, "col", offsets[j]))
    (full,) = call(
        functools.partial(join_kernel, stride), [(n, n)], [VMEM] * quad, *parts
    )
    other = swap(full, "row", 1)
    (grad,) = call(both_kernel, [(2, n, n)], [VMEM] * 2, full, other)
    return grad


def whole(object_field, probe, phase, amplitudes, offsets):
    tile = object_field.shape[2]
    n = probe.shape[1]
    h = n // 2
    margin = n // 4
    tables = [jnp.asarray(t) for t in dft_constants(n)]
    mats, tw_left, tw_right, order = tables

    row_rounds, col_rounds = edges("row"), edges("col")
    n_row = len(row_rounds)
    obj, offs, *packed = call(
        functools.partial(pack_kernel, margin),
        [(4, n, n), jax.ShapeDtypeStruct((1, 2), jnp.int32)]
        + [(n, h)] * 4
        + [(4, margin, n)] * n_row,
        [HBM, HBM],
        in_hbm(object_field.reshape(4, tile, tile)),
        in_hbm(offsets.reshape(1, 2)),
        scratch=[pltpu.SemaphoreType.DMA((3,))],
    )
    strips, halos, corners = [], [], [[], []]
    for i in range(4):
        strips.append(lax.ppermute(packed[i], "col", col_rounds[i % 2]))
    for i, pairs in enumerate(row_rounds):
        halos.append(lax.ppermute(packed[4 + i], "row", pairs))

    def cut(s, after):
        parts = call(
            functools.partial(corner_kernel, margin),
            [(2, margin, h)] * n_row,
            [VMEM] * 3,
            *strips[2 * s : 2 * s + 2],
            after,
        )
        for i, pairs in enumerate(row_rounds):
            corners[s].append(lax.ppermute(parts[i], "row", pairs))

    loads = (phase, order, mats, tw_left, tw_right, probe, amplitudes.reshape(n, n))
    kr, ki, order, mats, tw_left, tw_right, pr, am = call(
        prep_kernel,
        [(n, n), (n, n)] + [jax.ShapeDtypeStruct(x.shape, x.dtype) for x in loads[1:]],
        [HBM] * len(loads),
        *[in_hbm(x) for x in loads],
        scratch=[pltpu.VMEM((n, n), F32), pltpu.SemaphoreType.DMA((len(loads),))],
    )
    cut(0, kr)
    (pr,) = call(functools.partial(roll_kernel, margin), [(2, n, n)], [SMEM, VMEM], offs, pr)
    w1, arrive = call(
        functools.partial(arrive_kernel, n_row, margin),
        [(2, n, n), (2, n, n)],
        [VMEM] * (3 + 2 * n_row) + [SMEM] + [VMEM] * 6,
        obj,
        *halos,
        *corners[0],
        strips[0],
        strips[1],
        offs,
        pr,
        kr,
        ki,
        mats,
        tw_left,
        tw_right,
    )
    cut(1, arrive)
    (am,) = call(reorder_kernel, [(n, n)], [VMEM] * 3, am, order, arrive)
    keep, give, grads = call(
        functools.partial(back_kernel, n_row, margin),
        [(n, n), (n, n), (4, n, n)],
        [VMEM] * (3 + 2 * n_row) + [SMEM] + [VMEM] * 9,
        obj,
        *halos,
        *corners[1],
        strips[2],
        strips[3],
        offs,
        pr,
        kr,
        ki,
        am,
        w1,
        arrive,
        mats,
        tw_left,
        tw_right,
        mib=40,
    )
    probe_grad = reduce_probe(keep, give)
    own, strip, *sends = call(
        functools.partial(divide_kernel, margin),
        [(4, n, n), (4, n, h)] + [(4, margin, n + h)] * n_row,
        [VMEM, SMEM],
        grads,
        offs,
    )
    got = []
    for i, pairs in enumerate(row_rounds):
        got.append(lax.ppermute(sends[i], "row", pairs))
    total, send_e, send_o = call(
        functools.partial(fold_rows_kernel, n_row, margin),
        [(4, n, n), (2, n, h), (2, n, h)],
        [VMEM] * (2 + n_row),
        own,
        strip,
        *got,
    )
    send_e = lax.ppermute(send_e, "col", col_rounds[0])
    send_o = lax.ppermute(send_o, "col", col_rounds[1])
    (grad,) = call(fold_cols_kernel, [(4, n, n)], [VMEM] * 3, total, send_e, send_o)
    return (grad.reshape(2, 2, tile, tile), probe_grad)


def solution(mesh):
    placed = (
        P(None, None, "row", "col"),
        P(),
        P(),
        P("row", "col", None, None, None),
        P("row", "col", None, None),
    )
    return jax.shard_map(
        whole,
        mesh=mesh,
        in_specs=placed,
        out_specs=(P(None, None, "row", "col"), P()),
        check_vma=False,
    )
```

```python
import functools
import math

import jax
import jax.numpy as jnp
import numpy as np
from jax import lax
from jax.experimental import pallas as pl
from jax.experimental.pallas import tpu as pltpu
from jax.sharding import PartitionSpec as P


EPS_AMP = 0.5
F32 = jnp.float32
BF16 = jnp.bfloat16
VMEM = pl.BlockSpec(memory_space=pltpu.VMEM)
SMEM = pl.BlockSpec(memory_space=pltpu.SMEM)
HBM = pl.BlockSpec(memory_space=pltpu.HBM)


def split_np(table):
    high = table.astype(BF16)
    low = (table - high.astype(np.float64)).astype(BF16)
    return [high, low]


def dft_constants(n):
    h = n // 2
    k = np.arange(h)
    angle = 2.0 * np.pi * ((k[:, None] * k[None, :]) % h) / h
    scale = 1.0 / np.sqrt(n)
    c, s = np.cos(angle) * scale, np.sin(angle) * scale
    d = np.block([[c, s], [-s, c]])
    mats = np.stack(split_np(d) + split_np(d.T))
    w = np.exp(-2j * np.pi * k / n)
    tw_left = np.stack([np.tile(w.real[:, None], (1, h)), np.tile(w.imag[:, None], (1, h))])
    tw_right = np.stack([np.tile(w.real[None], (8, 1)), np.tile(w.imag[None], (8, 1))])
    order = np.zeros((n, n))
    order[2 * k, k] = 1.0
    order[2 * k + 1, h + k] = 1.0
    return (
        mats,
        tw_left.astype(np.float32),
        tw_right.astype(np.float32),
        np.stack([order.T, order]).astype(BF16),
    )


def split(x):
    high = x.astype(BF16)
    return high, (x - high.astype(F32)).astype(BF16)


def dot(a, b):
    return jnp.dot(a, b, preferred_element_type=F32)


def left_dot(mats, which, x):
    high, low = split(x)
    return dot(mats[which], high) + (dot(mats[which], low) + dot(mats[which + 1], high))


def right_dot(x, mats, which):
    high, low = split(x)
    return dot(high, mats[which]) + (dot(low, mats[which]) + dot(high, mats[which + 1]))


def cat(parts, axis):
    return jnp.concatenate(parts, axis=axis)


def product(a, b):
    return (a[0] * b[0] - a[1] * b[1], a[0] * b[1] + a[1] * b[0])


def conj_product(a, b):
    return (a[0] * b[0] + a[1] * b[1], a[0] * b[1] - a[1] * b[0])


class Dft:
    def __init__(self, mats, tw_left, tw_right, n):
        self.mats, self.n, self.h = mats, n, n // 2
        self.tw_left, self.tw_right = tw_left, tw_right

    def wl(self, width):
        parts = width // self.tw_left.shape[2]
        return [cat([self.tw_left[i]] * parts, 1) for i in range(2)]

    def wr(self):
        return [self.tw_right[i, 0:1] for i in range(2)]

    def left(self, x):
        h, w = self.h, x[0].shape[1]
        total = [p[:h] + p[h:] for p in x]
        odd = product([p[:h] - p[h:] for p in x], self.wl(w))
        u = left_dot(self.mats, 0, cat(total, 0))
        v = left_dot(self.mats, 0, cat(odd, 0))
        return [cat([u[:h], v[:h]], 0), cat([u[h:], v[h:]], 0)]

    def right(self, x):
        h, m = self.h, x[0].shape[0]
        total = [p[:, :h] + p[:, h:] for p in x]
        odd = product([p[:, :h] - p[:, h:] for p in x], self.wr())
        u = right_dot(cat(total, 1), self.mats, 2)
        v = right_dot(cat(odd, 1), self.mats, 2)
        return [cat([u[:, :h], v[:, :h]], 1), cat([u[:, h:], v[:, h:]], 1)]

    def right_inverse(self, x):
        h, m = self.h, x[0].shape[0]
        u = right_dot(cat([p[:, :h] for p in x], 1), self.mats, 0)
        v = right_dot(cat([p[:, h:] for p in x], 1), self.mats, 0)
        even = [u[:, :h], u[:, h:]]
        odd = conj_product(self.wr(), [v[:, :h], v[:, h:]])
        return [cat([e + o, e - o], 1) for e, o in zip(even, odd)]

    def left_inverse(self, x):
        h, w = self.h, x[0].shape[1]
        u = left_dot(self.mats, 2, cat([p[:h] for p in x], 0))
        v = left_dot(self.mats, 2, cat([p[h:] for p in x], 0))
        even = [u[:h], u[h:]]
        odd = conj_product(self.wl(w), [v[:h], v[h:]])
        return [cat([e + o, e - o], 0) for e, o in zip(even, odd)]


SIN = [(-1.0) ** i / math.factorial(2 * i + 1) for i in range(7)]
COS = [(-1.0) ** i / math.factorial(2 * i) for i in range(7)]


def series(coefficients, z):
    total = coefficients[-1]
    for c in coefficients[-2::-1]:
        total = total * z + c
    return total


def cos_sin(x):
    y = 0.5 * x
    z = y * y
    s, c = y * series(SIN, z), series(COS, z)
    return 1.0 - 2.0 * (s * s), 2.0 * (s * c)


def iota(shape, dim):
    return lax.broadcasted_iota(jnp.int32, shape, dim)


def dyn_roll(x, shift, axis):
    return pltpu.roll(x, shift, axis=axis)


def half_roll(x):
    return pltpu.roll(x, x.shape[-1] // 2, axis=x.ndim - 1)


def pack_cols(re, im):
    h = re.shape[1] // 2
    front = iota((re.shape[0], h), 1) < h // 2
    low = jnp.where(front, re[:, :h], half_roll(im[:, :h]))
    high = jnp.where(front, half_roll(im[:, h:]), re[:, h:])
    return low, high


def copy_all(sources, places, sems):
    copies = [
        pltpu.make_async_copy(a, b, sems.at[i]) for i, (a, b) in enumerate(zip(sources, places))
    ]
    for copy in copies:
        copy.start()
    return copies


def row_start(which, n, margin):
    even = lax.axis_index("row") % 2 == 0
    last = even if which == 0 else jnp.logical_not(even)
    return pl.multiple_of(jnp.where(last, n - margin, 0), 8)


def pack_kernel(margin, obj_hbm, offs_hbm, obj, offs, limits, *refs):
    strips, rows, sems = refs[:4], refs[4:-1], refs[-1]
    n = obj.shape[1]
    copies = copy_all(
        (obj_hbm.at[0:2], obj_hbm.at[2:4], offs_hbm), (obj.at[0:2], obj.at[2:4], offs), sems
    )
    even = lax.axis_index("col") % 2 == 0
    for s in range(2):
        copies[s].wait()
        low, high = pack_cols(obj[2 * s], obj[2 * s + 1])
        strips[2 * s][...] = jnp.where(even, high, low)
        strips[2 * s + 1][...] = jnp.where(even, low, high)
    for which, out in enumerate(rows):
        out[...] = obj[:, pl.ds(row_start(which, n, margin), margin), :]
    copies[2].wait()
    for i in range(2):
        limits[i] = jnp.full(limits.shape[1:], offs[0, i] - margin, jnp.int32)


def corner_kernel(margin, e, o, after, *outs):
    for which, out in enumerate(outs):
        rows = pl.ds(row_start(which, e.shape[0], margin), margin)
        out[0] = e[rows, :]
        out[1] = o[rows, :]


def reorder(x, order):
    def thirds(y):
        a = y.astype(BF16)
        return (a,) + split(y - a.astype(F32))

    a, b, c = thirds(x)
    a, b, c = thirds(dot(order[0], a) + (dot(order[0], b) + dot(order[0], c)))
    return dot(a, order[1]) + (dot(b, order[1]) + dot(c, order[1]))


def prep_kernel(*refs):
    hbm, (kr, ki, am), loaded = refs[:7], refs[7:10], refs[10:14]
    phase, order, amps, sems = refs[14:]
    copies = copy_all(hbm, (phase, order, amps) + loaded, sems)
    copies[0].wait()
    copies[1].wait()
    angle = reorder(phase[...], order)
    kr[...], ki[...] = cos_sin(angle)
    copies[2].wait()
    am[...] = reorder(amps[...], order)
    for copy in copies[3:]:
        copy.wait()


def roll_kernel(margin, offs, probe, pr):
    n = probe.shape[1]
    sy = (offs[0, 0] - margin + n) % n
    sx = (offs[0, 1] - margin + n) % n
    for i in range(2):
        pr[i] = dyn_roll(dyn_roll(probe[i], sy, 0), sx, 1)


def merge_cols(own, e, o, limits):
    n = own[0].shape[1]
    h = n // 2
    even = lax.axis_index("col") % 2 == 0
    high, low = jnp.where(even, e, o), jnp.where(even, o, e)
    lane = iota((1, h), 1)
    from_high = lane < limits[1, 0:1]
    from_low = lane >= limits[1, 0:1] + h
    out = []
    for i in range(2):
        strip_high = high if i == 0 else half_roll(high)
        strip_low = low if i == 0 else half_roll(low)
        out.append(
            cat(
                [
                    jnp.where(from_high, strip_high, own[i][:, :h]),
                    jnp.where(from_low, strip_low, own[i][:, h:]),
                ],
                1,
            )
        )
    return out


def merge_kernel(s, obj, e, o, limits, out):
    own = [obj[2 * s], obj[2 * s + 1]]
    out[0], out[1] = merge_cols(own, e[...], o[...], limits)


def window_of(main, s, halos, corners, limits, margin):
    n = main.shape[1]
    row_even = lax.axis_index("row") % 2 == 0
    blocks = []
    for halo, corner in zip(halos, corners):
        own = [halo[2 * s], halo[2 * s + 1]]
        blocks.append(merge_cols(own, corner[0], corner[1], limits))
    row = iota((margin, n), 0)
    limit = cat([limits[0, 0:1]] * 2, 1)
    take_high = row < limit
    take_low = row >= limit + margin
    out = []
    for i in range(2):
        e = blocks[0][i]
        o = blocks[1][i] if len(blocks) == 2 else jnp.zeros_like(e)
        high, low = jnp.where(row_even, e, o), jnp.where(row_even, o, e)
        out.append(
            cat(
                [
                    jnp.where(take_high, high, main[i, :margin]),
                    main[i, margin : n - margin],
                    jnp.where(take_low, low, main[i, n - margin :]),
                ],
                0,
            )
        )
    return out


def unpack(n_row, refs):
    return refs[0], refs[1 : 1 + n_row], refs[1 + n_row : 1 + 2 * n_row], refs[1 + 2 * n_row :]


def through(dft, x, re, im):
    return dft.right_inverse(product([re, im], dft.right(x)))


def arrive_kernel(n_row, margin, *refs):
    main, halos, corners, refs = unpack(n_row, refs)
    limits, pr, kr, ki, mats, twl, twr, w1, arrive = refs
    n = main.shape[1]
    dft = Dft(mats, twl[...], twr[...], n)
    win = window_of(main, 0, halos, corners, limits, margin)
    w1[0], w1[1] = win
    x = dft.left(product([pr[0], pr[1]], win))
    x = through(dft, x, kr[...], ki[...])
    arrive[0], arrive[1] = dft.left_inverse(x)


def back_kernel(n_row, margin, *refs):
    main, halos, corners, refs = unpack(n_row, refs)
    limits, offs_hbm, pr, kr, ki, am, w1, arrive, mats, twl, twr = refs[:11]
    keep, give, grads, offs, sem = refs[11:]
    scalars = pltpu.make_async_copy(offs_hbm, offs, sem)
    scalars.start()
    n = main.shape[1]
    dft = Dft(mats, twl[...], twr[...], n)
    win = window_of(main, 1, halos, corners, limits, margin)
    x = dft.left(product([arrive[0], arrive[1]], win))
    far = dft.right(x)
    modulus = jnp.sqrt(far[0] * far[0] + far[1] * far[1] + EPS_AMP)
    factor = 2.0 * (1.0 - am[...] / modulus)
    x = dft.right_inverse([factor * far[0], factor * far[1]])
    back_far = dft.left_inverse(x)
    grads[2], grads[3] = conj_product([arrive[0], arrive[1]], back_far)
    x = dft.left(conj_product(win, back_far))
    x = through(dft, x, kr[...], -ki[...])
    x = dft.left_inverse(x)
    grads[0], grads[1] = conj_product([pr[0], pr[1]], x)
    grad = conj_product([w1[0], w1[1]], x)
    scalars.wait()
    sy = (margin - offs[0, 0] + n) % n
    sx = (margin - offs[0, 1] + n) % n
    grad = [dyn_roll(dyn_roll(g, sy, 0), sx, 1) for g in grad]
    even = lax.axis_index("row") % 2 == 0
    keep[...] = jnp.where(even, grad[0], grad[1])
    give[...] = jnp.where(even, grad[1], grad[0])


def divide_kernel(margin, grads, limits, own, strip, *sends):
    for s in range(2):
        split_grad([grads[2 * s], grads[2 * s + 1]], s, limits, margin, own, strip, sends)


def split_grad(grad, s, limits, margin, own, strip, sends):
    n = grad[0].shape[0]
    h = n // 2
    row_even = lax.axis_index("row") % 2 == 0
    lane = iota((1, h), 1)
    to_high, to_low = lane < limits[1, 0:1], lane >= limits[1, 0:1] + h
    front = lane < h // 2
    spill = jnp.where(front, to_high.astype(jnp.int32), to_low.astype(jnp.int32)) != 0
    for i in range(2):
        g = grad[i]
        row = iota((n, h), 0)
        high_rows = row < limits[0, 0:1]
        low_rows = row >= limits[0, 0:1] + n
        inner = jnp.logical_not(jnp.logical_or(high_rows, low_rows))
        left = jnp.where(to_high, 0.0, g[:, :h])
        right = jnp.where(to_low, 0.0, g[:, h:])
        side = jnp.where(spill, jnp.where(front, g[:, :h], g[:, h:]), 0.0)
        pieces = [left, right, side]
        own[2 * s + i, :, :h] = jnp.where(inner, left, 0.0)
        own[2 * s + i, :, h:] = jnp.where(inner, right, 0.0)
        strip[2 * s + i] = jnp.where(inner, side, 0.0)
        for j, piece in enumerate(pieces):
            top = jnp.where(high_rows[:margin], piece[:margin], 0.0)
            bottom = jnp.where(low_rows[n - margin :], piece[n - margin :], 0.0)
            for which, send in enumerate(sends):
                first = row_even if which == 0 else jnp.logical_not(row_even)
                send[2 * s + i, :, j * h : (j + 1) * h] = jnp.where(first, top, bottom)


def fold_rows_kernel(n_row, margin, own, strip, *refs):
    got, (total, send_e, send_o) = refs[:n_row], refs[n_row:]
    row_even = lax.axis_index("row") % 2 == 0
    col_even = lax.axis_index("col") % 2 == 0
    n = own.shape[1]
    h = n // 2
    front = iota((n, h), 1) < h // 2
    for s in range(2):
        strips = []
        for i in range(2 * s, 2 * s + 2):
            total[i] = own[i]
            r = got[0][i]
            q = got[1][i] if n_row == 2 else jnp.zeros_like(r)
            top, bottom = jnp.where(row_even, q, r), jnp.where(row_even, r, q)
            total[i, :margin] += top[:, :n]
            total[i, n - margin :] += bottom[:, :n]
            st = strip[i]
            strips.append(
                cat(
                    [
                        st[:margin] + top[:, n:],
                        st[margin : n - margin],
                        st[n - margin :] + bottom[:, n:],
                    ],
                    0,
                )
            )
        moved = half_roll(strips[1])
        to_high = jnp.where(front, strips[0], moved)
        to_low = jnp.where(front, moved, strips[0])
        send_e[s] = jnp.where(col_even, to_high, to_low)
        send_o[s] = jnp.where(col_even, to_low, to_high)


def fold_cols_kernel(total, e, o, out):
    col_even = lax.axis_index("col") % 2 == 0
    n = total.shape[1]
    h = n // 2
    front = iota((n, h), 1) < h // 2
    for s in range(2):
        high = jnp.where(col_even, e[s], o[s])
        low = jnp.where(col_even, o[s], e[s])
        for i in range(2):
            a = low if i == 0 else half_roll(low)
            b = high if i == 0 else half_roll(high)
            at = 2 * s + i
            out[at, :, :h] = total[at, :, :h] + jnp.where(front, a, 0.0)
            out[at, :, h:] = total[at, :, h:] + jnp.where(front, 0.0, b)


def in_hbm(x):
    return pltpu.with_memory_space_constraint(x, pltpu.HBM)


def call(kernel, shapes, in_specs, *args, scratch=(), mib=16):
    shapes = [s if isinstance(s, jax.ShapeDtypeStruct) else jax.ShapeDtypeStruct(s, F32) for s in shapes]
    return pl.pallas_call(
        kernel,
        out_shape=shapes,
        in_specs=in_specs,
        out_specs=[SMEM if s.shape == (1, 2) else VMEM for s in shapes],
        scratch_shapes=list(scratch),
        compiler_params=pltpu.CompilerParams(vmem_limit_bytes=mib << 20),
    )(*args)


def edges(axis):
    count = lax.axis_size(axis)
    rounds = []
    for first in (0, 1):
        pairs = [(i, i + 1) for i in range(first, count - 1, 2)]
        pairs += [(b, a) for a, b in pairs]
        if pairs:
            rounds.append(pairs)
    return rounds


def swap(value, axis, distance):
    count = lax.axis_size(axis)
    return lax.ppermute(value, axis, [(i, i ^ distance) for i in range(count)])


def groups():
    cols = [("col", 1 << b) for b in range(lax.axis_size("col").bit_length() - 1)]
    rows = [("row", 1 << b) for b in range(1, lax.axis_size("row").bit_length() - 1)]
    first, rest = cols[:2], cols[2:]
    pairs = [first]
    for bits in (rest, rows):
        pairs += [bits[i : i + 2] for i in range(0, len(bits), 2)]
    out = []
    for pair in pairs:
        axis, masks = pair[0][0], [m for _, m in pair]
        out.append((axis, [0] + masks + ([sum(masks)] if len(masks) == 2 else [])))
    return out


def pair_sum(parts):
    while len(parts) > 1:
        parts = [parts[i] + parts[i + 1] for i in range(0, len(parts), 2)]
    return parts[0]


def share_kernel(quad, stride, keep, other, *parts):
    place = lax.axis_index("col") // stride % quad
    chunk = keep.shape[0] // quad
    for j, part in enumerate(parts):
        rows = pl.ds(pl.multiple_of((place ^ j) * chunk, 8), chunk)
        part[...] = keep[rows, :] + other[rows, :]


def sum_kernel(*refs):
    refs[-1][...] = pair_sum([r[...] for r in refs[:-1]])


def join_kernel(stride, *refs):
    parts, full = refs[:-1], refs[-1]
    quad, chunk = len(parts), parts[0].shape[0]
    place = lax.axis_index("col") // stride % quad
    for j, part in enumerate(parts):
        full[pl.ds(pl.multiple_of((place ^ j) * chunk, 8), chunk), :] = part[...]


def both_kernel(full, other, out):
    even = lax.axis_index("row") % 2 == 0
    out[0] = jnp.where(even, full[...], other[...])
    out[1] = jnp.where(even, other[...], full[...])


def reduce_probe(keep, give):
    n = keep.shape[0]
    (_, offsets), *rest = groups()
    quad, stride = len(offsets), offsets[1]
    chunk = n // quad
    other = swap(give, "row", 1)
    parts = call(
        functools.partial(share_kernel, quad, stride),
        [(chunk, n)] * quad,
        [VMEM] * 2,
        keep,
        other,
    )
    sums = [parts[0]]
    for j in range(1, quad):
        sums.append(swap(parts[j], "col", offsets[j]))
    (total,) = call(sum_kernel, [(chunk, n)], [VMEM] * quad, *sums)
    for axis, masks in rest:
        sums = [total]
        for mask in masks[1:]:
            sums.append(swap(total, axis, mask))
        (total,) = call(sum_kernel, [(chunk, n)], [VMEM] * len(sums), *sums)
    parts = [total]
    for j in range(1, quad):
        parts.append(swap(total, "col", offsets[j]))
    (full,) = call(
        functools.partial(join_kernel, stride), [(n, n)], [VMEM] * quad, *parts
    )
    other = swap(full, "row", 1)
    (grad,) = call(both_kernel, [(2, n, n)], [VMEM] * 2, full, other)
    return grad


def whole(object_field, probe, phase, amplitudes, offsets):
    tile = object_field.shape[2]
    n = probe.shape[1]
    h = n // 2
    margin = n // 4
    tables = [jnp.asarray(t) for t in dft_constants(n)]
    mats, tw_left, tw_right, order = tables

    row_rounds, col_rounds = edges("row"), edges("col")
    n_row = len(row_rounds)
    obj, offs, limits, *packed = call(
        functools.partial(pack_kernel, margin),
        [(4, n, n), jax.ShapeDtypeStruct((1, 2), jnp.int32)]
        + [jax.ShapeDtypeStruct((2, 8, h), jnp.int32)]
        + [(n, h)] * 4
        + [(4, margin, n)] * n_row,
        [HBM, HBM],
        in_hbm(object_field.reshape(4, tile, tile)),
        in_hbm(offsets.reshape(1, 2)),
        scratch=[pltpu.SemaphoreType.DMA((3,))],
    )
    strips, halos, corners = [], [], [[], []]
    for i in range(4):
        strips.append(lax.ppermute(packed[i], "col", col_rounds[i % 2]))
    for i, pairs in enumerate(row_rounds):
        halos.append(lax.ppermute(packed[4 + i], "row", pairs))

    def cut(s, after):
        parts = call(
            functools.partial(corner_kernel, margin),
            [(2, margin, h)] * n_row,
            [VMEM] * 3,
            *strips[2 * s : 2 * s + 2],
            after,
        )
        for i, pairs in enumerate(row_rounds):
            corners[s].append(lax.ppermute(parts[i], "row", pairs))

    def merge(s):
        (main,) = call(
            functools.partial(merge_kernel, s),
            [(2, n, n)],
            [VMEM] * 4,
            obj,
            *strips[2 * s : 2 * s + 2],
            limits,
        )
        return main

    loads = (phase, order, amplitudes.reshape(n, n), mats, tw_left, tw_right, probe)
    kr, ki, am, mats, tw_left, tw_right, pr = call(
        prep_kernel,
        [(n, n)] * 3 + [jax.ShapeDtypeStruct(x.shape, x.dtype) for x in loads[3:]],
        [HBM] * len(loads),
        *[in_hbm(x) for x in loads],
        scratch=[
            pltpu.VMEM((n, n), F32),
            pltpu.VMEM((2, n, n), BF16),
            pltpu.VMEM((n, n), F32),
            pltpu.SemaphoreType.DMA((len(loads),)),
        ],
    )
    cut(0, kr)
    (pr,) = call(functools.partial(roll_kernel, margin), [(2, n, n)], [SMEM, VMEM], offs, pr)
    main = merge(0)
    w1, arrive = call(
        functools.partial(arrive_kernel, n_row, margin),
        [(2, n, n), (2, n, n)],
        [VMEM] * (8 + 2 * n_row),
        main,
        *halos,
        *corners[0],
        limits,
        pr,
        kr,
        ki,
        mats,
        tw_left,
        tw_right,
    )
    cut(1, arrive)
    main = merge(1)
    keep, give, grads = call(
        functools.partial(back_kernel, n_row, margin),
        [(n, n), (n, n), (4, n, n)],
        [VMEM] * (2 + 2 * n_row) + [HBM] + [VMEM] * 9,
        main,
        *halos,
        *corners[1],
        limits,
        in_hbm(offsets.reshape(1, 2)),
        pr,
        kr,
        ki,
        am,
        w1,
        arrive,
        mats,
        tw_left,
        tw_right,
        scratch=[pltpu.SMEM((1, 2), jnp.int32), pltpu.SemaphoreType.DMA(())],
        mib=40,
    )
    probe_grad = reduce_probe(keep, give)
    own, strip, *sends = call(
        functools.partial(divide_kernel, margin),
        [(4, n, n), (4, n, h)] + [(4, margin, n + h)] * n_row,
        [VMEM, VMEM],
        grads,
        limits,
    )
    got = []
    for i, pairs in enumerate(row_rounds):
        got.append(lax.ppermute(sends[i], "row", pairs))
    total, send_e, send_o = call(
        functools.partial(fold_rows_kernel, n_row, margin),
        [(4, n, n), (2, n, h), (2, n, h)],
        [VMEM] * (2 + n_row),
        own,
        strip,
        *got,
    )
    send_e = lax.ppermute(send_e, "col", col_rounds[0])
    send_o = lax.ppermute(send_o, "col", col_rounds[1])
    (grad,) = call(fold_cols_kernel, [(4, n, n)], [VMEM] * 3, total, send_e, send_o)
    return (grad.reshape(2, 2, tile, tile), probe_grad)


def solution(mesh):
    placed = (
        P(None, None, "row", "col"),
        P(),
        P(),
        P("row", "col", None, None, None),
        P("row", "col", None, None),
    )
    return jax.shard_map(
        whole,
        mesh=mesh,
        in_specs=placed,
        out_specs=(P(None, None, "row", "col"), P()),
        check_vma=False,
    )
```

```python
import functools
import math

import jax
import jax.numpy as jnp
import numpy as np
from jax import lax
from jax.experimental import pallas as pl
from jax.experimental.pallas import tpu as pltpu
from jax.sharding import PartitionSpec as P


EPS_AMP = 0.5
F32 = jnp.float32
BF16 = jnp.bfloat16
VMEM = pl.BlockSpec(memory_space=pltpu.VMEM)
SMEM = pl.BlockSpec(memory_space=pltpu.SMEM)
HBM = pl.BlockSpec(memory_space=pltpu.HBM)


def split_np(table):
    high = table.astype(BF16)
    low = (table - high.astype(np.float64)).astype(BF16)
    return [high, low]


def dft_constants(n):
    h = n // 2
    k = np.arange(h)
    angle = 2.0 * np.pi * ((k[:, None] * k[None, :]) % h) / h
    scale = 1.0 / np.sqrt(n)
    c, s = np.cos(angle) * scale, np.sin(angle) * scale
    d = np.block([[c, s], [-s, c]])
    mats = np.stack(split_np(d))
    w = np.exp(-2j * np.pi * k / n)
    tw_left = np.stack([np.tile(w.real[:, None], (1, h)), np.tile(w.imag[:, None], (1, h))])
    tw_right = np.stack([np.tile(w.real[None], (8, 1)), np.tile(w.imag[None], (8, 1))])
    return mats, tw_left.astype(np.float32), tw_right.astype(np.float32)


def split(x):
    high = x.astype(BF16)
    return high, (x - high.astype(F32)).astype(BF16)


def dot(a, b):
    return jnp.dot(a, b, preferred_element_type=F32)


def left_dot(mats, which, x):
    high, low = split(x)
    return dot(mats[which], high) + (dot(mats[which], low) + dot(mats[which + 1], high))


def right_dot(x, mats, which):
    high, low = split(x)
    return dot(high, mats[which]) + (dot(low, mats[which]) + dot(high, mats[which + 1]))


def cat(parts, axis):
    return jnp.concatenate(parts, axis=axis)


def product(a, b):
    return (a[0] * b[0] - a[1] * b[1], a[0] * b[1] + a[1] * b[0])


def conj_product(a, b):
    return (a[0] * b[0] + a[1] * b[1], a[0] * b[1] - a[1] * b[0])


class Dft:
    def __init__(self, mats, tw_left, tw_right, n):
        self.mats, self.n, self.h = mats, n, n // 2
        self.tw_left, self.tw_right = tw_left, tw_right

    def wl(self, width):
        parts = width // self.tw_left.shape[2]
        return [cat([self.tw_left[i]] * parts, 1) for i in range(2)]

    def wr(self):
        return [self.tw_right[i, 0:1] for i in range(2)]

    def left(self, x):
        h, w = self.h, x[0].shape[1]
        total = [p[:h] + p[h:] for p in x]
        odd = product([p[:h] - p[h:] for p in x], self.wl(w))
        u = left_dot(self.mats, 0, cat(total, 0))
        v = left_dot(self.mats, 0, cat(odd, 0))
        return [cat([u[:h], v[:h]], 0), cat([u[h:], v[h:]], 0)]

    def right(self, x):
        h, m = self.h, x[0].shape[0]
        total = [p[:, :h] + p[:, h:] for p in x]
        odd = product([p[:, :h] - p[:, h:] for p in x], self.wr())
        u = right_dot(cat(total, 1), self.mats, 2)
        v = right_dot(cat(odd, 1), self.mats, 2)
        return [cat([u[:, :h], v[:, :h]], 1), cat([u[:, h:], v[:, h:]], 1)]

    def right_inverse(self, x):
        h, m = self.h, x[0].shape[0]
        u = right_dot(cat([p[:, :h] for p in x], 1), self.mats, 0)
        v = right_dot(cat([p[:, h:] for p in x], 1), self.mats, 0)
        even = [u[:, :h], u[:, h:]]
        odd = conj_product(self.wr(), [v[:, :h], v[:, h:]])
        return [cat([e + o, e - o], 1) for e, o in zip(even, odd)]

    def left_inverse(self, x):
        h, w = self.h, x[0].shape[1]
        u = left_dot(self.mats, 2, cat([p[:h] for p in x], 0))
        v = left_dot(self.mats, 2, cat([p[h:] for p in x], 0))
        even = [u[:h], u[h:]]
        odd = conj_product(self.wl(w), [v[:h], v[h:]])
        return [cat([e + o, e - o], 0) for e, o in zip(even, odd)]


SIN = [(-1.0) ** i / math.factorial(2 * i + 1) for i in range(7)]
COS = [(-1.0) ** i / math.factorial(2 * i) for i in range(7)]


def series(coefficients, z):
    total = coefficients[-1]
    for c in coefficients[-2::-1]:
        total = total * z + c
    return total


def cos_sin(x):
    y = 0.5 * x
    z = y * y
    s, c = y * series(SIN, z), series(COS, z)
    return 1.0 - 2.0 * (s * s), 2.0 * (s * c)


def iota(shape, dim):
    return lax.broadcasted_iota(jnp.int32, shape, dim)


def dyn_roll(x, shift, axis):
    return pltpu.roll(x, shift, axis=axis)


def half_roll(x):
    return pltpu.roll(x, x.shape[-1] // 2, axis=x.ndim - 1)


def pack_cols(re, im):
    h = re.shape[1] // 2
    front = iota((re.shape[0], h), 1) < h // 2
    low = jnp.where(front, re[:, :h], half_roll(im[:, :h]))
    high = jnp.where(front, half_roll(im[:, h:]), re[:, h:])
    return low, high


def copy_all(sources, places, sems):
    copies = [
        pltpu.make_async_copy(a, b, sems.at[i]) for i, (a, b) in enumerate(zip(sources, places))
    ]
    for copy in copies:
        copy.start()
    return copies


def row_start(which, n, margin):
    even = lax.axis_index("row") % 2 == 0
    last = even if which == 0 else jnp.logical_not(even)
    return pl.multiple_of(jnp.where(last, n - margin, 0), 8)


def pack_kernel(margin, obj_hbm, offs_hbm, obj, offs, limits, *refs):
    strips, rows, sems = refs[:4], refs[4:-1], refs[-1]
    n = obj.shape[1]
    copies = copy_all(
        (obj_hbm.at[0:2], obj_hbm.at[2:4], offs_hbm), (obj.at[0:2], obj.at[2:4], offs), sems
    )
    even = lax.axis_index("col") % 2 == 0
    for s in range(2):
        copies[s].wait()
        low, high = pack_cols(obj[2 * s], obj[2 * s + 1])
        strips[2 * s][...] = jnp.where(even, high, low)
        strips[2 * s + 1][...] = jnp.where(even, low, high)
    for which, out in enumerate(rows):
        out[...] = obj[:, pl.ds(row_start(which, n, margin), margin), :]
    copies[2].wait()
    for i in range(2):
        limits[i] = jnp.full(limits.shape[1:], offs[0, i] - margin, jnp.int32)


def corner_kernel(margin, e, o, after, *outs):
    for which, out in enumerate(outs):
        rows = pl.ds(row_start(which, e.shape[0], margin), margin)
        out[0] = e[rows, :]
        out[1] = o[rows, :]


def even_odd(n, axis):
    h = n // 2
    natural, sorted_ = iota((n, n), axis), iota((n, n), 1 - axis)
    source = jnp.where(sorted_ < h, 2 * sorted_, 2 * (sorted_ - h) + 1)
    return (natural == source).astype(F32).astype(BF16)


def reorder(x, order):
    def thirds(y):
        a = y.astype(BF16)
        return (a,) + split(y - a.astype(F32))

    a, b, c = thirds(x)
    a, b, c = thirds(dot(order[1], a) + (dot(order[1], b) + dot(order[1], c)))
    return dot(a, order[0]) + (dot(b, order[0]) + dot(c, order[0]))


def prep_kernel(*refs):
    hbm, (kr, ki, am, mats), loaded = refs[:6], refs[6:10], refs[10:13]
    phase, amps, table, sems = refs[13:]
    n = phase.shape[0]
    h = n // 2
    copies = copy_all(hbm, (phase, table, amps) + loaded, sems)
    order = [even_odd(n, axis) for axis in range(2)]
    copies[0].wait()
    angle = reorder(phase[...], order)
    kr[...], ki[...] = cos_sin(angle)
    copies[1].wait()
    for i in range(2):
        mats[i] = table[i]
        mats[2 + i, :h, :h] = table[i, :h, :h]
        mats[2 + i, :h, h:] = -table[i, :h, h:]
        mats[2 + i, h:, :h] = -table[i, h:, :h]
        mats[2 + i, h:, h:] = table[i, h:, h:]
    copies[2].wait()
    am[...] = reorder(amps[...], order)
    for copy in copies[3:]:
        copy.wait()


def roll_kernel(margin, offs, probe, pr):
    n = probe.shape[1]
    sy = (offs[0, 0] - margin + n) % n
    sx = (offs[0, 1] - margin + n) % n
    for i in range(2):
        pr[i] = dyn_roll(dyn_roll(probe[i], sy, 0), sx, 1)


def merge_cols(own, e, o, limits):
    n = own[0].shape[1]
    h = n // 2
    even = lax.axis_index("col") % 2 == 0
    high, low = jnp.where(even, e, o), jnp.where(even, o, e)
    lane = iota((1, h), 1)
    from_high = lane < limits[1, 0:1]
    from_low = lane >= limits[1, 0:1] + h
    out = []
    for i in range(2):
        strip_high = high if i == 0 else half_roll(high)
        strip_low = low if i == 0 else half_roll(low)
        out.append(
            cat(
                [
                    jnp.where(from_high, strip_high, own[i][:, :h]),
                    jnp.where(from_low, strip_low, own[i][:, h:]),
                ],
                1,
            )
        )
    return out


def merge_kernel(s, obj, e, o, limits, out):
    own = [obj[2 * s], obj[2 * s + 1]]
    out[0], out[1] = merge_cols(own, e[...], o[...], limits)


def window_of(main, s, halos, corners, limits, margin):
    n = main.shape[1]
    row_even = lax.axis_index("row") % 2 == 0
    blocks = []
    for halo, corner in zip(halos, corners):
        own = [halo[2 * s], halo[2 * s + 1]]
        blocks.append(merge_cols(own, corner[0], corner[1], limits))
    row = iota((margin, n), 0)
    limit = cat([limits[0, 0:1]] * 2, 1)
    take_high = row < limit
    take_low = row >= limit + margin
    out = []
    for i in range(2):
        e = blocks[0][i]
        o = blocks[1][i] if len(blocks) == 2 else jnp.zeros_like(e)
        high, low = jnp.where(row_even, e, o), jnp.where(row_even, o, e)
        out.append(
            cat(
                [
                    jnp.where(take_high, high, main[i, :margin]),
                    main[i, margin : n - margin],
                    jnp.where(take_low, low, main[i, n - margin :]),
                ],
                0,
            )
        )
    return out


def unpack(n_row, refs):
    return refs[0], refs[1 : 1 + n_row], refs[1 + n_row : 1 + 2 * n_row], refs[1 + 2 * n_row :]


def through(dft, x, re, im):
    return dft.right_inverse(product([re, im], dft.right(x)))


def arrive_kernel(n_row, margin, *refs):
    main, halos, corners, refs = unpack(n_row, refs)
    limits, pr, kr, ki, mats, twl, twr, w1, arrive = refs
    n = main.shape[1]
    dft = Dft(mats, twl[...], twr[...], n)
    win = window_of(main, 0, halos, corners, limits, margin)
    w1[0], w1[1] = win
    x = dft.left(product([pr[0], pr[1]], win))
    x = through(dft, x, kr[...], ki[...])
    arrive[0], arrive[1] = dft.left_inverse(x)


def back_kernel(n_row, margin, *refs):
    main, halos, corners, refs = unpack(n_row, refs)
    limits, offs_hbm, pr, kr, ki, am, w1, arrive, mats, twl, twr = refs[:11]
    keep, give, grads, offs, sem = refs[11:]
    scalars = pltpu.make_async_copy(offs_hbm, offs, sem)
    scalars.start()
    n = main.shape[1]
    dft = Dft(mats, twl[...], twr[...], n)
    win = window_of(main, 1, halos, corners, limits, margin)
    x = dft.left(product([arrive[0], arrive[1]], win))
    far = dft.right(x)
    modulus = jnp.sqrt(far[0] * far[0] + far[1] * far[1] + EPS_AMP)
    factor = 2.0 * (1.0 - am[...] / modulus)
    x = dft.right_inverse([factor * far[0], factor * far[1]])
    back_far = dft.left_inverse(x)
    grads[2], grads[3] = conj_product([arrive[0], arrive[1]], back_far)
    x = dft.left(conj_product(win, back_far))
    x = through(dft, x, kr[...], -ki[...])
    x = dft.left_inverse(x)
    grads[0], grads[1] = conj_product([pr[0], pr[1]], x)
    grad = conj_product([w1[0], w1[1]], x)
    scalars.wait()
    sy = (margin - offs[0, 0] + n) % n
    sx = (margin - offs[0, 1] + n) % n
    grad = [dyn_roll(dyn_roll(g, sy, 0), sx, 1) for g in grad]
    even = lax.axis_index("row") % 2 == 0
    keep[...] = jnp.where(even, grad[0], grad[1])
    give[...] = jnp.where(even, grad[1], grad[0])


def divide_kernel(margin, grads, limits, own, strip, *sends):
    for s in range(2):
        split_grad([grads[2 * s], grads[2 * s + 1]], s, limits, margin, own, strip, sends)


def split_grad(grad, s, limits, margin, own, strip, sends):
    n = grad[0].shape[0]
    h = n // 2
    row_even = lax.axis_index("row") % 2 == 0
    lane = iota((1, h), 1)
    to_high, to_low = lane < limits[1, 0:1], lane >= limits[1, 0:1] + h
    front = lane < h // 2
    spill = jnp.where(front, to_high.astype(jnp.int32), to_low.astype(jnp.int32)) != 0
    for i in range(2):
        g = grad[i]
        row = iota((n, h), 0)
        high_rows = row < limits[0, 0:1]
        low_rows = row >= limits[0, 0:1] + n
        inner = jnp.logical_not(jnp.logical_or(high_rows, low_rows))
        left = jnp.where(to_high, 0.0, g[:, :h])
        right = jnp.where(to_low, 0.0, g[:, h:])
        side = jnp.where(spill, jnp.where(front, g[:, :h], g[:, h:]), 0.0)
        pieces = [left, right, side]
        own[2 * s + i, :, :h] = jnp.where(inner, left, 0.0)
        own[2 * s + i, :, h:] = jnp.where(inner, right, 0.0)
        strip[2 * s + i] = jnp.where(inner, side, 0.0)
        for j, piece in enumerate(pieces):
            top = jnp.where(high_rows[:margin], piece[:margin], 0.0)
            bottom = jnp.where(low_rows[n - margin :], piece[n - margin :], 0.0)
            for which, send in enumerate(sends):
                first = row_even if which == 0 else jnp.logical_not(row_even)
                send[2 * s + i, :, j * h : (j + 1) * h] = jnp.where(first, top, bottom)


def fold_rows_kernel(n_row, margin, own, strip, *refs):
    got, (total, send_e, send_o) = refs[:n_row], refs[n_row:]
    row_even = lax.axis_index("row") % 2 == 0
    col_even = lax.axis_index("col") % 2 == 0
    n = own.shape[1]
    h = n // 2
    front = iota((n, h), 1) < h // 2
    for s in range(2):
        strips = []
        for i in range(2 * s, 2 * s + 2):
            total[i] = own[i]
            r = got[0][i]
            q = got[1][i] if n_row == 2 else jnp.zeros_like(r)
            top, bottom = jnp.where(row_even, q, r), jnp.where(row_even, r, q)
            total[i, :margin] += top[:, :n]
            total[i, n - margin :] += bottom[:, :n]
            st = strip[i]
            strips.append(
                cat(
                    [
                        st[:margin] + top[:, n:],
                        st[margin : n - margin],
                        st[n - margin :] + bottom[:, n:],
                    ],
                    0,
                )
            )
        moved = half_roll(strips[1])
        to_high = jnp.where(front, strips[0], moved)
        to_low = jnp.where(front, moved, strips[0])
        send_e[s] = jnp.where(col_even, to_high, to_low)
        send_o[s] = jnp.where(col_even, to_low, to_high)


def fold_cols_kernel(total, e, o, out):
    col_even = lax.axis_index("col") % 2 == 0
    n = total.shape[1]
    h = n // 2
    front = iota((n, h), 1) < h // 2
    for s in range(2):
        high = jnp.where(col_even, e[s], o[s])
        low = jnp.where(col_even, o[s], e[s])
        for i in range(2):
            a = low if i == 0 else half_roll(low)
            b = high if i == 0 else half_roll(high)
            at = 2 * s + i
            out[at, :, :h] = total[at, :, :h] + jnp.where(front, a, 0.0)
            out[at, :, h:] = total[at, :, h:] + jnp.where(front, 0.0, b)


def in_hbm(x):
    return pltpu.with_memory_space_constraint(x, pltpu.HBM)


def call(kernel, shapes, in_specs, *args, scratch=(), mib=16):
    shapes = [s if isinstance(s, jax.ShapeDtypeStruct) else jax.ShapeDtypeStruct(s, F32) for s in shapes]
    return pl.pallas_call(
        kernel,
        out_shape=shapes,
        in_specs=in_specs,
        out_specs=[SMEM if s.shape == (1, 2) else VMEM for s in shapes],
        scratch_shapes=list(scratch),
        compiler_params=pltpu.CompilerParams(vmem_limit_bytes=mib << 20),
    )(*args)


def edges(axis):
    count = lax.axis_size(axis)
    rounds = []
    for first in (0, 1):
        pairs = [(i, i + 1) for i in range(first, count - 1, 2)]
        pairs += [(b, a) for a, b in pairs]
        if pairs:
            rounds.append(pairs)
    return rounds


def swap(value, axis, distance):
    count = lax.axis_size(axis)
    return lax.ppermute(value, axis, [(i, i ^ distance) for i in range(count)])


def groups():
    cols = [("col", 1 << b) for b in range(lax.axis_size("col").bit_length() - 1)]
    rows = [("row", 1 << b) for b in range(1, lax.axis_size("row").bit_length() - 1)]
    first, rest = cols[:2], cols[2:]
    pairs = [first]
    for bits in (rest, rows):
        pairs += [bits[i : i + 2] for i in range(0, len(bits), 2)]
    out = []
    for pair in pairs:
        axis, masks = pair[0][0], [m for _, m in pair]
        out.append((axis, [0] + masks + ([sum(masks)] if len(masks) == 2 else [])))
    return out


def pair_sum(parts):
    while len(parts) > 1:
        parts = [parts[i] + parts[i + 1] for i in range(0, len(parts), 2)]
    return parts[0]


def share_kernel(quad, stride, keep, other, *parts):
    place = lax.axis_index("col") // stride % quad
    chunk = keep.shape[0] // quad
    for j, part in enumerate(parts):
        rows = pl.ds(pl.multiple_of((place ^ j) * chunk, 8), chunk)
        part[...] = keep[rows, :] + other[rows, :]


def sum_kernel(*refs):
    refs[-1][...] = pair_sum([r[...] for r in refs[:-1]])


def join_kernel(stride, *refs):
    parts, full = refs[:-1], refs[-1]
    quad, chunk = len(parts), parts[0].shape[0]
    place = lax.axis_index("col") // stride % quad
    for j, part in enumerate(parts):
        full[pl.ds(pl.multiple_of((place ^ j) * chunk, 8), chunk), :] = part[...]


def half_kernel(full, out, sem):
    copy = pltpu.make_async_copy(full, out.at[lax.axis_index("row") % 2], sem)
    copy.start()
    copy.wait()


def other_kernel(started, other, out, sem):
    copy = pltpu.make_async_copy(other, out.at[1 - lax.axis_index("row") % 2], sem)
    copy.start()
    copy.wait()


def reduce_probe(keep, give):
    n = keep.shape[0]
    (_, offsets), *rest = groups()
    quad, stride = len(offsets), offsets[1]
    chunk = n // quad
    other = swap(give, "row", 1)
    parts = call(
        functools.partial(share_kernel, quad, stride),
        [(chunk, n)] * quad,
        [VMEM] * 2,
        keep,
        other,
    )
    sums = [parts[0]]
    for j in range(1, quad):
        sums.append(swap(parts[j], "col", offsets[j]))
    (total,) = call(sum_kernel, [(chunk, n)], [VMEM] * quad, *sums)
    for axis, masks in rest:
        sums = [total]
        for mask in masks[1:]:
            sums.append(swap(total, axis, mask))
        (total,) = call(sum_kernel, [(chunk, n)], [VMEM] * len(sums), *sums)
    parts = [total]
    for j in range(1, quad):
        parts.append(swap(total, "col", offsets[j]))
    (full,) = call(
        functools.partial(join_kernel, stride), [(n, n)], [VMEM] * quad, *parts
    )
    other = swap(full, "row", 1)
    out = dict(
        out_shape=jax.ShapeDtypeStruct((2, n, n), F32),
        out_specs=HBM,
        scratch_shapes=[pltpu.SemaphoreType.DMA(())],
        compiler_params=pltpu.CompilerParams(vmem_limit_bytes=16 << 20),
    )
    grad = pl.pallas_call(half_kernel, in_specs=[VMEM], **out)(full)
    return pl.pallas_call(
        other_kernel, in_specs=[HBM, VMEM], input_output_aliases={0: 0}, **out
    )(grad, other)


def whole(object_field, probe, phase, amplitudes, offsets):
    tile = object_field.shape[2]
    n = probe.shape[1]
    h = n // 2
    margin = n // 4
    mats, tw_left, tw_right = [jnp.asarray(t) for t in dft_constants(n)]

    row_rounds, col_rounds = edges("row"), edges("col")
    n_row = len(row_rounds)
    obj, offs, limits, *packed = call(
        functools.partial(pack_kernel, margin),
        [(4, n, n), jax.ShapeDtypeStruct((1, 2), jnp.int32)]
        + [jax.ShapeDtypeStruct((2, 8, h), jnp.int32)]
        + [(n, h)] * 4
        + [(4, margin, n)] * n_row,
        [HBM, HBM],
        in_hbm(object_field.reshape(4, tile, tile)),
        in_hbm(offsets.reshape(1, 2)),
        scratch=[pltpu.SemaphoreType.DMA((3,))],
    )
    strips, halos, corners = [], [], [[], []]
    for i in range(4):
        strips.append(lax.ppermute(packed[i], "col", col_rounds[i % 2]))
    for i, pairs in enumerate(row_rounds):
        halos.append(lax.ppermute(packed[4 + i], "row", pairs))

    def cut(s, after):
        parts = call(
            functools.partial(corner_kernel, margin),
            [(2, margin, h)] * n_row,
            [VMEM] * 3,
            *strips[2 * s : 2 * s + 2],
            after,
        )
        for i, pairs in enumerate(row_rounds):
            corners[s].append(lax.ppermute(parts[i], "row", pairs))

    def merge(s):
        (main,) = call(
            functools.partial(merge_kernel, s),
            [(2, n, n)],
            [VMEM] * 4,
            obj,
            *strips[2 * s : 2 * s + 2],
            limits,
        )
        return main

    loads = (phase, mats, amplitudes.reshape(n, n), tw_left, tw_right, probe)
    kr, ki, am, mats, tw_left, tw_right, pr = call(
        prep_kernel,
        [(n, n)] * 3
        + [jax.ShapeDtypeStruct((4, n, n), BF16)]
        + [jax.ShapeDtypeStruct(x.shape, x.dtype) for x in loads[3:]],
        [HBM] * len(loads),
        *[in_hbm(x) for x in loads],
        scratch=[
            pltpu.VMEM((n, n), F32),
            pltpu.VMEM((n, n), F32),
            pltpu.VMEM((2, n, n), BF16),
            pltpu.SemaphoreType.DMA((len(loads),)),
        ],
    )
    cut(0, kr)
    (pr,) = call(functools.partial(roll_kernel, margin), [(2, n, n)], [SMEM, VMEM], offs, pr)
    main = merge(0)
    w1, arrive = call(
        functools.partial(arrive_kernel, n_row, margin),
        [(2, n, n), (2, n, n)],
        [VMEM] * (8 + 2 * n_row),
        main,
        *halos,
        *corners[0],
        limits,
        pr,
        kr,
        ki,
        mats,
        tw_left,
        tw_right,
    )
    cut(1, arrive)
    main = merge(1)
    keep, give, grads = call(
        functools.partial(back_kernel, n_row, margin),
        [(n, n), (n, n), (4, n, n)],
        [VMEM] * (2 + 2 * n_row) + [HBM] + [VMEM] * 9,
        main,
        *halos,
        *corners[1],
        limits,
        in_hbm(offsets.reshape(1, 2)),
        pr,
        kr,
        ki,
        am,
        w1,
        arrive,
        mats,
        tw_left,
        tw_right,
        scratch=[pltpu.SMEM((1, 2), jnp.int32), pltpu.SemaphoreType.DMA(())],
        mib=40,
    )
    probe_grad = reduce_probe(keep, give)
    own, strip, *sends = call(
        functools.partial(divide_kernel, margin),
        [(4, n, n), (4, n, h)] + [(4, margin, n + h)] * n_row,
        [VMEM, VMEM],
        grads,
        limits,
    )
    got = []
    for i, pairs in enumerate(row_rounds):
        got.append(lax.ppermute(sends[i], "row", pairs))
    total, send_e, send_o = call(
        functools.partial(fold_rows_kernel, n_row, margin),
        [(4, n, n), (2, n, h), (2, n, h)],
        [VMEM] * (2 + n_row),
        own,
        strip,
        *got,
    )
    send_e = lax.ppermute(send_e, "col", col_rounds[0])
    send_o = lax.ppermute(send_o, "col", col_rounds[1])
    (grad,) = call(fold_cols_kernel, [(4, n, n)], [VMEM] * 3, total, send_e, send_o)
    return (grad.reshape(2, 2, tile, tile), probe_grad)


def solution(mesh):
    placed = (
        P(None, None, "row", "col"),
        P(),
        P(),
        P("row", "col", None, None, None),
        P("row", "col", None, None),
    )
    return jax.shard_map(
        whole,
        mesh=mesh,
        in_specs=placed,
        out_specs=(P(None, None, "row", "col"), P()),
        check_vma=False,
    )
```

```python
import functools
import math

import jax
import jax.numpy as jnp
import numpy as np
from jax import lax
from jax.experimental import pallas as pl
from jax.experimental.pallas import tpu as pltpu
from jax.sharding import PartitionSpec as P


EPS_AMP = 0.5
F32 = jnp.float32
BF16 = jnp.bfloat16
VMEM = pl.BlockSpec(memory_space=pltpu.VMEM)
SMEM = pl.BlockSpec(memory_space=pltpu.SMEM)
HBM = pl.BlockSpec(memory_space=pltpu.HBM)


def split_np(table):
    high = table.astype(BF16)
    low = (table - high.astype(np.float64)).astype(BF16)
    return [high, low]


def dft_constants(n):
    h = n // 2
    k = np.arange(h)
    angle = 2.0 * np.pi * ((k[:, None] * k[None, :]) % h) / h
    scale = 1.0 / np.sqrt(n)
    c, s = np.cos(angle) * scale, np.sin(angle) * scale
    d = np.block([[c, s], [-s, c]])
    mats = np.stack(split_np(d))
    w = np.exp(-2j * np.pi * k / n)
    tw_left = np.stack([np.tile(w.real[:, None], (1, h)), np.tile(w.imag[:, None], (1, h))])
    tw_right = np.stack([np.tile(w.real[None], (8, 1)), np.tile(w.imag[None], (8, 1))])
    return mats, tw_left.astype(np.float32), tw_right.astype(np.float32)


def split(x):
    high = x.astype(BF16)
    return high, (x - high.astype(F32)).astype(BF16)


def dot(a, b):
    return jnp.dot(a, b, preferred_element_type=F32)


def left_dot(mats, which, x):
    high, low = split(x)
    return dot(mats[which], high) + (dot(mats[which], low) + dot(mats[which + 1], high))


def right_dot(x, mats, which):
    high, low = split(x)
    return dot(high, mats[which]) + (dot(low, mats[which]) + dot(high, mats[which + 1]))


def cat(parts, axis):
    return jnp.concatenate(parts, axis=axis)


def product(a, b):
    return (a[0] * b[0] - a[1] * b[1], a[0] * b[1] + a[1] * b[0])


def conj_product(a, b):
    return (a[0] * b[0] + a[1] * b[1], a[0] * b[1] - a[1] * b[0])


class Dft:
    def __init__(self, mats, tw_left, tw_right, n):
        self.mats, self.n, self.h = mats, n, n // 2
        self.tw_left, self.tw_right = tw_left, tw_right

    def wl(self, width):
        parts = width // self.tw_left.shape[2]
        return [cat([self.tw_left[i]] * parts, 1) for i in range(2)]

    def wr(self):
        return [self.tw_right[i, 0:1] for i in range(2)]

    def left(self, x):
        h, w = self.h, x[0].shape[1]
        total = [p[:h] + p[h:] for p in x]
        odd = product([p[:h] - p[h:] for p in x], self.wl(w))
        u = left_dot(self.mats, 0, cat(total, 0))
        v = left_dot(self.mats, 0, cat(odd, 0))
        return [cat([u[:h], v[:h]], 0), cat([u[h:], v[h:]], 0)]

    def right(self, x):
        h, m = self.h, x[0].shape[0]
        total = [p[:, :h] + p[:, h:] for p in x]
        odd = product([p[:, :h] - p[:, h:] for p in x], self.wr())
        u = right_dot(cat(total, 1), self.mats, 2)
        v = right_dot(cat(odd, 1), self.mats, 2)
        return [cat([u[:, :h], v[:, :h]], 1), cat([u[:, h:], v[:, h:]], 1)]

    def right_inverse(self, x):
        h, m = self.h, x[0].shape[0]
        u = right_dot(cat([p[:, :h] for p in x], 1), self.mats, 0)
        v = right_dot(cat([p[:, h:] for p in x], 1), self.mats, 0)
        even = [u[:, :h], u[:, h:]]
        odd = conj_product(self.wr(), [v[:, :h], v[:, h:]])
        return [cat([e + o, e - o], 1) for e, o in zip(even, odd)]

    def left_inverse(self, x):
        h, w = self.h, x[0].shape[1]
        u = left_dot(self.mats, 2, cat([p[:h] for p in x], 0))
        v = left_dot(self.mats, 2, cat([p[h:] for p in x], 0))
        even = [u[:h], u[h:]]
        odd = conj_product(self.wl(w), [v[:h], v[h:]])
        return [cat([e + o, e - o], 0) for e, o in zip(even, odd)]


SIN = [(-1.0) ** i / math.factorial(2 * i + 1) for i in range(7)]
COS = [(-1.0) ** i / math.factorial(2 * i) for i in range(7)]


def series(coefficients, z):
    total = coefficients[-1]
    for c in coefficients[-2::-1]:
        total = total * z + c
    return total


def cos_sin(x):
    y = 0.5 * x
    z = y * y
    s, c = y * series(SIN, z), series(COS, z)
    return 1.0 - 2.0 * (s * s), 2.0 * (s * c)


def iota(shape, dim):
    return lax.broadcasted_iota(jnp.int32, shape, dim)


def dyn_roll(x, shift, axis):
    return pltpu.roll(x, shift, axis=axis)


def half_roll(x):
    return pltpu.roll(x, x.shape[-1] // 2, axis=x.ndim - 1)


def pack_cols(re, im):
    h = re.shape[1] // 2
    front = iota((re.shape[0], h), 1) < h // 2
    low = jnp.where(front, re[:, :h], half_roll(im[:, :h]))
    high = jnp.where(front, half_roll(im[:, h:]), re[:, h:])
    return low, high


def copy_all(sources, places, sems):
    copies = [
        pltpu.make_async_copy(a, b, sems.at[i]) for i, (a, b) in enumerate(zip(sources, places))
    ]
    for copy in copies:
        copy.start()
    return copies


def row_start(which, n, margin):
    even = lax.axis_index("row") % 2 == 0
    last = even if which == 0 else jnp.logical_not(even)
    return pl.multiple_of(jnp.where(last, n - margin, 0), 8)


def pack_kernel(margin, obj_hbm, offs_hbm, obj, offs, limits, *refs):
    strips, rows, sems = refs[:4], refs[4:-1], refs[-1]
    n = obj.shape[1]
    copies = copy_all(
        (obj_hbm.at[0:2], obj_hbm.at[2:4], offs_hbm), (obj.at[0:2], obj.at[2:4], offs), sems
    )
    even = lax.axis_index("col") % 2 == 0
    for s in range(2):
        copies[s].wait()
        low, high = pack_cols(obj[2 * s], obj[2 * s + 1])
        strips[2 * s][...] = jnp.where(even, high, low)
        strips[2 * s + 1][...] = jnp.where(even, low, high)
    for which, out in enumerate(rows):
        out[...] = obj[:, pl.ds(row_start(which, n, margin), margin), :]
    copies[2].wait()
    for i in range(2):
        limits[i] = jnp.full(limits.shape[1:], offs[0, i] - margin, jnp.int32)


def corner_kernel(margin, e, o, after, *outs):
    for which, out in enumerate(outs):
        rows = pl.ds(row_start(which, e.shape[0], margin), margin)
        out[0] = e[rows, :]
        out[1] = o[rows, :]


def even_odd(n, axis):
    h = n // 2
    natural, sorted_ = iota((n, n), axis), iota((n, n), 1 - axis)
    source = jnp.where(sorted_ < h, 2 * sorted_, 2 * (sorted_ - h) + 1)
    return (natural == source).astype(F32).astype(BF16)


def reorder(x, order):
    def thirds(y):
        a = y.astype(BF16)
        return (a,) + split(y - a.astype(F32))

    a, b, c = thirds(x)
    a, b, c = thirds(dot(order[1], a) + (dot(order[1], b) + dot(order[1], c)))
    return dot(a, order[0]) + (dot(b, order[0]) + dot(c, order[0]))


def prep_kernel(*refs):
    hbm, (kr, ki, mats), loaded = refs[:6], refs[6:9], refs[9:13]
    phase, table, sems = refs[13:]
    n = phase.shape[0]
    h = n // 2
    first = pltpu.make_async_copy(hbm[0], phase, sems.at[0])
    first.start()
    order = [even_odd(n, axis) for axis in range(2)]
    first.wait()
    copies = copy_all(hbm[1:], (table,) + loaded, sems)
    angle = reorder(phase[...], order)
    kr[...], ki[...] = cos_sin(angle)
    copies[0].wait()
    for i in range(2):
        mats[i] = table[i]
        mats[2 + i, :h, :h] = table[i, :h, :h]
        mats[2 + i, :h, h:] = -table[i, :h, h:]
        mats[2 + i, h:, :h] = -table[i, h:, :h]
        mats[2 + i, h:, h:] = table[i, h:, h:]
    for copy in copies[1:]:
        copy.wait()


def reorder_kernel(x, after, out):
    out[...] = reorder(x[...], [even_odd(x.shape[0], axis) for axis in range(2)])


def roll_kernel(margin, offs, probe, pr):
    n = probe.shape[1]
    sy = (offs[0, 0] - margin + n) % n
    sx = (offs[0, 1] - margin + n) % n
    for i in range(2):
        pr[i] = dyn_roll(dyn_roll(probe[i], sy, 0), sx, 1)


def merge_cols(own, e, o, limits):
    n = own[0].shape[1]
    h = n // 2
    even = lax.axis_index("col") % 2 == 0
    high, low = jnp.where(even, e, o), jnp.where(even, o, e)
    lane = iota((1, h), 1)
    from_high = lane < limits[1, 0:1]
    from_low = lane >= limits[1, 0:1] + h
    out = []
    for i in range(2):
        strip_high = high if i == 0 else half_roll(high)
        strip_low = low if i == 0 else half_roll(low)
        out.append(
            cat(
                [
                    jnp.where(from_high, strip_high, own[i][:, :h]),
                    jnp.where(from_low, strip_low, own[i][:, h:]),
                ],
                1,
            )
        )
    return out


def merge_kernel(s, obj, e, o, limits, out):
    own = [obj[2 * s], obj[2 * s + 1]]
    out[0], out[1] = merge_cols(own, e[...], o[...], limits)


def window_of(main, s, halos, corners, limits, margin):
    n = main.shape[1]
    row_even = lax.axis_index("row") % 2 == 0
    blocks = []
    for halo, corner in zip(halos, corners):
        own = [halo[2 * s], halo[2 * s + 1]]
        blocks.append(merge_cols(own, corner[0], corner[1], limits))
    row = iota((margin, n), 0)
    limit = cat([limits[0, 0:1]] * 2, 1)
    take_high = row < limit
    take_low = row >= limit + margin
    out = []
    for i in range(2):
        e = blocks[0][i]
        o = blocks[1][i] if len(blocks) == 2 else jnp.zeros_like(e)
        high, low = jnp.where(row_even, e, o), jnp.where(row_even, o, e)
        out.append(
            cat(
                [
                    jnp.where(take_high, high, main[i, :margin]),
                    main[i, margin : n - margin],
                    jnp.where(take_low, low, main[i, n - margin :]),
                ],
                0,
            )
        )
    return out


def unpack(n_row, refs):
    return refs[0], refs[1 : 1 + n_row], refs[1 + n_row : 1 + 2 * n_row], refs[1 + 2 * n_row :]


def through(dft, x, re, im):
    return dft.right_inverse(product([re, im], dft.right(x)))


def arrive_kernel(n_row, margin, *refs):
    main, halos, corners, refs = unpack(n_row, refs)
    limits, pr, kr, ki, mats, twl, twr, w1, arrive = refs
    n = main.shape[1]
    dft = Dft(mats, twl[...], twr[...], n)
    win = window_of(main, 0, halos, corners, limits, margin)
    w1[0], w1[1] = win
    x = dft.left(product([pr[0], pr[1]], win))
    x = through(dft, x, kr[...], ki[...])
    arrive[0], arrive[1] = dft.left_inverse(x)


def back_kernel(n_row, margin, *refs):
    main, halos, corners, refs = unpack(n_row, refs)
    limits, offs_hbm, pr, kr, ki, am, w1, arrive, mats, twl, twr = refs[:11]
    keep, give, grads, offs, sem = refs[11:]
    scalars = pltpu.make_async_copy(offs_hbm, offs, sem)
    scalars.start()
    n = main.shape[1]
    dft = Dft(mats, twl[...], twr[...], n)
    win = window_of(main, 1, halos, corners, limits, margin)
    x = dft.left(product([arrive[0], arrive[1]], win))
    far = dft.right(x)
    modulus = jnp.sqrt(far[0] * far[0] + far[1] * far[1] + EPS_AMP)
    factor = 2.0 * (1.0 - am[...] / modulus)
    x = dft.right_inverse([factor * far[0], factor * far[1]])
    back_far = dft.left_inverse(x)
    grads[2], grads[3] = conj_product([arrive[0], arrive[1]], back_far)
    x = dft.left(conj_product(win, back_far))
    x = through(dft, x, kr[...], -ki[...])
    x = dft.left_inverse(x)
    grads[0], grads[1] = conj_product([pr[0], pr[1]], x)
    grad = conj_product([w1[0], w1[1]], x)
    scalars.wait()
    sy = (margin - offs[0, 0] + n) % n
    sx = (margin - offs[0, 1] + n) % n
    grad = [dyn_roll(dyn_roll(g, sy, 0), sx, 1) for g in grad]
    even = lax.axis_index("row") % 2 == 0
    keep[...] = jnp.where(even, grad[0], grad[1])
    give[...] = jnp.where(even, grad[1], grad[0])


def divide_kernel(margin, grads, limits, own, strip, *sends):
    for s in range(2):
        split_grad([grads[2 * s], grads[2 * s + 1]], s, limits, margin, own, strip, sends)


def split_grad(grad, s, limits, margin, own, strip, sends):
    n = grad[0].shape[0]
    h = n // 2
    row_even = lax.axis_index("row") % 2 == 0
    lane = iota((1, h), 1)
    to_high, to_low = lane < limits[1, 0:1], lane >= limits[1, 0:1] + h
    front = lane < h // 2
    spill = jnp.where(front, to_high.astype(jnp.int32), to_low.astype(jnp.int32)) != 0
    for i in range(2):
        g = grad[i]
        row = iota((n, h), 0)
        high_rows = row < limits[0, 0:1]
        low_rows = row >= limits[0, 0:1] + n
        inner = jnp.logical_not(jnp.logical_or(high_rows, low_rows))
        left = jnp.where(to_high, 0.0, g[:, :h])
        right = jnp.where(to_low, 0.0, g[:, h:])
        side = jnp.where(spill, jnp.where(front, g[:, :h], g[:, h:]), 0.0)
        pieces = [left, right, side]
        own[2 * s + i, :, :h] = jnp.where(inner, left, 0.0)
        own[2 * s + i, :, h:] = jnp.where(inner, right, 0.0)
        strip[2 * s + i] = jnp.where(inner, side, 0.0)
        for j, piece in enumerate(pieces):
            top = jnp.where(high_rows[:margin], piece[:margin], 0.0)
            bottom = jnp.where(low_rows[n - margin :], piece[n - margin :], 0.0)
            for which, send in enumerate(sends):
                first = row_even if which == 0 else jnp.logical_not(row_even)
                send[2 * s + i, :, j * h : (j + 1) * h] = jnp.where(first, top, bottom)


def fold_rows_kernel(n_row, margin, own, strip, *refs):
    got, (total, send_e, send_o) = refs[:n_row], refs[n_row:]
    row_even = lax.axis_index("row") % 2 == 0
    col_even = lax.axis_index("col") % 2 == 0
    n = own.shape[1]
    h = n // 2
    front = iota((n, h), 1) < h // 2
    for s in range(2):
        strips = []
        for i in range(2 * s, 2 * s + 2):
            total[i] = own[i]
            r = got[0][i]
            q = got[1][i] if n_row == 2 else jnp.zeros_like(r)
            top, bottom = jnp.where(row_even, q, r), jnp.where(row_even, r, q)
            total[i, :margin] += top[:, :n]
            total[i, n - margin :] += bottom[:, :n]
            st = strip[i]
            strips.append(
                cat(
                    [
                        st[:margin] + top[:, n:],
                        st[margin : n - margin],
                        st[n - margin :] + bottom[:, n:],
                    ],
                    0,
                )
            )
        moved = half_roll(strips[1])
        to_high = jnp.where(front, strips[0], moved)
        to_low = jnp.where(front, moved, strips[0])
        send_e[s] = jnp.where(col_even, to_high, to_low)
        send_o[s] = jnp.where(col_even, to_low, to_high)


def fold_cols_kernel(total, e, o, out):
    col_even = lax.axis_index("col") % 2 == 0
    n = total.shape[1]
    h = n // 2
    front = iota((n, h), 1) < h // 2
    for s in range(2):
        high = jnp.where(col_even, e[s], o[s])
        low = jnp.where(col_even, o[s], e[s])
        for i in range(2):
            a = low if i == 0 else half_roll(low)
            b = high if i == 0 else half_roll(high)
            at = 2 * s + i
            out[at, :, :h] = total[at, :, :h] + jnp.where(front, a, 0.0)
            out[at, :, h:] = total[at, :, h:] + jnp.where(front, 0.0, b)


def in_hbm(x):
    return pltpu.with_memory_space_constraint(x, pltpu.HBM)


def call(kernel, shapes, in_specs, *args, scratch=(), mib=16):
    shapes = [s if isinstance(s, jax.ShapeDtypeStruct) else jax.ShapeDtypeStruct(s, F32) for s in shapes]
    return pl.pallas_call(
        kernel,
        out_shape=shapes,
        in_specs=in_specs,
        out_specs=[SMEM if s.shape == (1, 2) else VMEM for s in shapes],
        scratch_shapes=list(scratch),
        compiler_params=pltpu.CompilerParams(vmem_limit_bytes=mib << 20),
    )(*args)


def edges(axis):
    count = lax.axis_size(axis)
    rounds = []
    for first in (0, 1):
        pairs = [(i, i + 1) for i in range(first, count - 1, 2)]
        pairs += [(b, a) for a, b in pairs]
        if pairs:
            rounds.append(pairs)
    return rounds


def swap(value, axis, distance):
    count = lax.axis_size(axis)
    return lax.ppermute(value, axis, [(i, i ^ distance) for i in range(count)])


def groups():
    cols = [("col", 1 << b) for b in range(lax.axis_size("col").bit_length() - 1)]
    rows = [("row", 1 << b) for b in range(1, lax.axis_size("row").bit_length() - 1)]
    first, rest = cols[:2], cols[2:]
    pairs = [first]
    for bits in (rest, rows):
        pairs += [bits[i : i + 2] for i in range(0, len(bits), 2)]
    out = []
    for pair in pairs:
        axis, masks = pair[0][0], [m for _, m in pair]
        out.append((axis, [0] + masks + ([sum(masks)] if len(masks) == 2 else [])))
    return out


def pair_sum(parts):
    while len(parts) > 1:
        parts = [parts[i] + parts[i + 1] for i in range(0, len(parts), 2)]
    return parts[0]


def share_kernel(quad, stride, keep, other, *parts):
    place = lax.axis_index("col") // stride % quad
    chunk = keep.shape[0] // quad
    for j, part in enumerate(parts):
        rows = pl.ds(pl.multiple_of((place ^ j) * chunk, 8), chunk)
        part[...] = keep[rows, :] + other[rows, :]


def sum_kernel(*refs):
    refs[-1][...] = pair_sum([r[...] for r in refs[:-1]])


def join_kernel(stride, *refs):
    parts, full = refs[:-1], refs[-1]
    quad, chunk = len(parts), parts[0].shape[0]
    place = lax.axis_index("col") // stride % quad
    for j, part in enumerate(parts):
        full[pl.ds(pl.multiple_of((place ^ j) * chunk, 8), chunk), :] = part[...]


def half_kernel(full, out, sem):
    copy = pltpu.make_async_copy(full, out.at[lax.axis_index("row") % 2], sem)
    copy.start()
    copy.wait()


def other_kernel(started, other, out, sem):
    copy = pltpu.make_async_copy(other, out.at[1 - lax.axis_index("row") % 2], sem)
    copy.start()
    copy.wait()


def reduce_probe(keep, give):
    n = keep.shape[0]
    (_, offsets), *rest = groups()
    quad, stride = len(offsets), offsets[1]
    chunk = n // quad
    other = swap(give, "row", 1)
    parts = call(
        functools.partial(share_kernel, quad, stride),
        [(chunk, n)] * quad,
        [VMEM] * 2,
        keep,
        other,
    )
    sums = [parts[0]]
    for j in range(1, quad):
        sums.append(swap(parts[j], "col", offsets[j]))
    (total,) = call(sum_kernel, [(chunk, n)], [VMEM] * quad, *sums)
    for axis, masks in rest:
        sums = [total]
        for mask in masks[1:]:
            sums.append(swap(total, axis, mask))
        (total,) = call(sum_kernel, [(chunk, n)], [VMEM] * len(sums), *sums)
    parts = [total]
    for j in range(1, quad):
        parts.append(swap(total, "col", offsets[j]))
    (full,) = call(
        functools.partial(join_kernel, stride), [(n, n)], [VMEM] * quad, *parts
    )
    other = swap(full, "row", 1)
    out = dict(
        out_shape=jax.ShapeDtypeStruct((2, n, n), F32),
        out_specs=HBM,
        scratch_shapes=[pltpu.SemaphoreType.DMA(())],
        compiler_params=pltpu.CompilerParams(vmem_limit_bytes=16 << 20),
    )
    grad = pl.pallas_call(half_kernel, in_specs=[VMEM], **out)(full)
    return pl.pallas_call(
        other_kernel, in_specs=[HBM, VMEM], input_output_aliases={0: 0}, **out
    )(grad, other)


def whole(object_field, probe, phase, amplitudes, offsets):
    tile = object_field.shape[2]
    n = probe.shape[1]
    h = n // 2
    margin = n // 4
    mats, tw_left, tw_right = [jnp.asarray(t) for t in dft_constants(n)]

    row_rounds, col_rounds = edges("row"), edges("col")
    n_row = len(row_rounds)
    obj, offs, limits, *packed = call(
        functools.partial(pack_kernel, margin),
        [(4, n, n), jax.ShapeDtypeStruct((1, 2), jnp.int32)]
        + [jax.ShapeDtypeStruct((2, 8, h), jnp.int32)]
        + [(n, h)] * 4
        + [(4, margin, n)] * n_row,
        [HBM, HBM],
        in_hbm(object_field.reshape(4, tile, tile)),
        in_hbm(offsets.reshape(1, 2)),
        scratch=[pltpu.SemaphoreType.DMA((3,))],
    )
    strips, halos, corners = [], [], [[], []]
    for i in range(4):
        strips.append(lax.ppermute(packed[i], "col", col_rounds[i % 2]))
    for i, pairs in enumerate(row_rounds):
        halos.append(lax.ppermute(packed[4 + i], "row", pairs))

    def cut(s, after):
        parts = call(
            functools.partial(corner_kernel, margin),
            [(2, margin, h)] * n_row,
            [VMEM] * 3,
            *strips[2 * s : 2 * s + 2],
            after,
        )
        for i, pairs in enumerate(row_rounds):
            corners[s].append(lax.ppermute(parts[i], "row", pairs))

    def merge(s):
        (main,) = call(
            functools.partial(merge_kernel, s),
            [(2, n, n)],
            [VMEM] * 4,
            obj,
            *strips[2 * s : 2 * s + 2],
            limits,
        )
        return main

    loads = (phase, mats, tw_left, tw_right, probe, amplitudes.reshape(n, n))
    kr, ki, mats, tw_left, tw_right, pr, am = call(
        prep_kernel,
        [(n, n)] * 2
        + [jax.ShapeDtypeStruct((4, n, n), BF16)]
        + [jax.ShapeDtypeStruct(x.shape, x.dtype) for x in loads[2:]],
        [HBM] * len(loads),
        *[in_hbm(x) for x in loads],
        scratch=[
            pltpu.VMEM((n, n), F32),
            pltpu.VMEM((2, n, n), BF16),
            pltpu.SemaphoreType.DMA((len(loads),)),
        ],
    )
    cut(0, kr)
    (pr,) = call(functools.partial(roll_kernel, margin), [(2, n, n)], [SMEM, VMEM], offs, pr)
    main = merge(0)
    w1, arrive = call(
        functools.partial(arrive_kernel, n_row, margin),
        [(2, n, n), (2, n, n)],
        [VMEM] * (8 + 2 * n_row),
        main,
        *halos,
        *corners[0],
        limits,
        pr,
        kr,
        ki,
        mats,
        tw_left,
        tw_right,
    )
    cut(1, arrive)
    (am,) = call(reorder_kernel, [(n, n)], [VMEM] * 2, am, arrive)
    main = merge(1)
    keep, give, grads = call(
        functools.partial(back_kernel, n_row, margin),
        [(n, n), (n, n), (4, n, n)],
        [VMEM] * (2 + 2 * n_row) + [HBM] + [VMEM] * 9,
        main,
        *halos,
        *corners[1],
        limits,
        in_hbm(offsets.reshape(1, 2)),
        pr,
        kr,
        ki,
        am,
        w1,
        arrive,
        mats,
        tw_left,
        tw_right,
        scratch=[pltpu.SMEM((1, 2), jnp.int32), pltpu.SemaphoreType.DMA(())],
        mib=40,
    )
    probe_grad = reduce_probe(keep, give)
    own, strip, *sends = call(
        functools.partial(divide_kernel, margin),
        [(4, n, n), (4, n, h)] + [(4, margin, n + h)] * n_row,
        [VMEM, VMEM],
        grads,
        limits,
    )
    got = []
    for i, pairs in enumerate(row_rounds):
        got.append(lax.ppermute(sends[i], "row", pairs))
    total, send_e, send_o = call(
        functools.partial(fold_rows_kernel, n_row, margin),
        [(4, n, n), (2, n, h), (2, n, h)],
        [VMEM] * (2 + n_row),
        own,
        strip,
        *got,
    )
    send_e = lax.ppermute(send_e, "col", col_rounds[0])
    send_o = lax.ppermute(send_o, "col", col_rounds[1])
    (grad,) = call(fold_cols_kernel, [(4, n, n)], [VMEM] * 3, total, send_e, send_o)
    return (grad.reshape(2, 2, tile, tile), probe_grad)


def solution(mesh):
    placed = (
        P(None, None, "row", "col"),
        P(),
        P(),
        P("row", "col", None, None, None),
        P("row", "col", None, None),
    )
    return jax.shard_map(
        whole,
        mesh=mesh,
        in_specs=placed,
        out_specs=(P(None, None, "row", "col"), P()),
        check_vma=False,
    )
```

```python
import functools
import math

import jax
import jax.numpy as jnp
import numpy as np
from jax import lax
from jax.experimental import pallas as pl
from jax.experimental.pallas import tpu as pltpu
from jax.sharding import PartitionSpec as P


EPS_AMP = 0.5
F32 = jnp.float32
BF16 = jnp.bfloat16
VMEM = pl.BlockSpec(memory_space=pltpu.VMEM)
SMEM = pl.BlockSpec(memory_space=pltpu.SMEM)
HBM = pl.BlockSpec(memory_space=pltpu.HBM)


def split_np(table):
    high = table.astype(BF16)
    low = (table - high.astype(np.float64)).astype(BF16)
    return [high, low]


def dft_constants(n):
    h = n // 2
    k = np.arange(h)
    angle = 2.0 * np.pi * ((k[:, None] * k[None, :]) % h) / h
    scale = 1.0 / np.sqrt(n)
    c, s = np.cos(angle) * scale, np.sin(angle) * scale
    d = np.block([[c, s], [-s, c]])
    mats = np.stack(split_np(d))
    w = np.exp(-2j * np.pi * k / n)
    tw_left = np.stack([np.tile(w.real[:, None], (1, h)), np.tile(w.imag[:, None], (1, h))])
    tw_right = np.stack([np.tile(w.real[None], (8, 1)), np.tile(w.imag[None], (8, 1))])
    return mats, tw_left.astype(np.float32), tw_right.astype(np.float32)


def split(x):
    high = x.astype(BF16)
    return high, (x - high.astype(F32)).astype(BF16)


def dot(a, b):
    return jnp.dot(a, b, preferred_element_type=F32)


def left_dot(mats, which, x):
    high, low = split(x)
    return dot(mats[which], high) + (dot(mats[which], low) + dot(mats[which + 1], high))


def right_dot(x, mats, which):
    high, low = split(x)
    return dot(high, mats[which]) + (dot(low, mats[which]) + dot(high, mats[which + 1]))


def cat(parts, axis):
    return jnp.concatenate(parts, axis=axis)


def product(a, b):
    return (a[0] * b[0] - a[1] * b[1], a[0] * b[1] + a[1] * b[0])


def conj_product(a, b):
    return (a[0] * b[0] + a[1] * b[1], a[0] * b[1] - a[1] * b[0])


class Dft:
    def __init__(self, mats, tw_left, tw_right, n):
        self.mats, self.n, self.h = mats, n, n // 2
        self.tw_left, self.tw_right = tw_left, tw_right

    def wl(self, width):
        parts = width // self.tw_left.shape[2]
        return [cat([self.tw_left[i]] * parts, 1) for i in range(2)]

    def wr(self):
        return [self.tw_right[i, 0:1] for i in range(2)]

    def left(self, x):
        h, w = self.h, x[0].shape[1]
        total = [p[:h] + p[h:] for p in x]
        odd = product([p[:h] - p[h:] for p in x], self.wl(w))
        u = left_dot(self.mats, 0, cat(total, 0))
        v = left_dot(self.mats, 0, cat(odd, 0))
        return [cat([u[:h], v[:h]], 0), cat([u[h:], v[h:]], 0)]

    def right(self, x):
        h, m = self.h, x[0].shape[0]
        total = [p[:, :h] + p[:, h:] for p in x]
        odd = product([p[:, :h] - p[:, h:] for p in x], self.wr())
        u = right_dot(cat(total, 1), self.mats, 2)
        v = right_dot(cat(odd, 1), self.mats, 2)
        return [cat([u[:, :h], v[:, :h]], 1), cat([u[:, h:], v[:, h:]], 1)]

    def right_inverse(self, x):
        h, m = self.h, x[0].shape[0]
        u = right_dot(cat([p[:, :h] for p in x], 1), self.mats, 0)
        v = right_dot(cat([p[:, h:] for p in x], 1), self.mats, 0)
        even = [u[:, :h], u[:, h:]]
        odd = conj_product(self.wr(), [v[:, :h], v[:, h:]])
        return [cat([e + o, e - o], 1) for e, o in zip(even, odd)]

    def left_inverse(self, x):
        h, w = self.h, x[0].shape[1]
        u = left_dot(self.mats, 2, cat([p[:h] for p in x], 0))
        v = left_dot(self.mats, 2, cat([p[h:] for p in x], 0))
        even = [u[:h], u[h:]]
        odd = conj_product(self.wl(w), [v[:h], v[h:]])
        return [cat([e + o, e - o], 0) for e, o in zip(even, odd)]


SIN = [(-1.0) ** i / math.factorial(2 * i + 1) for i in range(7)]
COS = [(-1.0) ** i / math.factorial(2 * i) for i in range(7)]


def series(coefficients, z):
    total = coefficients[-1]
    for c in coefficients[-2::-1]:
        total = total * z + c
    return total


def cos_sin(x):
    y = 0.5 * x
    z = y * y
    s, c = y * series(SIN, z), series(COS, z)
    return 1.0 - 2.0 * (s * s), 2.0 * (s * c)


def iota(shape, dim):
    return lax.broadcasted_iota(jnp.int32, shape, dim)


def dyn_roll(x, shift, axis):
    return pltpu.roll(x, shift, axis=axis)


def half_roll(x):
    return pltpu.roll(x, x.shape[-1] // 2, axis=x.ndim - 1)


def pack_cols(re, im):
    h = re.shape[1] // 2
    front = iota((re.shape[0], h), 1) < h // 2
    low = jnp.where(front, re[:, :h], half_roll(im[:, :h]))
    high = jnp.where(front, half_roll(im[:, h:]), re[:, h:])
    return low, high


def copy_all(sources, places, sems):
    copies = [
        pltpu.make_async_copy(a, b, sems.at[i]) for i, (a, b) in enumerate(zip(sources, places))
    ]
    for copy in copies:
        copy.start()
    return copies


def row_start(which, n, margin):
    even = lax.axis_index("row") % 2 == 0
    last = even if which == 0 else jnp.logical_not(even)
    return pl.multiple_of(jnp.where(last, n - margin, 0), 8)


def pack_kernel(margin, obj_hbm, offs_hbm, obj, offs, limits, *refs):
    evens, odds, rows, sems = refs[:2], refs[2], refs[3:-1], refs[-1]
    n = obj.shape[1]
    copies = copy_all(
        (obj_hbm.at[0:2], obj_hbm.at[2:4], offs_hbm), (obj.at[0:2], obj.at[2:4], offs), sems
    )
    even = lax.axis_index("col") % 2 == 0
    for s in range(2):
        copies[s].wait()
        low, high = pack_cols(obj[2 * s], obj[2 * s + 1])
        evens[s][...] = jnp.where(even, high, low)
        odds[s] = jnp.where(even, low, high)
    for which, out in enumerate(rows):
        out[...] = obj[:, pl.ds(row_start(which, n, margin), margin), :]
    copies[2].wait()
    for i in range(2):
        limits[i] = jnp.full(limits.shape[1:], offs[0, i] - margin, jnp.int32)


def corner_kernel(s, margin, e, o, after, *outs):
    for which, out in enumerate(outs):
        rows = pl.ds(row_start(which, e.shape[0], margin), margin)
        out[0] = e[rows, :]
        out[1] = o[s, rows, :]


def even_odd(n, axis):
    h = n // 2
    natural, sorted_ = iota((n, n), axis), iota((n, n), 1 - axis)
    source = jnp.where(sorted_ < h, 2 * sorted_, 2 * (sorted_ - h) + 1)
    return (natural == source).astype(F32).astype(BF16)


def reorder(x, order):
    def thirds(y):
        a = y.astype(BF16)
        return (a,) + split(y - a.astype(F32))

    a, b, c = thirds(x)
    a, b, c = thirds(dot(order[1], a) + (dot(order[1], b) + dot(order[1], c)))
    return dot(a, order[0]) + (dot(b, order[0]) + dot(c, order[0]))


def prep_kernel(*refs):
    hbm, (kr, ki, mats), loaded = refs[:6], refs[6:9], refs[9:13]
    phase, table, sems = refs[13:]
    n = phase.shape[0]
    h = n // 2
    first = pltpu.make_async_copy(hbm[0], phase, sems.at[0])
    first.start()
    order = [even_odd(n, axis) for axis in range(2)]
    first.wait()
    copies = copy_all(hbm[1:], (table,) + loaded, sems)
    angle = reorder(phase[...], order)
    kr[...], ki[...] = cos_sin(angle)
    copies[0].wait()
    for i in range(2):
        mats[i] = table[i]
        mats[2 + i, :h, :h] = table[i, :h, :h]
        mats[2 + i, :h, h:] = -table[i, :h, h:]
        mats[2 + i, h:, :h] = -table[i, h:, :h]
        mats[2 + i, h:, h:] = table[i, h:, h:]
    for copy in copies[1:]:
        copy.wait()


def reorder_kernel(x, after, out):
    out[...] = reorder(x[...], [even_odd(x.shape[0], axis) for axis in range(2)])


def roll_kernel(margin, offs, probe, pr):
    n = probe.shape[1]
    sy = (offs[0, 0] - margin + n) % n
    sx = (offs[0, 1] - margin + n) % n
    for i in range(2):
        pr[i] = dyn_roll(dyn_roll(probe[i], sy, 0), sx, 1)


def merge_cols(own, e, o, limits):
    n = own[0].shape[1]
    h = n // 2
    even = lax.axis_index("col") % 2 == 0
    high, low = jnp.where(even, e, o), jnp.where(even, o, e)
    lane = iota((1, h), 1)
    from_high = lane < limits[1, 0:1]
    from_low = lane >= limits[1, 0:1] + h
    out = []
    for i in range(2):
        strip_high = high if i == 0 else half_roll(high)
        strip_low = low if i == 0 else half_roll(low)
        out.append(
            cat(
                [
                    jnp.where(from_high, strip_high, own[i][:, :h]),
                    jnp.where(from_low, strip_low, own[i][:, h:]),
                ],
                1,
            )
        )
    return out


def merge_kernel(s, obj, e, o, limits, out):
    own = [obj[2 * s], obj[2 * s + 1]]
    out[0], out[1] = merge_cols(own, e[...], o[s], limits)


def window_of(main, s, halos, corners, limits, margin):
    n = main.shape[1]
    row_even = lax.axis_index("row") % 2 == 0
    blocks = []
    for halo, corner in zip(halos, corners):
        own = [halo[2 * s], halo[2 * s + 1]]
        blocks.append(merge_cols(own, corner[0], corner[1], limits))
    row = iota((margin, n), 0)
    limit = cat([limits[0, 0:1]] * 2, 1)
    take_high = row < limit
    take_low = row >= limit + margin
    out = []
    for i in range(2):
        e = blocks[0][i]
        o = blocks[1][i] if len(blocks) == 2 else jnp.zeros_like(e)
        high, low = jnp.where(row_even, e, o), jnp.where(row_even, o, e)
        out.append(
            cat(
                [
                    jnp.where(take_high, high, main[i, :margin]),
                    main[i, margin : n - margin],
                    jnp.where(take_low, low, main[i, n - margin :]),
                ],
                0,
            )
        )
    return out


def unpack(n_row, refs):
    return refs[0], refs[1 : 1 + n_row], refs[1 + n_row : 1 + 2 * n_row], refs[1 + 2 * n_row :]


def through(dft, x, re, im):
    return dft.right_inverse(product([re, im], dft.right(x)))


def arrive_kernel(n_row, margin, *refs):
    main, halos, corners, refs = unpack(n_row, refs)
    limits, pr, kr, ki, mats, twl, twr, w1, arrive = refs
    n = main.shape[1]
    dft = Dft(mats, twl[...], twr[...], n)
    win = window_of(main, 0, halos, corners, limits, margin)
    w1[0], w1[1] = win
    x = dft.left(product([pr[0], pr[1]], win))
    x = through(dft, x, kr[...], ki[...])
    arrive[0], arrive[1] = dft.left_inverse(x)


def back_kernel(n_row, margin, *refs):
    main, halos, corners, refs = unpack(n_row, refs)
    limits, offs_hbm, pr, kr, ki, am, w1, arrive, mats, twl, twr = refs[:11]
    keep, give, grads, offs, sem = refs[11:]
    scalars = pltpu.make_async_copy(offs_hbm, offs, sem)
    scalars.start()
    n = main.shape[1]
    dft = Dft(mats, twl[...], twr[...], n)
    win = window_of(main, 1, halos, corners, limits, margin)
    x = dft.left(product([arrive[0], arrive[1]], win))
    far = dft.right(x)
    modulus = jnp.sqrt(far[0] * far[0] + far[1] * far[1] + EPS_AMP)
    factor = 2.0 * (1.0 - am[...] / modulus)
    x = dft.right_inverse([factor * far[0], factor * far[1]])
    back_far = dft.left_inverse(x)
    grads[2], grads[3] = conj_product([arrive[0], arrive[1]], back_far)
    x = dft.left(conj_product(win, back_far))
    x = through(dft, x, kr[...], -ki[...])
    x = dft.left_inverse(x)
    grads[0], grads[1] = conj_product([pr[0], pr[1]], x)
    grad = conj_product([w1[0], w1[1]], x)
    scalars.wait()
    sy = (margin - offs[0, 0] + n) % n
    sx = (margin - offs[0, 1] + n) % n
    grad = [dyn_roll(dyn_roll(g, sy, 0), sx, 1) for g in grad]
    even = lax.axis_index("row") % 2 == 0
    keep[...] = jnp.where(even, grad[0], grad[1])
    give[...] = jnp.where(even, grad[1], grad[0])


def divide_kernel(margin, grads, limits, own, strip, *sends):
    for s in range(2):
        split_grad([grads[2 * s], grads[2 * s + 1]], s, limits, margin, own, strip, sends)


def split_grad(grad, s, limits, margin, own, strip, sends):
    n = grad[0].shape[0]
    h = n // 2
    row_even = lax.axis_index("row") % 2 == 0
    lane = iota((1, h), 1)
    to_high, to_low = lane < limits[1, 0:1], lane >= limits[1, 0:1] + h
    front = lane < h // 2
    spill = jnp.where(front, to_high.astype(jnp.int32), to_low.astype(jnp.int32)) != 0
    for i in range(2):
        g = grad[i]
        row = iota((n, h), 0)
        high_rows = row < limits[0, 0:1]
        low_rows = row >= limits[0, 0:1] + n
        inner = jnp.logical_not(jnp.logical_or(high_rows, low_rows))
        left = jnp.where(to_high, 0.0, g[:, :h])
        right = jnp.where(to_low, 0.0, g[:, h:])
        side = jnp.where(spill, jnp.where(front, g[:, :h], g[:, h:]), 0.0)
        pieces = [left, right, side]
        own[2 * s + i, :, :h] = jnp.where(inner, left, 0.0)
        own[2 * s + i, :, h:] = jnp.where(inner, right, 0.0)
        strip[2 * s + i] = jnp.where(inner, side, 0.0)
        for j, piece in enumerate(pieces):
            top = jnp.where(high_rows[:margin], piece[:margin], 0.0)
            bottom = jnp.where(low_rows[n - margin :], piece[n - margin :], 0.0)
            for which, send in enumerate(sends):
                first = row_even if which == 0 else jnp.logical_not(row_even)
                send[2 * s + i, :, j * h : (j + 1) * h] = jnp.where(first, top, bottom)


def fold_rows_kernel(n_row, margin, own, strip, *refs):
    got, (total, send_e, send_o) = refs[:n_row], refs[n_row:]
    row_even = lax.axis_index("row") % 2 == 0
    col_even = lax.axis_index("col") % 2 == 0
    n = own.shape[1]
    h = n // 2
    front = iota((n, h), 1) < h // 2
    for s in range(2):
        strips = []
        for i in range(2 * s, 2 * s + 2):
            total[i] = own[i]
            r = got[0][i]
            q = got[1][i] if n_row == 2 else jnp.zeros_like(r)
            top, bottom = jnp.where(row_even, q, r), jnp.where(row_even, r, q)
            total[i, :margin] += top[:, :n]
            total[i, n - margin :] += bottom[:, :n]
            st = strip[i]
            strips.append(
                cat(
                    [
                        st[:margin] + top[:, n:],
                        st[margin : n - margin],
                        st[n - margin :] + bottom[:, n:],
                    ],
                    0,
                )
            )
        moved = half_roll(strips[1])
        to_high = jnp.where(front, strips[0], moved)
        to_low = jnp.where(front, moved, strips[0])
        send_e[s] = jnp.where(col_even, to_high, to_low)
        send_o[s] = jnp.where(col_even, to_low, to_high)


def fold_cols_kernel(total, e, o, out):
    col_even = lax.axis_index("col") % 2 == 0
    n = total.shape[1]
    h = n // 2
    front = iota((n, h), 1) < h // 2
    for s in range(2):
        high = jnp.where(col_even, e[s], o[s])
        low = jnp.where(col_even, o[s], e[s])
        for i in range(2):
            a = low if i == 0 else half_roll(low)
            b = high if i == 0 else half_roll(high)
            at = 2 * s + i
            out[at, :, :h] = total[at, :, :h] + jnp.where(front, a, 0.0)
            out[at, :, h:] = total[at, :, h:] + jnp.where(front, 0.0, b)


def in_hbm(x):
    return pltpu.with_memory_space_constraint(x, pltpu.HBM)


def call(kernel, shapes, in_specs, *args, scratch=(), mib=16):
    shapes = [s if isinstance(s, jax.ShapeDtypeStruct) else jax.ShapeDtypeStruct(s, F32) for s in shapes]
    return pl.pallas_call(
        kernel,
        out_shape=shapes,
        in_specs=in_specs,
        out_specs=[SMEM if s.shape == (1, 2) else VMEM for s in shapes],
        scratch_shapes=list(scratch),
        compiler_params=pltpu.CompilerParams(vmem_limit_bytes=mib << 20),
    )(*args)


def edges(axis):
    count = lax.axis_size(axis)
    rounds = []
    for first in (0, 1):
        pairs = [(i, i + 1) for i in range(first, count - 1, 2)]
        pairs += [(b, a) for a, b in pairs]
        if pairs:
            rounds.append(pairs)
    return rounds


def swap(value, axis, distance):
    count = lax.axis_size(axis)
    return lax.ppermute(value, axis, [(i, i ^ distance) for i in range(count)])


def groups():
    cols = [("col", 1 << b) for b in range(lax.axis_size("col").bit_length() - 1)]
    rows = [("row", 1 << b) for b in range(1, lax.axis_size("row").bit_length() - 1)]
    first, rest = cols[:2], cols[2:]
    pairs = [first]
    for bits in (rest, rows):
        pairs += [bits[i : i + 2] for i in range(0, len(bits), 2)]
    out = []
    for pair in pairs:
        axis, masks = pair[0][0], [m for _, m in pair]
        out.append((axis, [0] + masks + ([sum(masks)] if len(masks) == 2 else [])))
    return out


def pair_sum(parts):
    while len(parts) > 1:
        parts = [parts[i] + parts[i + 1] for i in range(0, len(parts), 2)]
    return parts[0]


def share_kernel(quad, stride, keep, other, *parts):
    place = lax.axis_index("col") // stride % quad
    chunk = keep.shape[0] // quad
    for j, part in enumerate(parts):
        rows = pl.ds(pl.multiple_of((place ^ j) * chunk, 8), chunk)
        part[...] = keep[rows, :] + other[rows, :]


def sum_kernel(*refs):
    refs[-1][...] = pair_sum([r[...] for r in refs[:-1]])


def join_kernel(stride, *refs):
    parts, full = refs[:-1], refs[-1]
    quad, chunk = len(parts), parts[0].shape[0]
    place = lax.axis_index("col") // stride % quad
    for j, part in enumerate(parts):
        full[pl.ds(pl.multiple_of((place ^ j) * chunk, 8), chunk), :] = part[...]


def half_kernel(full, out, sem):
    copy = pltpu.make_async_copy(full, out.at[lax.axis_index("row") % 2], sem)
    copy.start()
    copy.wait()


def other_kernel(started, other, out, sem):
    copy = pltpu.make_async_copy(other, out.at[1 - lax.axis_index("row") % 2], sem)
    copy.start()
    copy.wait()


def reduce_probe(keep, give):
    n = keep.shape[0]
    (_, offsets), *rest = groups()
    quad, stride = len(offsets), offsets[1]
    chunk = n // quad
    other = swap(give, "row", 1)
    parts = call(
        functools.partial(share_kernel, quad, stride),
        [(chunk, n)] * quad,
        [VMEM] * 2,
        keep,
        other,
    )
    sums = [parts[0]]
    for j in range(1, quad):
        sums.append(swap(parts[j], "col", offsets[j]))
    (total,) = call(sum_kernel, [(chunk, n)], [VMEM] * quad, *sums)
    for axis, masks in rest:
        sums = [total]
        for mask in masks[1:]:
            sums.append(swap(total, axis, mask))
        (total,) = call(sum_kernel, [(chunk, n)], [VMEM] * len(sums), *sums)
    parts = [total]
    for j in range(1, quad):
        parts.append(swap(total, "col", offsets[j]))
    (full,) = call(
        functools.partial(join_kernel, stride), [(n, n)], [VMEM] * quad, *parts
    )
    other = swap(full, "row", 1)
    out = dict(
        out_shape=jax.ShapeDtypeStruct((2, n, n), F32),
        out_specs=HBM,
        scratch_shapes=[pltpu.SemaphoreType.DMA(())],
        compiler_params=pltpu.CompilerParams(vmem_limit_bytes=16 << 20),
    )
    grad = pl.pallas_call(half_kernel, in_specs=[VMEM], **out)(full)
    return pl.pallas_call(
        other_kernel, in_specs=[HBM, VMEM], input_output_aliases={0: 0}, **out
    )(grad, other)


def whole(object_field, probe, phase, amplitudes, offsets):
    tile = object_field.shape[2]
    n = probe.shape[1]
    h = n // 2
    margin = n // 4
    mats, tw_left, tw_right = [jnp.asarray(t) for t in dft_constants(n)]

    row_rounds, col_rounds = edges("row"), edges("col")
    n_row = len(row_rounds)
    obj, offs, limits, even0, even1, odds, *rows = call(
        functools.partial(pack_kernel, margin),
        [(4, n, n), jax.ShapeDtypeStruct((1, 2), jnp.int32)]
        + [jax.ShapeDtypeStruct((2, 8, h), jnp.int32)]
        + [(n, h), (n, h), (2, n, h)]
        + [(4, margin, n)] * n_row,
        [HBM, HBM],
        in_hbm(object_field.reshape(4, tile, tile)),
        in_hbm(offsets.reshape(1, 2)),
        scratch=[pltpu.SemaphoreType.DMA((3,))],
    )
    halos, corners = [], [[], []]
    even0 = lax.ppermute(even0, "col", col_rounds[0])
    odds = lax.ppermute(odds, "col", col_rounds[1])
    even1 = lax.ppermute(even1, "col", col_rounds[0])
    for i, pairs in enumerate(row_rounds):
        halos.append(lax.ppermute(rows[i], "row", pairs))
    evens = (even0, even1)

    def cut(s, after):
        parts = call(
            functools.partial(corner_kernel, s, margin),
            [(2, margin, h)] * n_row,
            [VMEM] * 3,
            evens[s],
            odds,
            after,
        )
        for i, pairs in enumerate(row_rounds):
            corners[s].append(lax.ppermute(parts[i], "row", pairs))

    def merge(s):
        (main,) = call(
            functools.partial(merge_kernel, s),
            [(2, n, n)],
            [VMEM] * 4,
            obj,
            evens[s],
            odds,
            limits,
        )
        return main

    loads = (phase, mats, tw_left, tw_right, probe, amplitudes.reshape(n, n))
    kr, ki, mats, tw_left, tw_right, pr, am = call(
        prep_kernel,
        [(n, n)] * 2
        + [jax.ShapeDtypeStruct((4, n, n), BF16)]
        + [jax.ShapeDtypeStruct(x.shape, x.dtype) for x in loads[2:]],
        [HBM] * len(loads),
        *[in_hbm(x) for x in loads],
        scratch=[
            pltpu.VMEM((n, n), F32),
            pltpu.VMEM((2, n, n), BF16),
            pltpu.SemaphoreType.DMA((len(loads),)),
        ],
    )
    (pr,) = call(functools.partial(roll_kernel, margin), [(2, n, n)], [SMEM, VMEM], offs, pr)
    (am,) = call(reorder_kernel, [(n, n)], [VMEM] * 2, am, pr)
    cut(0, am)
    main = merge(0)
    cut(1, main)
    w1, arrive = call(
        functools.partial(arrive_kernel, n_row, margin),
        [(2, n, n), (2, n, n)],
        [VMEM] * (8 + 2 * n_row),
        main,
        *halos,
        *corners[0],
        limits,
        pr,
        kr,
        ki,
        mats,
        tw_left,
        tw_right,
    )
    main = merge(1)
    keep, give, grads = call(
        functools.partial(back_kernel, n_row, margin),
        [(n, n), (n, n), (4, n, n)],
        [VMEM] * (2 + 2 * n_row) + [HBM] + [VMEM] * 9,
        main,
        *halos,
        *corners[1],
        limits,
        in_hbm(offsets.reshape(1, 2)),
        pr,
        kr,
        ki,
        am,
        w1,
        arrive,
        mats,
        tw_left,
        tw_right,
        scratch=[pltpu.SMEM((1, 2), jnp.int32), pltpu.SemaphoreType.DMA(())],
        mib=40,
    )
    probe_grad = reduce_probe(keep, give)
    own, strip, *sends = call(
        functools.partial(divide_kernel, margin),
        [(4, n, n), (4, n, h)] + [(4, margin, n + h)] * n_row,
        [VMEM, VMEM],
        grads,
        limits,
    )
    got = []
    for i, pairs in enumerate(row_rounds):
        got.append(lax.ppermute(sends[i], "row", pairs))
    total, send_e, send_o = call(
        functools.partial(fold_rows_kernel, n_row, margin),
        [(4, n, n), (2, n, h), (2, n, h)],
        [VMEM] * (2 + n_row),
        own,
        strip,
        *got,
    )
    send_e = lax.ppermute(send_e, "col", col_rounds[0])
    send_o = lax.ppermute(send_o, "col", col_rounds[1])
    (grad,) = call(fold_cols_kernel, [(4, n, n)], [VMEM] * 3, total, send_e, send_o)
    return (grad.reshape(2, 2, tile, tile), probe_grad)


def solution(mesh):
    placed = (
        P(None, None, "row", "col"),
        P(),
        P(),
        P("row", "col", None, None, None),
        P("row", "col", None, None),
    )
    return jax.shard_map(
        whole,
        mesh=mesh,
        in_specs=placed,
        out_specs=(P(None, None, "row", "col"), P()),
        check_vma=False,
    )
```

```python
import functools
import math

import jax
import jax.numpy as jnp
import numpy as np
from jax import lax
from jax.experimental import pallas as pl
from jax.experimental.pallas import tpu as pltpu
from jax.sharding import PartitionSpec as P


EPS_AMP = 0.5
F32 = jnp.float32
BF16 = jnp.bfloat16
VMEM = pl.BlockSpec(memory_space=pltpu.VMEM)
SMEM = pl.BlockSpec(memory_space=pltpu.SMEM)
HBM = pl.BlockSpec(memory_space=pltpu.HBM)


def split_np(table):
    high = table.astype(BF16)
    low = (table - high.astype(np.float64)).astype(BF16)
    return [high, low]


def dft_constants(n):
    h = n // 2
    k = np.arange(h)
    angle = 2.0 * np.pi * ((k[:, None] * k[None, :]) % h) / h
    scale = 1.0 / np.sqrt(n)
    c, s = np.cos(angle) * scale, np.sin(angle) * scale
    d = np.block([[c, s], [-s, c]])
    mats = np.stack(split_np(d))
    w = np.exp(-2j * np.pi * k / n)
    tw_left = np.stack([np.tile(w.real[:, None], (1, h)), np.tile(w.imag[:, None], (1, h))])
    tw_right = np.stack([np.tile(w.real[None], (8, 1)), np.tile(w.imag[None], (8, 1))])
    return mats, tw_left.astype(np.float32), tw_right.astype(np.float32)


def split(x):
    high = x.astype(BF16)
    return high, (x - high.astype(F32)).astype(BF16)


def dot(a, b):
    return jnp.dot(a, b, preferred_element_type=F32)


def left_dot(mats, which, x):
    high, low = split(x)
    return dot(mats[which], high) + (dot(mats[which], low) + dot(mats[which + 1], high))


def right_dot(x, mats, which):
    high, low = split(x)
    return dot(high, mats[which]) + (dot(low, mats[which]) + dot(high, mats[which + 1]))


def cat(parts, axis):
    return jnp.concatenate(parts, axis=axis)


def product(a, b):
    return (a[0] * b[0] - a[1] * b[1], a[0] * b[1] + a[1] * b[0])


def conj_product(a, b):
    return (a[0] * b[0] + a[1] * b[1], a[0] * b[1] - a[1] * b[0])


class Dft:
    def __init__(self, mats, tw_left, tw_right, n):
        self.mats, self.n, self.h = mats, n, n // 2
        self.tw_left, self.tw_right = tw_left, tw_right

    def wl(self, width):
        parts = width // self.tw_left.shape[2]
        return [cat([self.tw_left[i]] * parts, 1) for i in range(2)]

    def wr(self):
        return [self.tw_right[i, 0:1] for i in range(2)]

    def left(self, x):
        h, w = self.h, x[0].shape[1]
        total = [p[:h] + p[h:] for p in x]
        odd = product([p[:h] - p[h:] for p in x], self.wl(w))
        u = left_dot(self.mats, 0, cat(total, 0))
        v = left_dot(self.mats, 0, cat(odd, 0))
        return [cat([u[:h], v[:h]], 0), cat([u[h:], v[h:]], 0)]

    def right(self, x):
        h, m = self.h, x[0].shape[0]
        total = [p[:, :h] + p[:, h:] for p in x]
        odd = product([p[:, :h] - p[:, h:] for p in x], self.wr())
        u = right_dot(cat(total, 1), self.mats, 2)
        v = right_dot(cat(odd, 1), self.mats, 2)
        return [cat([u[:, :h], v[:, :h]], 1), cat([u[:, h:], v[:, h:]], 1)]

    def right_inverse(self, x):
        h, m = self.h, x[0].shape[0]
        u = right_dot(cat([p[:, :h] for p in x], 1), self.mats, 0)
        v = right_dot(cat([p[:, h:] for p in x], 1), self.mats, 0)
        even = [u[:, :h], u[:, h:]]
        odd = conj_product(self.wr(), [v[:, :h], v[:, h:]])
        return [cat([e + o, e - o], 1) for e, o in zip(even, odd)]

    def left_inverse(self, x):
        h, w = self.h, x[0].shape[1]
        u = left_dot(self.mats, 2, cat([p[:h] for p in x], 0))
        v = left_dot(self.mats, 2, cat([p[h:] for p in x], 0))
        even = [u[:h], u[h:]]
        odd = conj_product(self.wl(w), [v[:h], v[h:]])
        return [cat([e + o, e - o], 0) for e, o in zip(even, odd)]


SIN = [(-1.0) ** i / math.factorial(2 * i + 1) for i in range(7)]
COS = [(-1.0) ** i / math.factorial(2 * i) for i in range(7)]


def series(coefficients, z):
    total = coefficients[-1]
    for c in coefficients[-2::-1]:
        total = total * z + c
    return total


def cos_sin(x):
    y = 0.5 * x
    z = y * y
    s, c = y * series(SIN, z), series(COS, z)
    return 1.0 - 2.0 * (s * s), 2.0 * (s * c)


def iota(shape, dim):
    return lax.broadcasted_iota(jnp.int32, shape, dim)


def dyn_roll(x, shift, axis):
    return pltpu.roll(x, shift, axis=axis)


def half_roll(x):
    return pltpu.roll(x, x.shape[-1] // 2, axis=x.ndim - 1)


def pack_cols(re, im):
    h = re.shape[1] // 2
    front = iota((re.shape[0], h), 1) < h // 2
    low = jnp.where(front, re[:, :h], half_roll(im[:, :h]))
    high = jnp.where(front, half_roll(im[:, h:]), re[:, h:])
    return low, high


def copy_all(sources, places, sems):
    copies = [
        pltpu.make_async_copy(a, b, sems.at[i]) for i, (a, b) in enumerate(zip(sources, places))
    ]
    for copy in copies:
        copy.start()
    return copies


def row_start(which, n, margin):
    even = lax.axis_index("row") % 2 == 0
    last = even if which == 0 else jnp.logical_not(even)
    return pl.multiple_of(jnp.where(last, n - margin, 0), 8)


def pack_kernel(margin, obj_hbm, offs_hbm, obj, offs, limits, *refs):
    evens, odds, rows, sems = refs[:2], refs[2:4], refs[4:-1], refs[-1]
    n = obj.shape[1]
    copies = copy_all(
        (obj_hbm.at[0:2], obj_hbm.at[2:4], offs_hbm), (obj.at[0:2], obj.at[2:4], offs), sems
    )
    even = lax.axis_index("col") % 2 == 0
    for s in range(2):
        copies[s].wait()
        low, high = pack_cols(obj[2 * s], obj[2 * s + 1])
        evens[s][...] = jnp.where(even, high, low)
        odds[s][...] = jnp.where(even, low, high)
    for which, out in enumerate(rows):
        out[...] = obj[:, pl.ds(row_start(which, n, margin), margin), :]
    copies[2].wait()
    for i in range(2):
        limits[i] = jnp.full(limits.shape[1:], offs[0, i] - margin, jnp.int32)


def corner_kernel(margin, e, o, after, *outs):
    for which, out in enumerate(outs):
        rows = pl.ds(row_start(which, e.shape[0], margin), margin)
        out[0] = e[rows, :]
        out[1] = o[rows, :]


def even_odd(n, axis):
    h = n // 2
    natural, sorted_ = iota((n, n), axis), iota((n, n), 1 - axis)
    source = jnp.where(sorted_ < h, 2 * sorted_, 2 * (sorted_ - h) + 1)
    return (natural == source).astype(F32).astype(BF16)


def reorder(x, order):
    def thirds(y):
        a = y.astype(BF16)
        return (a,) + split(y - a.astype(F32))

    a, b, c = thirds(x)
    a, b, c = thirds(dot(order[1], a) + (dot(order[1], b) + dot(order[1], c)))
    return dot(a, order[0]) + (dot(b, order[0]) + dot(c, order[0]))


def prep_kernel(*refs):
    hbm, (kr, ki, mats), loaded = refs[:6], refs[6:9], refs[9:13]
    phase, table, sems = refs[13:]
    n = phase.shape[0]
    h = n // 2
    phase = hbm[0]
    copies = copy_all(hbm[1:], (table,) + loaded, sems)
    order = [even_odd(n, axis) for axis in range(2)]
    angle = reorder(phase[...], order)
    kr[...], ki[...] = cos_sin(angle)
    copies[0].wait()
    for i in range(2):
        mats[i] = table[i]
        mats[2 + i, :h, :h] = table[i, :h, :h]
        mats[2 + i, :h, h:] = -table[i, :h, h:]
        mats[2 + i, h:, :h] = -table[i, h:, :h]
        mats[2 + i, h:, h:] = table[i, h:, h:]
    for copy in copies[1:]:
        copy.wait()


def reorder_kernel(x, after, out):
    out[...] = reorder(x[...], [even_odd(x.shape[0], axis) for axis in range(2)])


def roll_kernel(margin, offs, probe, pr):
    n = probe.shape[1]
    sy = (offs[0, 0] - margin + n) % n
    sx = (offs[0, 1] - margin + n) % n
    for i in range(2):
        pr[i] = dyn_roll(dyn_roll(probe[i], sy, 0), sx, 1)


def merge_cols(own, e, o, limits):
    n = own[0].shape[1]
    h = n // 2
    even = lax.axis_index("col") % 2 == 0
    high, low = jnp.where(even, e, o), jnp.where(even, o, e)
    lane = iota((1, h), 1)
    from_high = lane < limits[1, 0:1]
    from_low = lane >= limits[1, 0:1] + h
    out = []
    for i in range(2):
        strip_high = high if i == 0 else half_roll(high)
        strip_low = low if i == 0 else half_roll(low)
        out.append(
            cat(
                [
                    jnp.where(from_high, strip_high, own[i][:, :h]),
                    jnp.where(from_low, strip_low, own[i][:, h:]),
                ],
                1,
            )
        )
    return out


def merge_kernel(s, obj, e, o, limits, out):
    own = [obj[2 * s], obj[2 * s + 1]]
    out[0], out[1] = merge_cols(own, e[...], o[...], limits)


def window_of(main, s, halos, corners, limits, margin):
    n = main.shape[1]
    row_even = lax.axis_index("row") % 2 == 0
    blocks = []
    for halo, corner in zip(halos, corners):
        own = [halo[2 * s], halo[2 * s + 1]]
        blocks.append(merge_cols(own, corner[0], corner[1], limits))
    row = iota((margin, n), 0)
    limit = cat([limits[0, 0:1]] * 2, 1)
    take_high = row < limit
    take_low = row >= limit + margin
    out = []
    for i in range(2):
        e = blocks[0][i]
        o = blocks[1][i] if len(blocks) == 2 else jnp.zeros_like(e)
        high, low = jnp.where(row_even, e, o), jnp.where(row_even, o, e)
        out.append(
            cat(
                [
                    jnp.where(take_high, high, main[i, :margin]),
                    main[i, margin : n - margin],
                    jnp.where(take_low, low, main[i, n - margin :]),
                ],
                0,
            )
        )
    return out


def unpack(n_row, refs):
    return refs[0], refs[1 : 1 + n_row], refs[1 + n_row : 1 + 2 * n_row], refs[1 + 2 * n_row :]


def through(dft, x, re, im):
    return dft.right_inverse(product([re, im], dft.right(x)))


def arrive_kernel(n_row, margin, *refs):
    main, halos, corners, refs = unpack(n_row, refs)
    limits, pr, kr, ki, mats, twl, twr, w1, arrive = refs
    n = main.shape[1]
    dft = Dft(mats, twl[...], twr[...], n)
    win = window_of(main, 0, halos, corners, limits, margin)
    w1[0], w1[1] = win
    x = dft.left(product([pr[0], pr[1]], win))
    x = through(dft, x, kr[...], ki[...])
    arrive[0], arrive[1] = dft.left_inverse(x)


def back_kernel(n_row, margin, *refs):
    main, halos, corners, refs = unpack(n_row, refs)
    limits, offs_hbm, pr, kr, ki, am, w1, arrive, mats, twl, twr = refs[:11]
    keep, give, grads, offs, sem = refs[11:]
    scalars = pltpu.make_async_copy(offs_hbm, offs, sem)
    scalars.start()
    n = main.shape[1]
    dft = Dft(mats, twl[...], twr[...], n)
    win = window_of(main, 1, halos, corners, limits, margin)
    x = dft.left(product([arrive[0], arrive[1]], win))
    far = dft.right(x)
    modulus = jnp.sqrt(far[0] * far[0] + far[1] * far[1] + EPS_AMP)
    factor = 2.0 * (1.0 - am[...] / modulus)
    x = dft.right_inverse([factor * far[0], factor * far[1]])
    back_far = dft.left_inverse(x)
    grads[2], grads[3] = conj_product([arrive[0], arrive[1]], back_far)
    x = dft.left(conj_product(win, back_far))
    x = through(dft, x, kr[...], -ki[...])
    x = dft.left_inverse(x)
    grads[0], grads[1] = conj_product([pr[0], pr[1]], x)
    grad = conj_product([w1[0], w1[1]], x)
    scalars.wait()
    sy = (margin - offs[0, 0] + n) % n
    sx = (margin - offs[0, 1] + n) % n
    grad = [dyn_roll(dyn_roll(g, sy, 0), sx, 1) for g in grad]
    even = lax.axis_index("row") % 2 == 0
    keep[...] = jnp.where(even, grad[0], grad[1])
    give[...] = jnp.where(even, grad[1], grad[0])


def divide_kernel(margin, grads, limits, own, strip, *sends):
    for s in range(2):
        split_grad([grads[2 * s], grads[2 * s + 1]], s, limits, margin, own, strip, sends)


def split_grad(grad, s, limits, margin, own, strip, sends):
    n = grad[0].shape[0]
    h = n // 2
    row_even = lax.axis_index("row") % 2 == 0
    lane = iota((1, h), 1)
    to_high, to_low = lane < limits[1, 0:1], lane >= limits[1, 0:1] + h
    front = lane < h // 2
    spill = jnp.where(front, to_high.astype(jnp.int32), to_low.astype(jnp.int32)) != 0
    for i in range(2):
        g = grad[i]
        row = iota((n, h), 0)
        high_rows = row < limits[0, 0:1]
        low_rows = row >= limits[0, 0:1] + n
        inner = jnp.logical_not(jnp.logical_or(high_rows, low_rows))
        left = jnp.where(to_high, 0.0, g[:, :h])
        right = jnp.where(to_low, 0.0, g[:, h:])
        side = jnp.where(spill, jnp.where(front, g[:, :h], g[:, h:]), 0.0)
        pieces = [left, right, side]
        own[2 * s + i, :, :h] = jnp.where(inner, left, 0.0)
        own[2 * s + i, :, h:] = jnp.where(inner, right, 0.0)
        strip[2 * s + i] = jnp.where(inner, side, 0.0)
        for j, piece in enumerate(pieces):
            top = jnp.where(high_rows[:margin], piece[:margin], 0.0)
            bottom = jnp.where(low_rows[n - margin :], piece[n - margin :], 0.0)
            for which, send in enumerate(sends):
                first = row_even if which == 0 else jnp.logical_not(row_even)
                send[2 * s + i, :, j * h : (j + 1) * h] = jnp.where(first, top, bottom)


def fold_rows_kernel(n_row, margin, own, strip, *refs):
    got, (total, send_e, send_o) = refs[:n_row], refs[n_row:]
    row_even = lax.axis_index("row") % 2 == 0
    col_even = lax.axis_index("col") % 2 == 0
    n = own.shape[1]
    h = n // 2
    front = iota((n, h), 1) < h // 2
    for s in range(2):
        strips = []
        for i in range(2 * s, 2 * s + 2):
            total[i] = own[i]
            r = got[0][i]
            q = got[1][i] if n_row == 2 else jnp.zeros_like(r)
            top, bottom = jnp.where(row_even, q, r), jnp.where(row_even, r, q)
            total[i, :margin] += top[:, :n]
            total[i, n - margin :] += bottom[:, :n]
            st = strip[i]
            strips.append(
                cat(
                    [
                        st[:margin] + top[:, n:],
                        st[margin : n - margin],
                        st[n - margin :] + bottom[:, n:],
                    ],
                    0,
                )
            )
        moved = half_roll(strips[1])
        to_high = jnp.where(front, strips[0], moved)
        to_low = jnp.where(front, moved, strips[0])
        send_e[s] = jnp.where(col_even, to_high, to_low)
        send_o[s] = jnp.where(col_even, to_low, to_high)


def fold_cols_kernel(total, e, o, out):
    col_even = lax.axis_index("col") % 2 == 0
    n = total.shape[1]
    h = n // 2
    front = iota((n, h), 1) < h // 2
    for s in range(2):
        high = jnp.where(col_even, e[s], o[s])
        low = jnp.where(col_even, o[s], e[s])
        for i in range(2):
            a = low if i == 0 else half_roll(low)
            b = high if i == 0 else half_roll(high)
            at = 2 * s + i
            out[at, :, :h] = total[at, :, :h] + jnp.where(front, a, 0.0)
            out[at, :, h:] = total[at, :, h:] + jnp.where(front, 0.0, b)


def in_hbm(x):
    return pltpu.with_memory_space_constraint(x, pltpu.HBM)


def call(kernel, shapes, in_specs, *args, scratch=(), mib=16):
    shapes = [s if isinstance(s, jax.ShapeDtypeStruct) else jax.ShapeDtypeStruct(s, F32) for s in shapes]
    return pl.pallas_call(
        kernel,
        out_shape=shapes,
        in_specs=in_specs,
        out_specs=[SMEM if s.shape == (1, 2) else VMEM for s in shapes],
        scratch_shapes=list(scratch),
        compiler_params=pltpu.CompilerParams(vmem_limit_bytes=mib << 20),
    )(*args)


def edges(axis):
    count = lax.axis_size(axis)
    rounds = []
    for first in (0, 1):
        pairs = [(i, i + 1) for i in range(first, count - 1, 2)]
        pairs += [(b, a) for a, b in pairs]
        if pairs:
            rounds.append(pairs)
    return rounds


def swap(value, axis, distance):
    count = lax.axis_size(axis)
    return lax.ppermute(value, axis, [(i, i ^ distance) for i in range(count)])


def groups():
    cols = [("col", 1 << b) for b in range(lax.axis_size("col").bit_length() - 1)]
    rows = [("row", 1 << b) for b in range(1, lax.axis_size("row").bit_length() - 1)]
    first, rest = cols[:2], cols[2:]
    pairs = [first]
    for bits in (rest, rows):
        pairs += [bits[i : i + 2] for i in range(0, len(bits), 2)]
    out = []
    for pair in pairs:
        axis, masks = pair[0][0], [m for _, m in pair]
        out.append((axis, [0] + masks + ([sum(masks)] if len(masks) == 2 else [])))
    return out


def pair_sum(parts):
    while len(parts) > 1:
        parts = [parts[i] + parts[i + 1] for i in range(0, len(parts), 2)]
    return parts[0]


def share_kernel(quad, stride, keep, other, *parts):
    place = lax.axis_index("col") // stride % quad
    chunk = keep.shape[0] // quad
    for j, part in enumerate(parts):
        rows = pl.ds(pl.multiple_of((place ^ j) * chunk, 8), chunk)
        part[...] = keep[rows, :] + other[rows, :]


def sum_kernel(*refs):
    refs[-1][...] = pair_sum([r[...] for r in refs[:-1]])


def join_kernel(stride, *refs):
    parts, full = refs[:-1], refs[-1]
    quad, chunk = len(parts), parts[0].shape[0]
    place = lax.axis_index("col") // stride % quad
    for j, part in enumerate(parts):
        full[pl.ds(pl.multiple_of((place ^ j) * chunk, 8), chunk), :] = part[...]


def half_kernel(full, out, sem):
    copy = pltpu.make_async_copy(full, out.at[lax.axis_index("row") % 2], sem)
    copy.start()
    copy.wait()


def other_kernel(started, other, out, sem):
    copy = pltpu.make_async_copy(other, out.at[1 - lax.axis_index("row") % 2], sem)
    copy.start()
    copy.wait()


def reduce_probe(keep, give):
    n = keep.shape[0]
    (_, offsets), *rest = groups()
    quad, stride = len(offsets), offsets[1]
    chunk = n // quad
    other = swap(give, "row", 1)
    parts = call(
        functools.partial(share_kernel, quad, stride),
        [(chunk, n)] * quad,
        [VMEM] * 2,
        keep,
        other,
    )
    sums = [parts[0]]
    for j in range(1, quad):
        sums.append(swap(parts[j], "col", offsets[j]))
    (total,) = call(sum_kernel, [(chunk, n)], [VMEM] * quad, *sums)
    for axis, masks in rest:
        sums = [total]
        for mask in masks[1:]:
            sums.append(swap(total, axis, mask))
        (total,) = call(sum_kernel, [(chunk, n)], [VMEM] * len(sums), *sums)
    parts = [total]
    for j in range(1, quad):
        parts.append(swap(total, "col", offsets[j]))
    (full,) = call(
        functools.partial(join_kernel, stride), [(n, n)], [VMEM] * quad, *parts
    )
    other = swap(full, "row", 1)
    out = dict(
        out_shape=jax.ShapeDtypeStruct((2, n, n), F32),
        out_specs=HBM,
        scratch_shapes=[pltpu.SemaphoreType.DMA(())],
        compiler_params=pltpu.CompilerParams(vmem_limit_bytes=16 << 20),
    )
    grad = pl.pallas_call(half_kernel, in_specs=[VMEM], **out)(full)
    return pl.pallas_call(
        other_kernel, in_specs=[HBM, VMEM], input_output_aliases={0: 0}, **out
    )(grad, other)


def whole(object_field, probe, phase, amplitudes, offsets):
    tile = object_field.shape[2]
    n = probe.shape[1]
    h = n // 2
    margin = n // 4
    mats, tw_left, tw_right = [jnp.asarray(t) for t in dft_constants(n)]

    row_rounds, col_rounds = edges("row"), edges("col")
    n_row = len(row_rounds)
    obj, offs, limits, even0, even1, odd0, odd1, *rows = call(
        functools.partial(pack_kernel, margin),
        [(4, n, n), jax.ShapeDtypeStruct((1, 2), jnp.int32)]
        + [jax.ShapeDtypeStruct((2, 8, h), jnp.int32)]
        + [(n, h)] * 4
        + [(4, margin, n)] * n_row,
        [HBM, HBM],
        in_hbm(object_field.reshape(4, tile, tile)),
        in_hbm(offsets.reshape(1, 2)),
        scratch=[pltpu.SemaphoreType.DMA((3,))],
    )
    halos, corners = [], [[], []]
    even0 = lax.ppermute(even0, "col", col_rounds[0])
    even1 = lax.ppermute(even1, "col", col_rounds[0])
    odd0 = lax.ppermute(odd0, "col", col_rounds[1])
    odd1 = lax.ppermute(odd1, "col", col_rounds[1])
    for i, pairs in enumerate(row_rounds):
        halos.append(lax.ppermute(rows[i], "row", pairs))
    evens, odds = (even0, even1), (odd0, odd1)

    def cut(s, after):
        parts = call(
            functools.partial(corner_kernel, margin),
            [(2, margin, h)] * n_row,
            [VMEM] * 3,
            evens[s],
            odds[s],
            after,
        )
        for i, pairs in enumerate(row_rounds):
            corners[s].append(lax.ppermute(parts[i], "row", pairs))

    def merge(s):
        (main,) = call(
            functools.partial(merge_kernel, s),
            [(2, n, n)],
            [VMEM] * 4,
            obj,
            evens[s],
            odds[s],
            limits,
        )
        return main

    loads = (phase, mats, tw_left, tw_right, probe, amplitudes.reshape(n, n))
    kr, ki, mats, tw_left, tw_right, pr, am = call(
        prep_kernel,
        [(n, n)] * 2
        + [jax.ShapeDtypeStruct((4, n, n), BF16)]
        + [jax.ShapeDtypeStruct(x.shape, x.dtype) for x in loads[2:]],
        [VMEM] + [HBM] * (len(loads) - 1),
        loads[0],
        *[in_hbm(x) for x in loads[1:]],
        scratch=[
            pltpu.VMEM((n, n), F32),
            pltpu.VMEM((2, n, n), BF16),
            pltpu.SemaphoreType.DMA((len(loads),)),
        ],
    )
    cut(0, kr)
    (pr,) = call(functools.partial(roll_kernel, margin), [(2, n, n)], [SMEM, VMEM], offs, pr)
    main = merge(0)
    w1, arrive = call(
        functools.partial(arrive_kernel, n_row, margin),
        [(2, n, n), (2, n, n)],
        [VMEM] * (8 + 2 * n_row),
        main,
        *halos,
        *corners[0],
        limits,
        pr,
        kr,
        ki,
        mats,
        tw_left,
        tw_right,
    )
    cut(1, arrive)
    (am,) = call(reorder_kernel, [(n, n)], [VMEM] * 2, am, arrive)
    main = merge(1)
    keep, give, grads = call(
        functools.partial(back_kernel, n_row, margin),
        [(n, n), (n, n), (4, n, n)],
        [VMEM] * (2 + 2 * n_row) + [HBM] + [VMEM] * 9,
        main,
        *halos,
        *corners[1],
        limits,
        in_hbm(offsets.reshape(1, 2)),
        pr,
        kr,
        ki,
        am,
        w1,
        arrive,
        mats,
        tw_left,
        tw_right,
        scratch=[pltpu.SMEM((1, 2), jnp.int32), pltpu.SemaphoreType.DMA(())],
        mib=40,
    )
    probe_grad = reduce_probe(keep, give)
    own, strip, *sends = call(
        functools.partial(divide_kernel, margin),
        [(4, n, n), (4, n, h)] + [(4, margin, n + h)] * n_row,
        [VMEM, VMEM],
        grads,
        limits,
    )
    got = []
    for i, pairs in enumerate(row_rounds):
        got.append(lax.ppermute(sends[i], "row", pairs))
    total, send_e, send_o = call(
        functools.partial(fold_rows_kernel, n_row, margin),
        [(4, n, n), (2, n, h), (2, n, h)],
        [VMEM] * (2 + n_row),
        own,
        strip,
        *got,
    )
    send_e = lax.ppermute(send_e, "col", col_rounds[0])
    send_o = lax.ppermute(send_o, "col", col_rounds[1])
    (grad,) = call(fold_cols_kernel, [(4, n, n)], [VMEM] * 3, total, send_e, send_o)
    return (grad.reshape(2, 2, tile, tile), probe_grad)


def solution(mesh):
    placed = (
        P(None, None, "row", "col"),
        P(),
        P(),
        P("row", "col", None, None, None),
        P("row", "col", None, None),
    )
    return jax.shard_map(
        whole,
        mesh=mesh,
        in_specs=placed,
        out_specs=(P(None, None, "row", "col"), P()),
        check_vma=False,
    )
```

```python
import functools
import math

import jax
import jax.numpy as jnp
import numpy as np
from jax import lax
from jax.experimental import pallas as pl
from jax.experimental.pallas import tpu as pltpu
from jax.sharding import PartitionSpec as P


EPS_AMP = 0.5
F32 = jnp.float32
BF16 = jnp.bfloat16
VMEM = pl.BlockSpec(memory_space=pltpu.VMEM)
SMEM = pl.BlockSpec(memory_space=pltpu.SMEM)
HBM = pl.BlockSpec(memory_space=pltpu.HBM)


def split_np(table):
    high = table.astype(BF16)
    low = (table - high.astype(np.float64)).astype(BF16)
    return [high, low]


def dft_constants(n):
    h = n // 2
    k = np.arange(h)
    angle = 2.0 * np.pi * ((k[:, None] * k[None, :]) % h) / h
    scale = 1.0 / np.sqrt(n)
    c, s = np.cos(angle) * scale, np.sin(angle) * scale
    d = np.block([[c, s], [-s, c]])
    mats = np.stack(split_np(d))
    w = np.exp(-2j * np.pi * k / n)
    tw_left = np.stack([np.tile(w.real[:, None], (1, h)), np.tile(w.imag[:, None], (1, h))])
    tw_right = np.stack([np.tile(w.real[None], (8, 1)), np.tile(w.imag[None], (8, 1))])
    return mats, tw_left.astype(np.float32), tw_right.astype(np.float32)


def split(x):
    high = x.astype(BF16)
    return high, (x - high.astype(F32)).astype(BF16)


def dot(a, b):
    return jnp.dot(a, b, preferred_element_type=F32)


def left_dot(mats, which, x):
    high, low = split(x)
    return dot(mats[which], high) + (dot(mats[which], low) + dot(mats[which + 1], high))


def right_dot(x, mats, which):
    high, low = split(x)
    return dot(high, mats[which]) + (dot(low, mats[which]) + dot(high, mats[which + 1]))


def cat(parts, axis):
    return jnp.concatenate(parts, axis=axis)


def product(a, b):
    return (a[0] * b[0] - a[1] * b[1], a[0] * b[1] + a[1] * b[0])


def conj_product(a, b):
    return (a[0] * b[0] + a[1] * b[1], a[0] * b[1] - a[1] * b[0])


class Dft:
    def __init__(self, mats, tw_left, tw_right, n):
        self.mats, self.n, self.h = mats, n, n // 2
        self.tw_left, self.tw_right = tw_left, tw_right

    def wl(self, width):
        parts = width // self.tw_left.shape[2]
        return [cat([self.tw_left[i]] * parts, 1) for i in range(2)]

    def wr(self):
        return [self.tw_right[i, 0:1] for i in range(2)]

    def left(self, x):
        h, w = self.h, x[0].shape[1]
        total = [p[:h] + p[h:] for p in x]
        odd = product([p[:h] - p[h:] for p in x], self.wl(w))
        u = left_dot(self.mats, 0, cat(total, 0))
        v = left_dot(self.mats, 0, cat(odd, 0))
        return [cat([u[:h], v[:h]], 0), cat([u[h:], v[h:]], 0)]

    def right(self, x):
        h, m = self.h, x[0].shape[0]
        total = [p[:, :h] + p[:, h:] for p in x]
        odd = product([p[:, :h] - p[:, h:] for p in x], self.wr())
        u = right_dot(cat(total, 1), self.mats, 2)
        v = right_dot(cat(odd, 1), self.mats, 2)
        return [cat([u[:, :h], v[:, :h]], 1), cat([u[:, h:], v[:, h:]], 1)]

    def right_inverse(self, x):
        h, m = self.h, x[0].shape[0]
        u = right_dot(cat([p[:, :h] for p in x], 1), self.mats, 0)
        v = right_dot(cat([p[:, h:] for p in x], 1), self.mats, 0)
        even = [u[:, :h], u[:, h:]]
        odd = conj_product(self.wr(), [v[:, :h], v[:, h:]])
        return [cat([e + o, e - o], 1) for e, o in zip(even, odd)]

    def left_inverse(self, x):
        h, w = self.h, x[0].shape[1]
        u = left_dot(self.mats, 2, cat([p[:h] for p in x], 0))
        v = left_dot(self.mats, 2, cat([p[h:] for p in x], 0))
        even = [u[:h], u[h:]]
        odd = conj_product(self.wl(w), [v[:h], v[h:]])
        return [cat([e + o, e - o], 0) for e, o in zip(even, odd)]


SIN = [(-1.0) ** i / math.factorial(2 * i + 1) for i in range(7)]
COS = [(-1.0) ** i / math.factorial(2 * i) for i in range(7)]


def series(coefficients, z):
    total = coefficients[-1]
    for c in coefficients[-2::-1]:
        total = total * z + c
    return total


def cos_sin(x):
    y = 0.5 * x
    z = y * y
    s, c = y * series(SIN, z), series(COS, z)
    return 1.0 - 2.0 * (s * s), 2.0 * (s * c)


def iota(shape, dim):
    return lax.broadcasted_iota(jnp.int32, shape, dim)


def dyn_roll(x, shift, axis):
    return pltpu.roll(x, shift, axis=axis)


def half_roll(x):
    return pltpu.roll(x, x.shape[-1] // 2, axis=x.ndim - 1)


def pack_cols(re, im):
    h = re.shape[1] // 2
    front = iota((re.shape[0], h), 1) < h // 2
    low = jnp.where(front, re[:, :h], half_roll(im[:, :h]))
    high = jnp.where(front, half_roll(im[:, h:]), re[:, h:])
    return low, high


def copy_all(sources, places, sems):
    copies = [
        pltpu.make_async_copy(a, b, sems.at[i]) for i, (a, b) in enumerate(zip(sources, places))
    ]
    for copy in copies:
        copy.start()
    return copies


def row_start(which, n, margin):
    even = lax.axis_index("row") % 2 == 0
    last = even if which == 0 else jnp.logical_not(even)
    return pl.multiple_of(jnp.where(last, n - margin, 0), 8)


def pack_kernel(margin, obj_hbm, offs_hbm, obj, offs, limits, *refs):
    evens, odds, rows, sems = refs[:2], refs[2], refs[3:-1], refs[-1]
    n = obj.shape[1]
    copies = copy_all(
        (obj_hbm.at[0:2], obj_hbm.at[2:4], offs_hbm), (obj.at[0:2], obj.at[2:4], offs), sems
    )
    even = lax.axis_index("col") % 2 == 0
    for s in range(2):
        copies[s].wait()
        low, high = pack_cols(obj[2 * s], obj[2 * s + 1])
        strip = jnp.where(even, high, low)
        if s == 0:
            evens[0][:n] = strip
        else:
            evens[0][n:], evens[1][...] = strip[: n // 2], strip[n // 2 :]
        odds[s] = jnp.where(even, low, high)
    for which, out in enumerate(rows):
        out[...] = obj[:, pl.ds(row_start(which, n, margin), margin), :]
    copies[2].wait()
    for i in range(2):
        limits[i] = jnp.full(limits.shape[1:], offs[0, i] - margin, jnp.int32)


def corner_kernel(s, margin, *refs):
    evens, o, outs = refs[: s + 1], refs[s + 1], refs[s + 3 :]
    n = o.shape[1]
    for which, out in enumerate(outs):
        start = row_start(which, n, margin)
        if s == 0:
            out[0] = evens[0][pl.ds(start, margin), :]
        else:
            top, bottom = evens[0][n : n + margin], evens[1][n // 2 - margin :]
            out[0] = jnp.where(start == 0, top, bottom)
        out[1] = o[s, pl.ds(start, margin), :]


def even_odd(n, axis):
    h = n // 2
    natural, sorted_ = iota((n, n), axis), iota((n, n), 1 - axis)
    source = jnp.where(sorted_ < h, 2 * sorted_, 2 * (sorted_ - h) + 1)
    return (natural == source).astype(F32).astype(BF16)


def reorder(x, order):
    def thirds(y):
        a = y.astype(BF16)
        return (a,) + split(y - a.astype(F32))

    a, b, c = thirds(x)
    a, b, c = thirds(dot(order[1], a) + (dot(order[1], b) + dot(order[1], c)))
    return dot(a, order[0]) + (dot(b, order[0]) + dot(c, order[0]))


def prep_kernel(*refs):
    hbm, (kr, ki, mats), loaded = refs[:6], refs[6:9], refs[9:13]
    phase, table, sems = refs[13:]
    n = phase.shape[0]
    h = n // 2
    first = pltpu.make_async_copy(hbm[0], phase, sems.at[0])
    first.start()
    order = [even_odd(n, axis) for axis in range(2)]
    first.wait()
    copies = copy_all(hbm[1:], (table,) + loaded, sems)
    angle = reorder(phase[...], order)
    kr[...], ki[...] = cos_sin(angle)
    copies[0].wait()
    for i in range(2):
        mats[i] = table[i]
        mats[2 + i, :h, :h] = table[i, :h, :h]
        mats[2 + i, :h, h:] = -table[i, :h, h:]
        mats[2 + i, h:, :h] = -table[i, h:, :h]
        mats[2 + i, h:, h:] = table[i, h:, h:]
    for copy in copies[1:]:
        copy.wait()


def reorder_kernel(x, after, out):
    out[...] = reorder(x[...], [even_odd(x.shape[0], axis) for axis in range(2)])


def roll_kernel(margin, offs, probe, pr):
    n = probe.shape[1]
    sy = (offs[0, 0] - margin + n) % n
    sx = (offs[0, 1] - margin + n) % n
    for i in range(2):
        pr[i] = dyn_roll(dyn_roll(probe[i], sy, 0), sx, 1)


def merge_cols(own, e, o, limits):
    n = own[0].shape[1]
    h = n // 2
    even = lax.axis_index("col") % 2 == 0
    high, low = jnp.where(even, e, o), jnp.where(even, o, e)
    lane = iota((1, h), 1)
    from_high = lane < limits[1, 0:1]
    from_low = lane >= limits[1, 0:1] + h
    out = []
    for i in range(2):
        strip_high = high if i == 0 else half_roll(high)
        strip_low = low if i == 0 else half_roll(low)
        out.append(
            cat(
                [
                    jnp.where(from_high, strip_high, own[i][:, :h]),
                    jnp.where(from_low, strip_low, own[i][:, h:]),
                ],
                1,
            )
        )
    return out


def merge_kernel(s, obj, *refs):
    evens, (o, limits, out) = refs[: s + 1], refs[s + 1 :]
    n = obj.shape[1]
    e = cat([evens[0][n:], evens[1][...]], 0) if s else evens[0][:n]
    own = [obj[2 * s], obj[2 * s + 1]]
    out[0], out[1] = merge_cols(own, e, o[s], limits)


def window_of(main, s, halos, corners, limits, margin):
    n = main.shape[1]
    row_even = lax.axis_index("row") % 2 == 0
    blocks = []
    for halo, corner in zip(halos, corners):
        own = [halo[2 * s], halo[2 * s + 1]]
        blocks.append(merge_cols(own, corner[0], corner[1], limits))
    row = iota((margin, n), 0)
    limit = cat([limits[0, 0:1]] * 2, 1)
    take_high = row < limit
    take_low = row >= limit + margin
    out = []
    for i in range(2):
        e = blocks[0][i]
        o = blocks[1][i] if len(blocks) == 2 else jnp.zeros_like(e)
        high, low = jnp.where(row_even, e, o), jnp.where(row_even, o, e)
        out.append(
            cat(
                [
                    jnp.where(take_high, high, main[i, :margin]),
                    main[i, margin : n - margin],
                    jnp.where(take_low, low, main[i, n - margin :]),
                ],
                0,
            )
        )
    return out


def unpack(n_row, refs):
    return refs[0], refs[1 : 1 + n_row], refs[1 + n_row : 1 + 2 * n_row], refs[1 + 2 * n_row :]


def through(dft, x, re, im):
    return dft.right_inverse(product([re, im], dft.right(x)))


def arrive_kernel(n_row, margin, *refs):
    main, halos, corners, refs = unpack(n_row, refs)
    limits, pr, kr, ki, mats, twl, twr, w1, arrive = refs
    n = main.shape[1]
    dft = Dft(mats, twl[...], twr[...], n)
    win = window_of(main, 0, halos, corners, limits, margin)
    w1[0], w1[1] = win
    x = dft.left(product([pr[0], pr[1]], win))
    x = through(dft, x, kr[...], ki[...])
    arrive[0], arrive[1] = dft.left_inverse(x)


def back_kernel(n_row, margin, *refs):
    main, halos, corners, refs = unpack(n_row, refs)
    limits, offs_hbm, pr, kr, ki, am, w1, arrive, mats, twl, twr = refs[:11]
    keep, give, grads, offs, sem = refs[11:]
    scalars = pltpu.make_async_copy(offs_hbm, offs, sem)
    scalars.start()
    n = main.shape[1]
    dft = Dft(mats, twl[...], twr[...], n)
    win = window_of(main, 1, halos, corners, limits, margin)
    x = dft.left(product([arrive[0], arrive[1]], win))
    far = dft.right(x)
    modulus = jnp.sqrt(far[0] * far[0] + far[1] * far[1] + EPS_AMP)
    factor = 2.0 * (1.0 - am[...] / modulus)
    x = dft.right_inverse([factor * far[0], factor * far[1]])
    back_far = dft.left_inverse(x)
    grads[2], grads[3] = conj_product([arrive[0], arrive[1]], back_far)
    x = dft.left(conj_product(win, back_far))
    x = through(dft, x, kr[...], -ki[...])
    x = dft.left_inverse(x)
    grads[0], grads[1] = conj_product([pr[0], pr[1]], x)
    grad = conj_product([w1[0], w1[1]], x)
    scalars.wait()
    sy = (margin - offs[0, 0] + n) % n
    sx = (margin - offs[0, 1] + n) % n
    grad = [dyn_roll(dyn_roll(g, sy, 0), sx, 1) for g in grad]
    even = lax.axis_index("row") % 2 == 0
    keep[...] = jnp.where(even, grad[0], grad[1])
    give[...] = jnp.where(even, grad[1], grad[0])


def divide_kernel(margin, grads, limits, own, strip, *sends):
    for s in range(2):
        split_grad([grads[2 * s], grads[2 * s + 1]], s, limits, margin, own, strip, sends)


def split_grad(grad, s, limits, margin, own, strip, sends):
    n = grad[0].shape[0]
    h = n // 2
    row_even = lax.axis_index("row") % 2 == 0
    lane = iota((1, h), 1)
    to_high, to_low = lane < limits[1, 0:1], lane >= limits[1, 0:1] + h
    front = lane < h // 2
    spill = jnp.where(front, to_high.astype(jnp.int32), to_low.astype(jnp.int32)) != 0
    for i in range(2):
        g = grad[i]
        row = iota((n, h), 0)
        high_rows = row < limits[0, 0:1]
        low_rows = row >= limits[0, 0:1] + n
        inner = jnp.logical_not(jnp.logical_or(high_rows, low_rows))
        left = jnp.where(to_high, 0.0, g[:, :h])
        right = jnp.where(to_low, 0.0, g[:, h:])
        side = jnp.where(spill, jnp.where(front, g[:, :h], g[:, h:]), 0.0)
        pieces = [left, right, side]
        own[2 * s + i, :, :h] = jnp.where(inner, left, 0.0)
        own[2 * s + i, :, h:] = jnp.where(inner, right, 0.0)
        strip[2 * s + i] = jnp.where(inner, side, 0.0)
        for j, piece in enumerate(pieces):
            top = jnp.where(high_rows[:margin], piece[:margin], 0.0)
            bottom = jnp.where(low_rows[n - margin :], piece[n - margin :], 0.0)
            for which, send in enumerate(sends):
                first = row_even if which == 0 else jnp.logical_not(row_even)
                send[2 * s + i, :, j * h : (j + 1) * h] = jnp.where(first, top, bottom)


def fold_rows_kernel(n_row, margin, own, strip, *refs):
    got, (total, send_e, send_o) = refs[:n_row], refs[n_row:]
    row_even = lax.axis_index("row") % 2 == 0
    col_even = lax.axis_index("col") % 2 == 0
    n = own.shape[1]
    h = n // 2
    front = iota((n, h), 1) < h // 2
    for s in range(2):
        strips = []
        for i in range(2 * s, 2 * s + 2):
            total[i] = own[i]
            r = got[0][i]
            q = got[1][i] if n_row == 2 else jnp.zeros_like(r)
            top, bottom = jnp.where(row_even, q, r), jnp.where(row_even, r, q)
            total[i, :margin] += top[:, :n]
            total[i, n - margin :] += bottom[:, :n]
            st = strip[i]
            strips.append(
                cat(
                    [
                        st[:margin] + top[:, n:],
                        st[margin : n - margin],
                        st[n - margin :] + bottom[:, n:],
                    ],
                    0,
                )
            )
        moved = half_roll(strips[1])
        to_high = jnp.where(front, strips[0], moved)
        to_low = jnp.where(front, moved, strips[0])
        send_e[s] = jnp.where(col_even, to_high, to_low)
        send_o[s] = jnp.where(col_even, to_low, to_high)


def fold_cols_kernel(total, e, o, out):
    col_even = lax.axis_index("col") % 2 == 0
    n = total.shape[1]
    h = n // 2
    front = iota((n, h), 1) < h // 2
    for s in range(2):
        high = jnp.where(col_even, e[s], o[s])
        low = jnp.where(col_even, o[s], e[s])
        for i in range(2):
            a = low if i == 0 else half_roll(low)
            b = high if i == 0 else half_roll(high)
            at = 2 * s + i
            out[at, :, :h] = total[at, :, :h] + jnp.where(front, a, 0.0)
            out[at, :, h:] = total[at, :, h:] + jnp.where(front, 0.0, b)


def in_hbm(x):
    return pltpu.with_memory_space_constraint(x, pltpu.HBM)


def call(kernel, shapes, in_specs, *args, scratch=(), mib=16):
    shapes = [s if isinstance(s, jax.ShapeDtypeStruct) else jax.ShapeDtypeStruct(s, F32) for s in shapes]
    return pl.pallas_call(
        kernel,
        out_shape=shapes,
        in_specs=in_specs,
        out_specs=[SMEM if s.shape == (1, 2) else VMEM for s in shapes],
        scratch_shapes=list(scratch),
        compiler_params=pltpu.CompilerParams(vmem_limit_bytes=mib << 20),
    )(*args)


def edges(axis):
    count = lax.axis_size(axis)
    rounds = []
    for first in (0, 1):
        pairs = [(i, i + 1) for i in range(first, count - 1, 2)]
        pairs += [(b, a) for a, b in pairs]
        if pairs:
            rounds.append(pairs)
    return rounds


def swap(value, axis, distance):
    count = lax.axis_size(axis)
    return lax.ppermute(value, axis, [(i, i ^ distance) for i in range(count)])


def groups():
    cols = [("col", 1 << b) for b in range(lax.axis_size("col").bit_length() - 1)]
    rows = [("row", 1 << b) for b in range(1, lax.axis_size("row").bit_length() - 1)]
    first, rest = cols[:2], cols[2:]
    pairs = [first]
    for bits in (rest, rows):
        pairs += [bits[i : i + 2] for i in range(0, len(bits), 2)]
    out = []
    for pair in pairs:
        axis, masks = pair[0][0], [m for _, m in pair]
        out.append((axis, [0] + masks + ([sum(masks)] if len(masks) == 2 else [])))
    return out


def pair_sum(parts):
    while len(parts) > 1:
        parts = [parts[i] + parts[i + 1] for i in range(0, len(parts), 2)]
    return parts[0]


def share_kernel(quad, stride, keep, other, *parts):
    place = lax.axis_index("col") // stride % quad
    chunk = keep.shape[0] // quad
    for j, part in enumerate(parts):
        rows = pl.ds(pl.multiple_of((place ^ j) * chunk, 8), chunk)
        part[...] = keep[rows, :] + other[rows, :]


def sum_kernel(*refs):
    refs[-1][...] = pair_sum([r[...] for r in refs[:-1]])


def join_kernel(stride, *refs):
    parts, full = refs[:-1], refs[-1]
    quad, chunk = len(parts), parts[0].shape[0]
    place = lax.axis_index("col") // stride % quad
    for j, part in enumerate(parts):
        full[pl.ds(pl.multiple_of((place ^ j) * chunk, 8), chunk), :] = part[...]


def half_kernel(full, out, sem):
    copy = pltpu.make_async_copy(full, out.at[lax.axis_index("row") % 2], sem)
    copy.start()
    copy.wait()


def other_kernel(started, other, out, sem):
    copy = pltpu.make_async_copy(other, out.at[1 - lax.axis_index("row") % 2], sem)
    copy.start()
    copy.wait()


def reduce_probe(keep, give):
    n = keep.shape[0]
    (_, offsets), *rest = groups()
    quad, stride = len(offsets), offsets[1]
    chunk = n // quad
    other = swap(give, "row", 1)
    parts = call(
        functools.partial(share_kernel, quad, stride),
        [(chunk, n)] * quad,
        [VMEM] * 2,
        keep,
        other,
    )
    sums = [parts[0]]
    for j in range(1, quad):
        sums.append(swap(parts[j], "col", offsets[j]))
    (total,) = call(sum_kernel, [(chunk, n)], [VMEM] * quad, *sums)
    for axis, masks in rest:
        sums = [total]
        for mask in masks[1:]:
            sums.append(swap(total, axis, mask))
        (total,) = call(sum_kernel, [(chunk, n)], [VMEM] * len(sums), *sums)
    parts = [total]
    for j in range(1, quad):
        parts.append(swap(total, "col", offsets[j]))
    (full,) = call(
        functools.partial(join_kernel, stride), [(n, n)], [VMEM] * quad, *parts
    )
    other = swap(full, "row", 1)
    out = dict(
        out_shape=jax.ShapeDtypeStruct((2, n, n), F32),
        out_specs=HBM,
        scratch_shapes=[pltpu.SemaphoreType.DMA(())],
        compiler_params=pltpu.CompilerParams(vmem_limit_bytes=16 << 20),
    )
    grad = pl.pallas_call(half_kernel, in_specs=[VMEM], **out)(full)
    return pl.pallas_call(
        other_kernel, in_specs=[HBM, VMEM], input_output_aliases={0: 0}, **out
    )(grad, other)


def whole(object_field, probe, phase, amplitudes, offsets):
    tile = object_field.shape[2]
    n = probe.shape[1]
    h = n // 2
    margin = n // 4
    mats, tw_left, tw_right = [jnp.asarray(t) for t in dft_constants(n)]

    row_rounds, col_rounds = edges("row"), edges("col")
    n_row = len(row_rounds)
    obj, offs, limits, even0, even1, odds, *rows = call(
        functools.partial(pack_kernel, margin),
        [(4, n, n), jax.ShapeDtypeStruct((1, 2), jnp.int32)]
        + [jax.ShapeDtypeStruct((2, 8, h), jnp.int32)]
        + [(n + n // 2, h), (n // 2, h), (2, n, h)]
        + [(4, margin, n)] * n_row,
        [HBM, HBM],
        in_hbm(object_field.reshape(4, tile, tile)),
        in_hbm(offsets.reshape(1, 2)),
        scratch=[pltpu.SemaphoreType.DMA((3,))],
    )
    halos, corners = [], [[], []]
    even0 = lax.ppermute(even0, "col", col_rounds[0])
    odds = lax.ppermute(odds, "col", col_rounds[1])
    even1 = lax.ppermute(even1, "col", col_rounds[0])
    for i, pairs in enumerate(row_rounds):
        halos.append(lax.ppermute(rows[i], "row", pairs))
    evens = (even0, even1)

    def cut(s, after):
        parts = call(
            functools.partial(corner_kernel, s, margin),
            [(2, margin, h)] * n_row,
            [VMEM] * (3 + s),
            *evens[: s + 1],
            odds,
            after,
        )
        for i, pairs in enumerate(row_rounds):
            corners[s].append(lax.ppermute(parts[i], "row", pairs))

    def merge(s):
        (main,) = call(
            functools.partial(merge_kernel, s),
            [(2, n, n)],
            [VMEM] * (4 + s),
            obj,
            *evens[: s + 1],
            odds,
            limits,
        )
        return main

    loads = (phase, mats, tw_left, tw_right, probe, amplitudes.reshape(n, n))
    kr, ki, mats, tw_left, tw_right, pr, am = call(
        prep_kernel,
        [(n, n)] * 2
        + [jax.ShapeDtypeStruct((4, n, n), BF16)]
        + [jax.ShapeDtypeStruct(x.shape, x.dtype) for x in loads[2:]],
        [HBM] * len(loads),
        *[in_hbm(x) for x in loads],
        scratch=[
            pltpu.VMEM((n, n), F32),
            pltpu.VMEM((2, n, n), BF16),
            pltpu.SemaphoreType.DMA((len(loads),)),
        ],
    )
    (pr,) = call(functools.partial(roll_kernel, margin), [(2, n, n)], [SMEM, VMEM], offs, pr)
    (am,) = call(reorder_kernel, [(n, n)], [VMEM] * 2, am, pr)
    cut(0, am)
    main = merge(0)
    cut(1, main)
    w1, arrive = call(
        functools.partial(arrive_kernel, n_row, margin),
        [(2, n, n), (2, n, n)],
        [VMEM] * (8 + 2 * n_row),
        main,
        *halos,
        *corners[0],
        limits,
        pr,
        kr,
        ki,
        mats,
        tw_left,
        tw_right,
    )
    main = merge(1)
    keep, give, grads = call(
        functools.partial(back_kernel, n_row, margin),
        [(n, n), (n, n), (4, n, n)],
        [VMEM] * (2 + 2 * n_row) + [HBM] + [VMEM] * 9,
        main,
        *halos,
        *corners[1],
        limits,
        in_hbm(offsets.reshape(1, 2)),
        pr,
        kr,
        ki,
        am,
        w1,
        arrive,
        mats,
        tw_left,
        tw_right,
        scratch=[pltpu.SMEM((1, 2), jnp.int32), pltpu.SemaphoreType.DMA(())],
        mib=40,
    )
    probe_grad = reduce_probe(keep, give)
    own, strip, *sends = call(
        functools.partial(divide_kernel, margin),
        [(4, n, n), (4, n, h)] + [(4, margin, n + h)] * n_row,
        [VMEM, VMEM],
        grads,
        limits,
    )
    got = []
    for i, pairs in enumerate(row_rounds):
        got.append(lax.ppermute(sends[i], "row", pairs))
    total, send_e, send_o = call(
        functools.partial(fold_rows_kernel, n_row, margin),
        [(4, n, n), (2, n, h), (2, n, h)],
        [VMEM] * (2 + n_row),
        own,
        strip,
        *got,
    )
    send_e = lax.ppermute(send_e, "col", col_rounds[0])
    send_o = lax.ppermute(send_o, "col", col_rounds[1])
    (grad,) = call(fold_cols_kernel, [(4, n, n)], [VMEM] * 3, total, send_e, send_o)
    return (grad.reshape(2, 2, tile, tile), probe_grad)


def solution(mesh):
    placed = (
        P(None, None, "row", "col"),
        P(),
        P(),
        P("row", "col", None, None, None),
        P("row", "col", None, None),
    )
    return jax.shard_map(
        whole,
        mesh=mesh,
        in_specs=placed,
        out_specs=(P(None, None, "row", "col"), P()),
        check_vma=False,
    )
```

```python
import functools
import math

import jax
import jax.numpy as jnp
import numpy as np
from jax import lax
from jax.experimental import pallas as pl
from jax.experimental.pallas import tpu as pltpu
from jax.sharding import PartitionSpec as P


EPS_AMP = 0.5
F32 = jnp.float32
BF16 = jnp.bfloat16
VMEM = pl.BlockSpec(memory_space=pltpu.VMEM)
SMEM = pl.BlockSpec(memory_space=pltpu.SMEM)
HBM = pl.BlockSpec(memory_space=pltpu.HBM)


def split_np(table):
    high = table.astype(BF16)
    low = (table - high.astype(np.float64)).astype(BF16)
    return [high, low]


def dft_constants(n):
    h = n // 2
    k = np.arange(h)
    angle = 2.0 * np.pi * ((k[:, None] * k[None, :]) % h) / h
    scale = 1.0 / np.sqrt(n)
    c, s = np.cos(angle) * scale, np.sin(angle) * scale
    d = np.block([[c, s], [-s, c]])
    mats = np.stack(split_np(d))
    w = np.exp(-2j * np.pi * k / n)
    tw_left = np.stack([np.tile(w.real[:, None], (1, h)), np.tile(w.imag[:, None], (1, h))])
    tw_right = np.stack([np.tile(w.real[None], (8, 1)), np.tile(w.imag[None], (8, 1))])
    return mats, tw_left.astype(np.float32), tw_right.astype(np.float32)


def split(x):
    high = x.astype(BF16)
    return high, (x - high.astype(F32)).astype(BF16)


def dot(a, b):
    return jnp.dot(a, b, preferred_element_type=F32)


def left_dot(mats, which, x):
    high, low = split(x)
    return dot(mats[which], high) + (dot(mats[which], low) + dot(mats[which + 1], high))


def right_dot(x, mats, which):
    high, low = split(x)
    return dot(high, mats[which]) + (dot(low, mats[which]) + dot(high, mats[which + 1]))


def cat(parts, axis):
    return jnp.concatenate(parts, axis=axis)


def product(a, b):
    return (a[0] * b[0] - a[1] * b[1], a[0] * b[1] + a[1] * b[0])


def conj_product(a, b):
    return (a[0] * b[0] + a[1] * b[1], a[0] * b[1] - a[1] * b[0])


class Dft:
    def __init__(self, mats, tw_left, tw_right, n):
        self.mats, self.n, self.h = mats, n, n // 2
        self.tw_left, self.tw_right = tw_left, tw_right

    def wl(self, width):
        parts = width // self.tw_left.shape[2]
        return [cat([self.tw_left[i]] * parts, 1) for i in range(2)]

    def wr(self):
        return [self.tw_right[i, 0:1] for i in range(2)]

    def left(self, x):
        h, w = self.h, x[0].shape[1]
        total = [p[:h] + p[h:] for p in x]
        odd = product([p[:h] - p[h:] for p in x], self.wl(w))
        u = left_dot(self.mats, 0, cat(total, 0))
        v = left_dot(self.mats, 0, cat(odd, 0))
        return [cat([u[:h], v[:h]], 0), cat([u[h:], v[h:]], 0)]

    def right(self, x):
        h, m = self.h, x[0].shape[0]
        total = [p[:, :h] + p[:, h:] for p in x]
        odd = product([p[:, :h] - p[:, h:] for p in x], self.wr())
        u = right_dot(cat(total, 1), self.mats, 2)
        v = right_dot(cat(odd, 1), self.mats, 2)
        return [cat([u[:, :h], v[:, :h]], 1), cat([u[:, h:], v[:, h:]], 1)]

    def right_inverse(self, x):
        h, m = self.h, x[0].shape[0]
        u = right_dot(cat([p[:, :h] for p in x], 1), self.mats, 0)
        v = right_dot(cat([p[:, h:] for p in x], 1), self.mats, 0)
        even = [u[:, :h], u[:, h:]]
        odd = conj_product(self.wr(), [v[:, :h], v[:, h:]])
        return [cat([e + o, e - o], 1) for e, o in zip(even, odd)]

    def left_inverse(self, x):
        h, w = self.h, x[0].shape[1]
        u = left_dot(self.mats, 2, cat([p[:h] for p in x], 0))
        v = left_dot(self.mats, 2, cat([p[h:] for p in x], 0))
        even = [u[:h], u[h:]]
        odd = conj_product(self.wl(w), [v[:h], v[h:]])
        return [cat([e + o, e - o], 0) for e, o in zip(even, odd)]


SIN = [(-1.0) ** i / math.factorial(2 * i + 1) for i in range(7)]
COS = [(-1.0) ** i / math.factorial(2 * i) for i in range(7)]


def series(coefficients, z):
    total = coefficients[-1]
    for c in coefficients[-2::-1]:
        total = total * z + c
    return total


def cos_sin(x):
    y = 0.5 * x
    z = y * y
    s, c = y * series(SIN, z), series(COS, z)
    return 1.0 - 2.0 * (s * s), 2.0 * (s * c)


def iota(shape, dim):
    return lax.broadcasted_iota(jnp.int32, shape, dim)


def dyn_roll(x, shift, axis):
    return pltpu.roll(x, shift, axis=axis)


def half_roll(x):
    return pltpu.roll(x, x.shape[-1] // 2, axis=x.ndim - 1)


def pack_cols(re, im):
    h = re.shape[1] // 2
    front = iota((re.shape[0], h), 1) < h // 2
    low = jnp.where(front, re[:, :h], half_roll(im[:, :h]))
    high = jnp.where(front, half_roll(im[:, h:]), re[:, h:])
    return low, high


def copy_all(sources, places, sems):
    copies = [
        pltpu.make_async_copy(a, b, sems.at[i]) for i, (a, b) in enumerate(zip(sources, places))
    ]
    for copy in copies:
        copy.start()
    return copies


def row_start(which, n, margin):
    even = lax.axis_index("row") % 2 == 0
    last = even if which == 0 else jnp.logical_not(even)
    return pl.multiple_of(jnp.where(last, n - margin, 0), 8)


def pack_kernel(margin, obj_hbm, obj, *refs):
    evens, odds, rows, sems = refs[:2], refs[2], refs[3:-1], refs[-1]
    n = obj.shape[1]
    copies = copy_all((obj_hbm.at[0:2], obj_hbm.at[2:4]), (obj.at[0:2], obj.at[2:4]), sems)
    even = lax.axis_index("col") % 2 == 0
    for s in range(2):
        copies[s].wait()
        low, high = pack_cols(obj[2 * s], obj[2 * s + 1])
        strip = jnp.where(even, high, low)
        if s == 0:
            evens[0][:n] = strip
        else:
            evens[0][n:], evens[1][...] = strip[: n // 2], strip[n // 2 :]
        odds[s] = jnp.where(even, low, high)
    for which, out in enumerate(rows):
        out[...] = obj[:, pl.ds(row_start(which, n, margin), margin), :]


def corner_kernel(s, margin, *refs):
    evens, o, outs = refs[: s + 1], refs[s + 1], refs[s + 3 :]
    n = o.shape[1]
    for which, out in enumerate(outs):
        start = row_start(which, n, margin)
        if s == 0:
            out[0] = evens[0][pl.ds(start, margin), :]
        else:
            top, bottom = evens[0][n : n + margin], evens[1][n // 2 - margin :]
            out[0] = jnp.where(start == 0, top, bottom)
        out[1] = o[s, pl.ds(start, margin), :]


def even_odd(n, axis):
    h = n // 2
    natural, sorted_ = iota((n, n), axis), iota((n, n), 1 - axis)
    source = jnp.where(sorted_ < h, 2 * sorted_, 2 * (sorted_ - h) + 1)
    return (natural == source).astype(F32).astype(BF16)


def reorder(x, order):
    def thirds(y):
        a = y.astype(BF16)
        return (a,) + split(y - a.astype(F32))

    a, b, c = thirds(x)
    a, b, c = thirds(dot(order[1], a) + (dot(order[1], b) + dot(order[1], c)))
    return dot(a, order[0]) + (dot(b, order[0]) + dot(c, order[0]))


def prep_kernel(margin, *refs):
    hbm, (offs, limits, kr, ki, mats), loaded = refs[:7], refs[7:12], refs[12:16]
    phase, table, sems = refs[16:]
    n = phase.shape[0]
    h = n // 2
    first = pltpu.make_async_copy(hbm[0], phase, sems.at[0])
    first.start()
    order = [even_odd(n, axis) for axis in range(2)]
    first.wait()
    copies = copy_all(hbm[1:], (table,) + loaded + (offs,), sems)
    angle = reorder(phase[...], order)
    kr[...], ki[...] = cos_sin(angle)
    copies[0].wait()
    for i in range(2):
        mats[i] = table[i]
        mats[2 + i, :h, :h] = table[i, :h, :h]
        mats[2 + i, :h, h:] = -table[i, :h, h:]
        mats[2 + i, h:, :h] = -table[i, h:, :h]
        mats[2 + i, h:, h:] = table[i, h:, h:]
    for copy in copies[1:]:
        copy.wait()
    for i in range(2):
        limits[i] = jnp.full(limits.shape[1:], offs[0, i] - margin, jnp.int32)


def reorder_kernel(x, after, out):
    out[...] = reorder(x[...], [even_odd(x.shape[0], axis) for axis in range(2)])


def roll_kernel(margin, offs, probe, pr):
    n = probe.shape[1]
    sy = (offs[0, 0] - margin + n) % n
    sx = (offs[0, 1] - margin + n) % n
    for i in range(2):
        pr[i] = dyn_roll(dyn_roll(probe[i], sy, 0), sx, 1)


def merge_cols(own, e, o, limits):
    n = own[0].shape[1]
    h = n // 2
    even = lax.axis_index("col") % 2 == 0
    high, low = jnp.where(even, e, o), jnp.where(even, o, e)
    lane = iota((1, h), 1)
    from_high = lane < limits[1, 0:1]
    from_low = lane >= limits[1, 0:1] + h
    out = []
    for i in range(2):
        strip_high = high if i == 0 else half_roll(high)
        strip_low = low if i == 0 else half_roll(low)
        out.append(
            cat(
                [
                    jnp.where(from_high, strip_high, own[i][:, :h]),
                    jnp.where(from_low, strip_low, own[i][:, h:]),
                ],
                1,
            )
        )
    return out


def merge_kernel(s, obj, *refs):
    evens, (o, limits, out) = refs[: s + 1], refs[s + 1 :]
    n = obj.shape[1]
    e = cat([evens[0][n:], evens[1][...]], 0) if s else evens[0][:n]
    own = [obj[2 * s], obj[2 * s + 1]]
    out[0], out[1] = merge_cols(own, e, o[s], limits)


def window_of(main, s, halos, corners, limits, margin):
    n = main.shape[1]
    row_even = lax.axis_index("row") % 2 == 0
    blocks = []
    for halo, corner in zip(halos, corners):
        own = [halo[2 * s], halo[2 * s + 1]]
        blocks.append(merge_cols(own, corner[0], corner[1], limits))
    row = iota((margin, n), 0)
    limit = cat([limits[0, 0:1]] * 2, 1)
    take_high = row < limit
    take_low = row >= limit + margin
    out = []
    for i in range(2):
        e = blocks[0][i]
        o = blocks[1][i] if len(blocks) == 2 else jnp.zeros_like(e)
        high, low = jnp.where(row_even, e, o), jnp.where(row_even, o, e)
        out.append(
            cat(
                [
                    jnp.where(take_high, high, main[i, :margin]),
                    main[i, margin : n - margin],
                    jnp.where(take_low, low, main[i, n - margin :]),
                ],
                0,
            )
        )
    return out


def unpack(n_row, refs):
    return refs[0], refs[1 : 1 + n_row], refs[1 + n_row : 1 + 2 * n_row], refs[1 + 2 * n_row :]


def through(dft, x, re, im):
    return dft.right_inverse(product([re, im], dft.right(x)))


def arrive_kernel(n_row, margin, *refs):
    main, halos, corners, refs = unpack(n_row, refs)
    limits, pr, kr, ki, mats, twl, twr, w1, arrive = refs
    n = main.shape[1]
    dft = Dft(mats, twl[...], twr[...], n)
    win = window_of(main, 0, halos, corners, limits, margin)
    w1[0], w1[1] = win
    x = dft.left(product([pr[0], pr[1]], win))
    x = through(dft, x, kr[...], ki[...])
    arrive[0], arrive[1] = dft.left_inverse(x)


def back_kernel(n_row, margin, *refs):
    main, halos, corners, refs = unpack(n_row, refs)
    limits, offs_hbm, pr, kr, ki, am, w1, arrive, mats, twl, twr = refs[:11]
    keep, give, grads, offs, sem = refs[11:]
    scalars = pltpu.make_async_copy(offs_hbm, offs, sem)
    scalars.start()
    n = main.shape[1]
    dft = Dft(mats, twl[...], twr[...], n)
    win = window_of(main, 1, halos, corners, limits, margin)
    x = dft.left(product([arrive[0], arrive[1]], win))
    far = dft.right(x)
    modulus = jnp.sqrt(far[0] * far[0] + far[1] * far[1] + EPS_AMP)
    factor = 2.0 * (1.0 - am[...] / modulus)
    x = dft.right_inverse([factor * far[0], factor * far[1]])
    back_far = dft.left_inverse(x)
    grads[2], grads[3] = conj_product([arrive[0], arrive[1]], back_far)
    x = dft.left(conj_product(win, back_far))
    x = through(dft, x, kr[...], -ki[...])
    x = dft.left_inverse(x)
    grads[0], grads[1] = conj_product([pr[0], pr[1]], x)
    grad = conj_product([w1[0], w1[1]], x)
    scalars.wait()
    sy = (margin - offs[0, 0] + n) % n
    sx = (margin - offs[0, 1] + n) % n
    grad = [dyn_roll(dyn_roll(g, sy, 0), sx, 1) for g in grad]
    even = lax.axis_index("row") % 2 == 0
    keep[...] = jnp.where(even, grad[0], grad[1])
    give[...] = jnp.where(even, grad[1], grad[0])


def divide_kernel(margin, grads, limits, own, strip, *sends):
    for s in range(2):
        split_grad([grads[2 * s], grads[2 * s + 1]], s, limits, margin, own, strip, sends)


def split_grad(grad, s, limits, margin, own, strip, sends):
    n = grad[0].shape[0]
    h = n // 2
    row_even = lax.axis_index("row") % 2 == 0
    lane = iota((1, h), 1)
    to_high, to_low = lane < limits[1, 0:1], lane >= limits[1, 0:1] + h
    front = lane < h // 2
    spill = jnp.where(front, to_high.astype(jnp.int32), to_low.astype(jnp.int32)) != 0
    for i in range(2):
        g = grad[i]
        row = iota((n, h), 0)
        high_rows = row < limits[0, 0:1]
        low_rows = row >= limits[0, 0:1] + n
        inner = jnp.logical_not(jnp.logical_or(high_rows, low_rows))
        left = jnp.where(to_high, 0.0, g[:, :h])
        right = jnp.where(to_low, 0.0, g[:, h:])
        side = jnp.where(spill, jnp.where(front, g[:, :h], g[:, h:]), 0.0)
        pieces = [left, right, side]
        own[2 * s + i, :, :h] = jnp.where(inner, left, 0.0)
        own[2 * s + i, :, h:] = jnp.where(inner, right, 0.0)
        strip[2 * s + i] = jnp.where(inner, side, 0.0)
        for j, piece in enumerate(pieces):
            top = jnp.where(high_rows[:margin], piece[:margin], 0.0)
            bottom = jnp.where(low_rows[n - margin :], piece[n - margin :], 0.0)
            for which, send in enumerate(sends):
                first = row_even if which == 0 else jnp.logical_not(row_even)
                send[2 * s + i, :, j * h : (j + 1) * h] = jnp.where(first, top, bottom)


def fold_rows_kernel(n_row, margin, own, strip, *refs):
    got, (total, send_e, send_o) = refs[:n_row], refs[n_row:]
    row_even = lax.axis_index("row") % 2 == 0
    col_even = lax.axis_index("col") % 2 == 0
    n = own.shape[1]
    h = n // 2
    front = iota((n, h), 1) < h // 2
    for s in range(2):
        strips = []
        for i in range(2 * s, 2 * s + 2):
            total[i] = own[i]
            r = got[0][i]
            q = got[1][i] if n_row == 2 else jnp.zeros_like(r)
            top, bottom = jnp.where(row_even, q, r), jnp.where(row_even, r, q)
            total[i, :margin] += top[:, :n]
            total[i, n - margin :] += bottom[:, :n]
            st = strip[i]
            strips.append(
                cat(
                    [
                        st[:margin] + top[:, n:],
                        st[margin : n - margin],
                        st[n - margin :] + bottom[:, n:],
                    ],
                    0,
                )
            )
        moved = half_roll(strips[1])
        to_high = jnp.where(front, strips[0], moved)
        to_low = jnp.where(front, moved, strips[0])
        send_e[s] = jnp.where(col_even, to_high, to_low)
        send_o[s] = jnp.where(col_even, to_low, to_high)


def fold_cols_kernel(total, e, o, out):
    col_even = lax.axis_index("col") % 2 == 0
    n = total.shape[1]
    h = n // 2
    front = iota((n, h), 1) < h // 2
    for s in range(2):
        high = jnp.where(col_even, e[s], o[s])
        low = jnp.where(col_even, o[s], e[s])
        for i in range(2):
            a = low if i == 0 else half_roll(low)
            b = high if i == 0 else half_roll(high)
            at = 2 * s + i
            out[at, :, :h] = total[at, :, :h] + jnp.where(front, a, 0.0)
            out[at, :, h:] = total[at, :, h:] + jnp.where(front, 0.0, b)


def in_hbm(x):
    return pltpu.with_memory_space_constraint(x, pltpu.HBM)


def call(kernel, shapes, in_specs, *args, scratch=(), mib=16):
    shapes = [s if isinstance(s, jax.ShapeDtypeStruct) else jax.ShapeDtypeStruct(s, F32) for s in shapes]
    return pl.pallas_call(
        kernel,
        out_shape=shapes,
        in_specs=in_specs,
        out_specs=[SMEM if s.shape == (1, 2) else VMEM for s in shapes],
        scratch_shapes=list(scratch),
        compiler_params=pltpu.CompilerParams(vmem_limit_bytes=mib << 20),
    )(*args)


def edges(axis):
    count = lax.axis_size(axis)
    rounds = []
    for first in (0, 1):
        pairs = [(i, i + 1) for i in range(first, count - 1, 2)]
        pairs += [(b, a) for a, b in pairs]
        if pairs:
            rounds.append(pairs)
    return rounds


def swap(value, axis, distance):
    count = lax.axis_size(axis)
    return lax.ppermute(value, axis, [(i, i ^ distance) for i in range(count)])


def groups():
    cols = [("col", 1 << b) for b in range(lax.axis_size("col").bit_length() - 1)]
    rows = [("row", 1 << b) for b in range(1, lax.axis_size("row").bit_length() - 1)]
    first, rest = cols[:2], cols[2:]
    pairs = [first]
    for bits in (rest, rows):
        pairs += [bits[i : i + 2] for i in range(0, len(bits), 2)]
    out = []
    for pair in pairs:
        axis, masks = pair[0][0], [m for _, m in pair]
        out.append((axis, [0] + masks + ([sum(masks)] if len(masks) == 2 else [])))
    return out


def pair_sum(parts):
    while len(parts) > 1:
        parts = [parts[i] + parts[i + 1] for i in range(0, len(parts), 2)]
    return parts[0]


def share_kernel(quad, stride, keep, other, *parts):
    place = lax.axis_index("col") // stride % quad
    chunk = keep.shape[0] // quad
    for j, part in enumerate(parts):
        rows = pl.ds(pl.multiple_of((place ^ j) * chunk, 8), chunk)
        part[...] = keep[rows, :] + other[rows, :]


def sum_kernel(*refs):
    refs[-1][...] = pair_sum([r[...] for r in refs[:-1]])


def join_kernel(stride, *refs):
    parts, full = refs[:-1], refs[-1]
    quad, chunk = len(parts), parts[0].shape[0]
    place = lax.axis_index("col") // stride % quad
    for j, part in enumerate(parts):
        full[pl.ds(pl.multiple_of((place ^ j) * chunk, 8), chunk), :] = part[...]


def half_kernel(full, out, sem):
    copy = pltpu.make_async_copy(full, out.at[lax.axis_index("row") % 2], sem)
    copy.start()
    copy.wait()


def other_kernel(started, other, out, sem):
    copy = pltpu.make_async_copy(other, out.at[1 - lax.axis_index("row") % 2], sem)
    copy.start()
    copy.wait()


def reduce_probe(keep, give):
    n = keep.shape[0]
    (_, offsets), *rest = groups()
    quad, stride = len(offsets), offsets[1]
    chunk = n // quad
    other = swap(give, "row", 1)
    parts = call(
        functools.partial(share_kernel, quad, stride),
        [(chunk, n)] * quad,
        [VMEM] * 2,
        keep,
        other,
    )
    sums = [parts[0]]
    for j in range(1, quad):
        sums.append(swap(parts[j], "col", offsets[j]))
    (total,) = call(sum_kernel, [(chunk, n)], [VMEM] * quad, *sums)
    for axis, masks in rest:
        sums = [total]
        for mask in masks[1:]:
            sums.append(swap(total, axis, mask))
        (total,) = call(sum_kernel, [(chunk, n)], [VMEM] * len(sums), *sums)
    parts = [total]
    for j in range(1, quad):
        parts.append(swap(total, "col", offsets[j]))
    (full,) = call(
        functools.partial(join_kernel, stride), [(n, n)], [VMEM] * quad, *parts
    )
    other = swap(full, "row", 1)
    out = dict(
        out_shape=jax.ShapeDtypeStruct((2, n, n), F32),
        out_specs=HBM,
        scratch_shapes=[pltpu.SemaphoreType.DMA(())],
        compiler_params=pltpu.CompilerParams(vmem_limit_bytes=16 << 20),
    )
    grad = pl.pallas_call(half_kernel, in_specs=[VMEM], **out)(full)
    return pl.pallas_call(
        other_kernel, in_specs=[HBM, VMEM], input_output_aliases={0: 0}, **out
    )(grad, other)


def whole(object_field, probe, phase, amplitudes, offsets):
    tile = object_field.shape[2]
    n = probe.shape[1]
    h = n // 2
    margin = n // 4
    mats, tw_left, tw_right = [jnp.asarray(t) for t in dft_constants(n)]

    row_rounds, col_rounds = edges("row"), edges("col")
    n_row = len(row_rounds)
    obj, even0, even1, odds, *rows = call(
        functools.partial(pack_kernel, margin),
        [(4, n, n)]
        + [(n + n // 2, h), (n // 2, h), (2, n, h)]
        + [(4, margin, n)] * n_row,
        [HBM],
        in_hbm(object_field.reshape(4, tile, tile)),
        scratch=[pltpu.SemaphoreType.DMA((2,))],
    )
    halos, corners = [], [[], []]
    even0 = lax.ppermute(even0, "col", col_rounds[0])
    odds = lax.ppermute(odds, "col", col_rounds[1])
    even1 = lax.ppermute(even1, "col", col_rounds[0])
    for i, pairs in enumerate(row_rounds):
        halos.append(lax.ppermute(rows[i], "row", pairs))
    evens = (even0, even1)

    def cut(s, after):
        parts = call(
            functools.partial(corner_kernel, s, margin),
            [(2, margin, h)] * n_row,
            [VMEM] * (3 + s),
            *evens[: s + 1],
            odds,
            after,
        )
        for i, pairs in enumerate(row_rounds):
            corners[s].append(lax.ppermute(parts[i], "row", pairs))

    def merge(s):
        (main,) = call(
            functools.partial(merge_kernel, s),
            [(2, n, n)],
            [VMEM] * (4 + s),
            obj,
            *evens[: s + 1],
            odds,
            limits,
        )
        return main

    loads = (phase, mats, tw_left, tw_right, probe, amplitudes.reshape(n, n))
    loads += (offsets.reshape(1, 2),)
    offs, limits, kr, ki, mats, tw_left, tw_right, pr, am = call(
        functools.partial(prep_kernel, margin),
        [jax.ShapeDtypeStruct((1, 2), jnp.int32), jax.ShapeDtypeStruct((2, 8, h), jnp.int32)]
        + [(n, n)] * 2
        + [jax.ShapeDtypeStruct((4, n, n), BF16)]
        + [jax.ShapeDtypeStruct(x.shape, x.dtype) for x in loads[2:-1]],
        [HBM] * len(loads),
        *[in_hbm(x) for x in loads],
        scratch=[
            pltpu.VMEM((n, n), F32),
            pltpu.VMEM((2, n, n), BF16),
            pltpu.SemaphoreType.DMA((len(loads),)),
        ],
    )
    (pr,) = call(functools.partial(roll_kernel, margin), [(2, n, n)], [SMEM, VMEM], offs, pr)
    (am,) = call(reorder_kernel, [(n, n)], [VMEM] * 2, am, pr)
    cut(0, am)
    main = merge(0)
    cut(1, main)
    w1, arrive = call(
        functools.partial(arrive_kernel, n_row, margin),
        [(2, n, n), (2, n, n)],
        [VMEM] * (8 + 2 * n_row),
        main,
        *halos,
        *corners[0],
        limits,
        pr,
        kr,
        ki,
        mats,
        tw_left,
        tw_right,
    )
    main = merge(1)
    keep, give, grads = call(
        functools.partial(back_kernel, n_row, margin),
        [(n, n), (n, n), (4, n, n)],
        [VMEM] * (2 + 2 * n_row) + [HBM] + [VMEM] * 9,
        main,
        *halos,
        *corners[1],
        limits,
        in_hbm(offsets.reshape(1, 2)),
        pr,
        kr,
        ki,
        am,
        w1,
        arrive,
        mats,
        tw_left,
        tw_right,
        scratch=[pltpu.SMEM((1, 2), jnp.int32), pltpu.SemaphoreType.DMA(())],
        mib=40,
    )
    probe_grad = reduce_probe(keep, give)
    own, strip, *sends = call(
        functools.partial(divide_kernel, margin),
        [(4, n, n), (4, n, h)] + [(4, margin, n + h)] * n_row,
        [VMEM, VMEM],
        grads,
        limits,
    )
    got = []
    for i, pairs in enumerate(row_rounds):
        got.append(lax.ppermute(sends[i], "row", pairs))
    total, send_e, send_o = call(
        functools.partial(fold_rows_kernel, n_row, margin),
        [(4, n, n), (2, n, h), (2, n, h)],
        [VMEM] * (2 + n_row),
        own,
        strip,
        *got,
    )
    send_e = lax.ppermute(send_e, "col", col_rounds[0])
    send_o = lax.ppermute(send_o, "col", col_rounds[1])
    (grad,) = call(fold_cols_kernel, [(4, n, n)], [VMEM] * 3, total, send_e, send_o)
    return (grad.reshape(2, 2, tile, tile), probe_grad)


def solution(mesh):
    placed = (
        P(None, None, "row", "col"),
        P(),
        P(),
        P("row", "col", None, None, None),
        P("row", "col", None, None),
    )
    return jax.shard_map(
        whole,
        mesh=mesh,
        in_specs=placed,
        out_specs=(P(None, None, "row", "col"), P()),
        check_vma=False,
    )
```

```python
import functools
import math

import jax
import jax.numpy as jnp
import numpy as np
from jax import lax
from jax.experimental import pallas as pl
from jax.experimental.pallas import tpu as pltpu
from jax.sharding import PartitionSpec as P


EPS_AMP = 0.5
F32 = jnp.float32
BF16 = jnp.bfloat16
VMEM = pl.BlockSpec(memory_space=pltpu.VMEM)
SMEM = pl.BlockSpec(memory_space=pltpu.SMEM)
HBM = pl.BlockSpec(memory_space=pltpu.HBM)


def split_np(table):
    high = table.astype(BF16)
    low = (table - high.astype(np.float64)).astype(BF16)
    return [high, low]


def dft_constants(n):
    h = n // 2
    k = np.arange(h)
    angle = 2.0 * np.pi * ((k[:, None] * k[None, :]) % h) / h
    scale = 1.0 / np.sqrt(n)
    c, s = np.cos(angle) * scale, np.sin(angle) * scale
    d = np.block([[c, s], [-s, c]])
    mats = np.stack(split_np(d))
    w = np.exp(-2j * np.pi * k / n)
    tw_left = np.stack([np.tile(w.real[:, None], (1, h)), np.tile(w.imag[:, None], (1, h))])
    tw_right = np.stack([np.tile(w.real[None], (8, 1)), np.tile(w.imag[None], (8, 1))])
    return mats, tw_left.astype(np.float32), tw_right.astype(np.float32)


def split(x):
    high = x.astype(BF16)
    return high, (x - high.astype(F32)).astype(BF16)


def dot(a, b):
    return jnp.dot(a, b, preferred_element_type=F32)


def left_dot(mats, which, x):
    high, low = split(x)
    return dot(mats[which], high) + (dot(mats[which], low) + dot(mats[which + 1], high))


def right_dot(x, mats, which):
    high, low = split(x)
    return dot(high, mats[which]) + (dot(low, mats[which]) + dot(high, mats[which + 1]))


def cat(parts, axis):
    return jnp.concatenate(parts, axis=axis)


def product(a, b):
    return (a[0] * b[0] - a[1] * b[1], a[0] * b[1] + a[1] * b[0])


def conj_product(a, b):
    return (a[0] * b[0] + a[1] * b[1], a[0] * b[1] - a[1] * b[0])


class Dft:
    def __init__(self, mats, tw_left, tw_right, n):
        self.mats, self.n, self.h = mats, n, n // 2
        self.tw_left, self.tw_right = tw_left, tw_right

    def wl(self, width):
        parts = width // self.tw_left.shape[2]
        return [cat([self.tw_left[i]] * parts, 1) for i in range(2)]

    def wr(self):
        return [self.tw_right[i, 0:1] for i in range(2)]

    def left(self, x):
        h, w = self.h, x[0].shape[1]
        total = [p[:h] + p[h:] for p in x]
        odd = product([p[:h] - p[h:] for p in x], self.wl(w))
        u = left_dot(self.mats, 0, cat(total, 0))
        v = left_dot(self.mats, 0, cat(odd, 0))
        return [cat([u[:h], v[:h]], 0), cat([u[h:], v[h:]], 0)]

    def right(self, x):
        h, m = self.h, x[0].shape[0]
        total = [p[:, :h] + p[:, h:] for p in x]
        odd = product([p[:, :h] - p[:, h:] for p in x], self.wr())
        u = right_dot(cat(total, 1), self.mats, 2)
        v = right_dot(cat(odd, 1), self.mats, 2)
        return [cat([u[:, :h], v[:, :h]], 1), cat([u[:, h:], v[:, h:]], 1)]

    def right_inverse(self, x):
        h, m = self.h, x[0].shape[0]
        u = right_dot(cat([p[:, :h] for p in x], 1), self.mats, 0)
        v = right_dot(cat([p[:, h:] for p in x], 1), self.mats, 0)
        even = [u[:, :h], u[:, h:]]
        odd = conj_product(self.wr(), [v[:, :h], v[:, h:]])
        return [cat([e + o, e - o], 1) for e, o in zip(even, odd)]

    def left_inverse(self, x):
        h, w = self.h, x[0].shape[1]
        u = left_dot(self.mats, 2, cat([p[:h] for p in x], 0))
        v = left_dot(self.mats, 2, cat([p[h:] for p in x], 0))
        even = [u[:h], u[h:]]
        odd = conj_product(self.wl(w), [v[:h], v[h:]])
        return [cat([e + o, e - o], 0) for e, o in zip(even, odd)]


SIN = [(-1.0) ** i / math.factorial(2 * i + 1) for i in range(7)]
COS = [(-1.0) ** i / math.factorial(2 * i) for i in range(7)]


def series(coefficients, z):
    total = coefficients[-1]
    for c in coefficients[-2::-1]:
        total = total * z + c
    return total


def cos_sin(x):
    y = 0.5 * x
    z = y * y
    s, c = y * series(SIN, z), series(COS, z)
    return 1.0 - 2.0 * (s * s), 2.0 * (s * c)


def iota(shape, dim):
    return lax.broadcasted_iota(jnp.int32, shape, dim)


def dyn_roll(x, shift, axis):
    return pltpu.roll(x, shift, axis=axis)


def half_roll(x):
    return pltpu.roll(x, x.shape[-1] // 2, axis=x.ndim - 1)


def pack_cols(re, im):
    h = re.shape[1] // 2
    front = iota((re.shape[0], h), 1) < h // 2
    low = jnp.where(front, re[:, :h], half_roll(im[:, :h]))
    high = jnp.where(front, half_roll(im[:, h:]), re[:, h:])
    return low, high


def copy_all(sources, places, sems):
    copies = [
        pltpu.make_async_copy(a, b, sems.at[i]) for i, (a, b) in enumerate(zip(sources, places))
    ]
    for copy in copies:
        copy.start()
    return copies


def row_start(which, n, margin):
    even = lax.axis_index("row") % 2 == 0
    last = even if which == 0 else jnp.logical_not(even)
    return pl.multiple_of(jnp.where(last, n - margin, 0), 8)


def pack_kernel(margin, obj_hbm, obj, *refs):
    evens, odds, rows, sems = refs[:2], refs[2], refs[3:-1], refs[-1]
    n = obj.shape[1]
    copies = copy_all((obj_hbm.at[0:2], obj_hbm.at[2:4]), (obj.at[0:2], obj.at[2:4]), sems)
    even = lax.axis_index("col") % 2 == 0
    for s in range(2):
        copies[s].wait()
        low, high = pack_cols(obj[2 * s], obj[2 * s + 1])
        strip = jnp.where(even, high, low)
        if s == 0:
            evens[0][:n] = strip
        else:
            evens[0][n:], evens[1][...] = strip[: n // 2], strip[n // 2 :]
        odds[s] = jnp.where(even, low, high)
    for which, out in enumerate(rows):
        out[...] = obj[:, pl.ds(row_start(which, n, margin), margin), :]


def corner_kernel(s, margin, *refs):
    evens, o, outs = refs[: s + 1], refs[s + 1], refs[s + 3 :]
    n = o.shape[1]
    for which, out in enumerate(outs):
        start = row_start(which, n, margin)
        if s == 0:
            out[0] = evens[0][pl.ds(start, margin), :]
        else:
            top, bottom = evens[0][n : n + margin], evens[1][n // 2 - margin :]
            out[0] = jnp.where(start == 0, top, bottom)
        out[1] = o[s, pl.ds(start, margin), :]


def even_odd(n, axis):
    h = n // 2
    natural, sorted_ = iota((n, n), axis), iota((n, n), 1 - axis)
    source = jnp.where(sorted_ < h, 2 * sorted_, 2 * (sorted_ - h) + 1)
    return (natural == source).astype(F32).astype(BF16)


def reorder(x, order):
    def thirds(y):
        a = y.astype(BF16)
        return (a,) + split(y - a.astype(F32))

    a, b, c = thirds(x)
    a, b, c = thirds(dot(order[1], a) + (dot(order[1], b) + dot(order[1], c)))
    return dot(a, order[0]) + (dot(b, order[0]) + dot(c, order[0]))


def prep_kernel(margin, *refs):
    hbm, (offs, limits, kr, ki, mats), loaded = refs[:7], refs[7:12], refs[12:16]
    phase, table, sems = refs[16:]
    n = phase.shape[0]
    h = n // 2
    first = pltpu.make_async_copy(hbm[0], phase, sems.at[0])
    first.start()
    order = [even_odd(n, axis) for axis in range(2)]
    first.wait()
    copies = copy_all(hbm[1:], (table,) + loaded + (offs,), sems)
    angle = reorder(phase[...], order)
    kr[...], ki[...] = cos_sin(angle)
    copies[0].wait()
    for i in range(2):
        mats[i] = table[i]
        mats[2 + i, :h, :h] = table[i, :h, :h]
        mats[2 + i, :h, h:] = -table[i, :h, h:]
        mats[2 + i, h:, :h] = -table[i, h:, :h]
        mats[2 + i, h:, h:] = table[i, h:, h:]
    for copy in copies[1:]:
        copy.wait()
    for i in range(2):
        limits[i] = jnp.full(limits.shape[1:], offs[0, i] - margin, jnp.int32)


def reorder_kernel(x, after, out):
    out[...] = reorder(x[...], [even_odd(x.shape[0], axis) for axis in range(2)])


def roll_back_kernel(margin, offs, x, out):
    n = x.shape[0]
    sy = (margin - offs[0, 0] + n) % n
    sx = (margin - offs[0, 1] + n) % n
    out[...] = dyn_roll(dyn_roll(x[...], sy, 0), sx, 1)


def roll_kernel(margin, offs, probe, pr):
    n = probe.shape[1]
    sy = (offs[0, 0] - margin + n) % n
    sx = (offs[0, 1] - margin + n) % n
    for i in range(2):
        pr[i] = dyn_roll(dyn_roll(probe[i], sy, 0), sx, 1)


def merge_cols(own, e, o, limits):
    n = own[0].shape[1]
    h = n // 2
    even = lax.axis_index("col") % 2 == 0
    high, low = jnp.where(even, e, o), jnp.where(even, o, e)
    lane = iota((1, h), 1)
    from_high = lane < limits[1, 0:1]
    from_low = lane >= limits[1, 0:1] + h
    out = []
    for i in range(2):
        strip_high = high if i == 0 else half_roll(high)
        strip_low = low if i == 0 else half_roll(low)
        out.append(
            cat(
                [
                    jnp.where(from_high, strip_high, own[i][:, :h]),
                    jnp.where(from_low, strip_low, own[i][:, h:]),
                ],
                1,
            )
        )
    return out


def merge_kernel(s, obj, *refs):
    evens, (o, limits, out) = refs[: s + 1], refs[s + 1 :]
    n = obj.shape[1]
    e = cat([evens[0][n:], evens[1][...]], 0) if s else evens[0][:n]
    own = [obj[2 * s], obj[2 * s + 1]]
    out[0], out[1] = merge_cols(own, e, o[s], limits)


def window_of(main, s, halos, corners, limits, margin):
    n = main.shape[1]
    row_even = lax.axis_index("row") % 2 == 0
    blocks = []
    for halo, corner in zip(halos, corners):
        own = [halo[2 * s], halo[2 * s + 1]]
        blocks.append(merge_cols(own, corner[0], corner[1], limits))
    row = iota((margin, n), 0)
    limit = cat([limits[0, 0:1]] * 2, 1)
    take_high = row < limit
    take_low = row >= limit + margin
    out = []
    for i in range(2):
        e = blocks[0][i]
        o = blocks[1][i] if len(blocks) == 2 else jnp.zeros_like(e)
        high, low = jnp.where(row_even, e, o), jnp.where(row_even, o, e)
        out.append(
            cat(
                [
                    jnp.where(take_high, high, main[i, :margin]),
                    main[i, margin : n - margin],
                    jnp.where(take_low, low, main[i, n - margin :]),
                ],
                0,
            )
        )
    return out


def unpack(n_row, refs):
    return refs[0], refs[1 : 1 + n_row], refs[1 + n_row : 1 + 2 * n_row], refs[1 + 2 * n_row :]


def through(dft, x, re, im):
    return dft.right_inverse(product([re, im], dft.right(x)))


def arrive_kernel(n_row, margin, *refs):
    main, halos, corners, refs = unpack(n_row, refs)
    limits, pr, kr, ki, mats, twl, twr, w1, arrive = refs
    n = main.shape[1]
    dft = Dft(mats, twl[...], twr[...], n)
    win = window_of(main, 0, halos, corners, limits, margin)
    w1[0], w1[1] = win
    x = dft.left(product([pr[0], pr[1]], win))
    x = through(dft, x, kr[...], ki[...])
    arrive[0], arrive[1] = dft.left_inverse(x)


def back_kernel(n_row, margin, *refs):
    main, halos, corners, refs = unpack(n_row, refs)
    limits, offs_hbm, pr, kr, ki, am, w1, arrive, mats, twl, twr = refs[:11]
    keep, give, grads, offs, sem = refs[11:]
    scalars = pltpu.make_async_copy(offs_hbm, offs, sem)
    scalars.start()
    n = main.shape[1]
    dft = Dft(mats, twl[...], twr[...], n)
    win = window_of(main, 1, halos, corners, limits, margin)
    x = dft.left(product([arrive[0], arrive[1]], win))
    far = dft.right(x)
    modulus = jnp.sqrt(far[0] * far[0] + far[1] * far[1] + EPS_AMP)
    factor = 2.0 * (1.0 - am[...] / modulus)
    x = dft.right_inverse([factor * far[0], factor * far[1]])
    back_far = dft.left_inverse(x)
    grads[2], grads[3] = conj_product([arrive[0], arrive[1]], back_far)
    x = dft.left(conj_product(win, back_far))
    x = through(dft, x, kr[...], -ki[...])
    x = dft.left_inverse(x)
    grads[0], grads[1] = conj_product([pr[0], pr[1]], x)
    grad = conj_product([w1[0], w1[1]], x)
    scalars.wait()
    sy = (margin - offs[0, 0] + n) % n
    sx = (margin - offs[0, 1] + n) % n
    even = lax.axis_index("row") % 2 == 0
    keep[...] = jnp.where(even, grad[0], grad[1])
    give[...] = dyn_roll(dyn_roll(jnp.where(even, grad[1], grad[0]), sy, 0), sx, 1)


def divide_kernel(margin, grads, limits, own, strip, *sends):
    for s in range(2):
        split_grad([grads[2 * s], grads[2 * s + 1]], s, limits, margin, own, strip, sends)


def split_grad(grad, s, limits, margin, own, strip, sends):
    n = grad[0].shape[0]
    h = n // 2
    row_even = lax.axis_index("row") % 2 == 0
    lane = iota((1, h), 1)
    to_high, to_low = lane < limits[1, 0:1], lane >= limits[1, 0:1] + h
    front = lane < h // 2
    spill = jnp.where(front, to_high.astype(jnp.int32), to_low.astype(jnp.int32)) != 0
    for i in range(2):
        g = grad[i]
        row = iota((n, h), 0)
        high_rows = row < limits[0, 0:1]
        low_rows = row >= limits[0, 0:1] + n
        inner = jnp.logical_not(jnp.logical_or(high_rows, low_rows))
        left = jnp.where(to_high, 0.0, g[:, :h])
        right = jnp.where(to_low, 0.0, g[:, h:])
        side = jnp.where(spill, jnp.where(front, g[:, :h], g[:, h:]), 0.0)
        pieces = [left, right, side]
        own[2 * s + i, :, :h] = jnp.where(inner, left, 0.0)
        own[2 * s + i, :, h:] = jnp.where(inner, right, 0.0)
        strip[2 * s + i] = jnp.where(inner, side, 0.0)
        for j, piece in enumerate(pieces):
            top = jnp.where(high_rows[:margin], piece[:margin], 0.0)
            bottom = jnp.where(low_rows[n - margin :], piece[n - margin :], 0.0)
            for which, send in enumerate(sends):
                first = row_even if which == 0 else jnp.logical_not(row_even)
                send[2 * s + i, :, j * h : (j + 1) * h] = jnp.where(first, top, bottom)


def fold_rows_kernel(n_row, margin, own, strip, *refs):
    got, (total, send_e, send_o) = refs[:n_row], refs[n_row:]
    row_even = lax.axis_index("row") % 2 == 0
    col_even = lax.axis_index("col") % 2 == 0
    n = own.shape[1]
    h = n // 2
    front = iota((n, h), 1) < h // 2
    for s in range(2):
        strips = []
        for i in range(2 * s, 2 * s + 2):
            total[i] = own[i]
            r = got[0][i]
            q = got[1][i] if n_row == 2 else jnp.zeros_like(r)
            top, bottom = jnp.where(row_even, q, r), jnp.where(row_even, r, q)
            total[i, :margin] += top[:, :n]
            total[i, n - margin :] += bottom[:, :n]
            st = strip[i]
            strips.append(
                cat(
                    [
                        st[:margin] + top[:, n:],
                        st[margin : n - margin],
                        st[n - margin :] + bottom[:, n:],
                    ],
                    0,
                )
            )
        moved = half_roll(strips[1])
        to_high = jnp.where(front, strips[0], moved)
        to_low = jnp.where(front, moved, strips[0])
        send_e[s] = jnp.where(col_even, to_high, to_low)
        send_o[s] = jnp.where(col_even, to_low, to_high)


def fold_cols_kernel(total, e, o, out):
    col_even = lax.axis_index("col") % 2 == 0
    n = total.shape[1]
    h = n // 2
    front = iota((n, h), 1) < h // 2
    for s in range(2):
        high = jnp.where(col_even, e[s], o[s])
        low = jnp.where(col_even, o[s], e[s])
        for i in range(2):
            a = low if i == 0 else half_roll(low)
            b = high if i == 0 else half_roll(high)
            at = 2 * s + i
            out[at, :, :h] = total[at, :, :h] + jnp.where(front, a, 0.0)
            out[at, :, h:] = total[at, :, h:] + jnp.where(front, 0.0, b)


def in_hbm(x):
    return pltpu.with_memory_space_constraint(x, pltpu.HBM)


def call(kernel, shapes, in_specs, *args, scratch=(), mib=16):
    shapes = [s if isinstance(s, jax.ShapeDtypeStruct) else jax.ShapeDtypeStruct(s, F32) for s in shapes]
    return pl.pallas_call(
        kernel,
        out_shape=shapes,
        in_specs=in_specs,
        out_specs=[SMEM if s.shape == (1, 2) else VMEM for s in shapes],
        scratch_shapes=list(scratch),
        compiler_params=pltpu.CompilerParams(vmem_limit_bytes=mib << 20),
    )(*args)


def edges(axis):
    count = lax.axis_size(axis)
    rounds = []
    for first in (0, 1):
        pairs = [(i, i + 1) for i in range(first, count - 1, 2)]
        pairs += [(b, a) for a, b in pairs]
        if pairs:
            rounds.append(pairs)
    return rounds


def swap(value, axis, distance):
    count = lax.axis_size(axis)
    return lax.ppermute(value, axis, [(i, i ^ distance) for i in range(count)])


def groups():
    cols = [("col", 1 << b) for b in range(lax.axis_size("col").bit_length() - 1)]
    rows = [("row", 1 << b) for b in range(1, lax.axis_size("row").bit_length() - 1)]
    first, rest = cols[:2], cols[2:]
    pairs = [first]
    for bits in (rest, rows):
        pairs += [bits[i : i + 2] for i in range(0, len(bits), 2)]
    out = []
    for pair in pairs:
        axis, masks = pair[0][0], [m for _, m in pair]
        out.append((axis, [0] + masks + ([sum(masks)] if len(masks) == 2 else [])))
    return out


def pair_sum(parts):
    while len(parts) > 1:
        parts = [parts[i] + parts[i + 1] for i in range(0, len(parts), 2)]
    return parts[0]


def share_kernel(quad, stride, keep, other, *parts):
    place = lax.axis_index("col") // stride % quad
    chunk = keep.shape[0] // quad
    for j, part in enumerate(parts):
        rows = pl.ds(pl.multiple_of((place ^ j) * chunk, 8), chunk)
        part[...] = keep[rows, :] + other[rows, :]


def sum_kernel(*refs):
    refs[-1][...] = pair_sum([r[...] for r in refs[:-1]])


def write_kernel(stride, quad, mine, others, started, *refs):
    parts, out, sems = refs[started:-2], refs[-2], refs[-1]
    half = lax.axis_index("row") % 2
    place = lax.axis_index("col") // stride % quad
    chunk = parts[0].shape[0]
    copies = []
    for i, (part, j) in enumerate(zip(parts, mine + others)):
        rows = pl.ds(pl.multiple_of((place ^ j) * chunk, 8), chunk)
        at = half if i < len(mine) else 1 - half
        copies.append(pltpu.make_async_copy(part, out.at[at, rows, :], sems.at[i]))
        copies[-1].start()
    for copy in copies:
        copy.wait()


def reduce_probe(keep, give):
    n = keep.shape[0]
    (_, offsets), *rest = groups()
    quad, stride = len(offsets), offsets[1]
    chunk = n // quad
    other = swap(give, "row", 1)
    parts = call(
        functools.partial(share_kernel, quad, stride),
        [(chunk, n)] * quad,
        [VMEM] * 2,
        keep,
        other,
    )
    sums = [parts[0]]
    for j in range(1, quad):
        sums.append(swap(parts[j], "col", offsets[j]))
    (total,) = call(sum_kernel, [(chunk, n)], [VMEM] * quad, *sums)
    for axis, masks in rest:
        sums = [total]
        for mask in masks[1:]:
            sums.append(swap(total, axis, mask))
        (total,) = call(sum_kernel, [(chunk, n)], [VMEM] * len(sums), *sums)
    parts, others = {0: total}, {}
    for j in range(1, quad):
        parts[j] = swap(total, "col", offsets[j])
    for j in range(quad):
        others[j] = swap(parts[j], "row", 1)

    def write(mine, theirs, *started):
        count = len(mine) + len(theirs)
        return pl.pallas_call(
            functools.partial(write_kernel, stride, quad, mine, theirs, len(started)),
            out_shape=jax.ShapeDtypeStruct((2, n, n), F32),
            in_specs=[HBM] * len(started) + [VMEM] * count,
            out_specs=HBM,
            scratch_shapes=[pltpu.SemaphoreType.DMA((count,))],
            input_output_aliases={0: 0} if started else {},
            compiler_params=pltpu.CompilerParams(vmem_limit_bytes=16 << 20),
        )(*started, *[parts[j] for j in mine], *[others[j] for j in theirs])

    order = [0] + list(range(quad - 1, 0, -1))
    grad = write(order, order[:-1])
    return write([], order[-1:], grad)


def whole(object_field, probe, phase, amplitudes, offsets):
    tile = object_field.shape[2]
    n = probe.shape[1]
    h = n // 2
    margin = n // 4
    mats, tw_left, tw_right = [jnp.asarray(t) for t in dft_constants(n)]

    row_rounds, col_rounds = edges("row"), edges("col")
    n_row = len(row_rounds)
    obj, even0, even1, odds, *rows = call(
        functools.partial(pack_kernel, margin),
        [(4, n, n)]
        + [(n + n // 2, h), (n // 2, h), (2, n, h)]
        + [(4, margin, n)] * n_row,
        [HBM],
        in_hbm(object_field.reshape(4, tile, tile)),
        scratch=[pltpu.SemaphoreType.DMA((2,))],
    )
    halos, corners = [], [[], []]
    even0 = lax.ppermute(even0, "col", col_rounds[0])
    odds = lax.ppermute(odds, "col", col_rounds[1])
    even1 = lax.ppermute(even1, "col", col_rounds[0])
    for i, pairs in enumerate(row_rounds):
        halos.append(lax.ppermute(rows[i], "row", pairs))
    evens = (even0, even1)

    def cut(s, after):
        parts = call(
            functools.partial(corner_kernel, s, margin),
            [(2, margin, h)] * n_row,
            [VMEM] * (3 + s),
            *evens[: s + 1],
            odds,
            after,
        )
        for i, pairs in enumerate(row_rounds):
            corners[s].append(lax.ppermute(parts[i], "row", pairs))

    def merge(s):
        (main,) = call(
            functools.partial(merge_kernel, s),
            [(2, n, n)],
            [VMEM] * (4 + s),
            obj,
            *evens[: s + 1],
            odds,
            limits,
        )
        return main

    loads = (phase, mats, tw_left, tw_right, probe, amplitudes.reshape(n, n))
    loads += (offsets.reshape(1, 2),)
    offs, limits, kr, ki, mats, tw_left, tw_right, pr, am = call(
        functools.partial(prep_kernel, margin),
        [jax.ShapeDtypeStruct((1, 2), jnp.int32), jax.ShapeDtypeStruct((2, 8, h), jnp.int32)]
        + [(n, n)] * 2
        + [jax.ShapeDtypeStruct((4, n, n), BF16)]
        + [jax.ShapeDtypeStruct(x.shape, x.dtype) for x in loads[2:-1]],
        [HBM] * len(loads),
        *[in_hbm(x) for x in loads],
        scratch=[
            pltpu.VMEM((n, n), F32),
            pltpu.VMEM((2, n, n), BF16),
            pltpu.SemaphoreType.DMA((len(loads),)),
        ],
    )
    (pr,) = call(functools.partial(roll_kernel, margin), [(2, n, n)], [SMEM, VMEM], offs, pr)
    (am,) = call(reorder_kernel, [(n, n)], [VMEM] * 2, am, pr)
    cut(0, am)
    main = merge(0)
    cut(1, main)
    w1, arrive = call(
        functools.partial(arrive_kernel, n_row, margin),
        [(2, n, n), (2, n, n)],
        [VMEM] * (8 + 2 * n_row),
        main,
        *halos,
        *corners[0],
        limits,
        pr,
        kr,
        ki,
        mats,
        tw_left,
        tw_right,
    )
    main = merge(1)
    keep, give, grads = call(
        functools.partial(back_kernel, n_row, margin),
        [(n, n), (n, n), (4, n, n)],
        [VMEM] * (2 + 2 * n_row) + [HBM] + [VMEM] * 9,
        main,
        *halos,
        *corners[1],
        limits,
        in_hbm(offsets.reshape(1, 2)),
        pr,
        kr,
        ki,
        am,
        w1,
        arrive,
        mats,
        tw_left,
        tw_right,
        scratch=[pltpu.SMEM((1, 2), jnp.int32), pltpu.SemaphoreType.DMA(())],
        mib=40,
    )
    (keep,) = call(functools.partial(roll_back_kernel, margin), [(n, n)], [SMEM, VMEM], offs, keep)
    probe_grad = reduce_probe(keep, give)
    own, strip, *sends = call(
        functools.partial(divide_kernel, margin),
        [(4, n, n), (4, n, h)] + [(4, margin, n + h)] * n_row,
        [VMEM, VMEM],
        grads,
        limits,
    )
    got = []
    for i, pairs in enumerate(row_rounds):
        got.append(lax.ppermute(sends[i], "row", pairs))
    total, send_e, send_o = call(
        functools.partial(fold_rows_kernel, n_row, margin),
        [(4, n, n), (2, n, h), (2, n, h)],
        [VMEM] * (2 + n_row),
        own,
        strip,
        *got,
    )
    send_e = lax.ppermute(send_e, "col", col_rounds[0])
    send_o = lax.ppermute(send_o, "col", col_rounds[1])
    (grad,) = call(fold_cols_kernel, [(4, n, n)], [VMEM] * 3, total, send_e, send_o)
    return (grad.reshape(2, 2, tile, tile), probe_grad)


def solution(mesh):
    placed = (
        P(None, None, "row", "col"),
        P(),
        P(),
        P("row", "col", None, None, None),
        P("row", "col", None, None),
    )
    return jax.shard_map(
        whole,
        mesh=mesh,
        in_specs=placed,
        out_specs=(P(None, None, "row", "col"), P()),
        check_vma=False,
    )
```

```python
import functools
import math

import jax
import jax.numpy as jnp
import numpy as np
from jax import lax
from jax.experimental import pallas as pl
from jax.experimental.pallas import tpu as pltpu
from jax.sharding import PartitionSpec as P


EPS_AMP = 0.5
F32 = jnp.float32
BF16 = jnp.bfloat16
VMEM = pl.BlockSpec(memory_space=pltpu.VMEM)
SMEM = pl.BlockSpec(memory_space=pltpu.SMEM)
HBM = pl.BlockSpec(memory_space=pltpu.HBM)


def split_np(table):
    high = table.astype(BF16)
    low = (table - high.astype(np.float64)).astype(BF16)
    return [high, low]


def dft_constants(n):
    h = n // 2
    k = np.arange(h)
    even = np.exp(-2j * np.pi * ((k[:, None] * k[None, :]) % h) / h) / np.sqrt(n)
    odd = even * np.exp(-2j * np.pi * k / n)[None, :]
    real = [np.block([[m.real, -m.imag], [m.imag, m.real]]) for m in (even, odd)]
    return np.stack(split_np(real[0])), np.stack(split_np(real[1]) + split_np(real[1].T))


def split(x):
    high = x.astype(BF16)
    return high, (x - high.astype(F32)).astype(BF16)


def dot(a, b):
    return jnp.dot(a, b, preferred_element_type=F32)


def left_dot(mats, which, x):
    high, low = split(x)
    return dot(mats[which], high) + (dot(mats[which], low) + dot(mats[which + 1], high))


def right_dot(x, mats, which):
    high, low = split(x)
    return dot(high, mats[which]) + (dot(low, mats[which]) + dot(high, mats[which + 1]))


def cat(parts, axis):
    return jnp.concatenate(parts, axis=axis)


def product(a, b):
    return (a[0] * b[0] - a[1] * b[1], a[0] * b[1] + a[1] * b[0])


def conj_product(a, b):
    return (a[0] * b[0] + a[1] * b[1], a[0] * b[1] - a[1] * b[0])


class Dft:
    def __init__(self, mats, n):
        self.mats, self.h = mats, n // 2

    def left(self, x):
        h = self.h
        u = left_dot(self.mats, 0, cat([p[:h] + p[h:] for p in x], 0))
        v = left_dot(self.mats, 4, cat([p[:h] - p[h:] for p in x], 0))
        return [cat([u[:h], v[:h]], 0), cat([u[h:], v[h:]], 0)]

    def right(self, x):
        h = self.h
        u = right_dot(cat([p[:, :h] + p[:, h:] for p in x], 1), self.mats, 2)
        v = right_dot(cat([p[:, :h] - p[:, h:] for p in x], 1), self.mats, 6)
        return [cat([u[:, :h], v[:, :h]], 1), cat([u[:, h:], v[:, h:]], 1)]

    def right_inverse(self, x):
        h = self.h
        u = right_dot(cat([p[:, :h] for p in x], 1), self.mats, 0)
        v = right_dot(cat([p[:, h:] for p in x], 1), self.mats, 4)
        return [cat([e + o, e - o], 1) for e, o in ((u[:, :h], v[:, :h]), (u[:, h:], v[:, h:]))]

    def left_inverse(self, x):
        h = self.h
        u = left_dot(self.mats, 2, cat([p[:h] for p in x], 0))
        v = left_dot(self.mats, 6, cat([p[h:] for p in x], 0))
        return [cat([e + o, e - o], 0) for e, o in ((u[:h], v[:h]), (u[h:], v[h:]))]


SIN = [(-1.0) ** i / math.factorial(2 * i + 1) for i in range(7)]
COS = [(-1.0) ** i / math.factorial(2 * i) for i in range(7)]


def series(coefficients, z):
    total = coefficients[-1]
    for c in coefficients[-2::-1]:
        total = total * z + c
    return total


def cos_sin(x):
    y = 0.5 * x
    z = y * y
    s, c = y * series(SIN, z), series(COS, z)
    return 1.0 - 2.0 * (s * s), 2.0 * (s * c)


def iota(shape, dim):
    return lax.broadcasted_iota(jnp.int32, shape, dim)


def dyn_roll(x, shift, axis):
    return pltpu.roll(x, shift, axis=axis)


def half_roll(x):
    return pltpu.roll(x, x.shape[-1] // 2, axis=x.ndim - 1)


def pack_cols(re, im):
    h = re.shape[1] // 2
    front = iota((re.shape[0], h), 1) < h // 2
    low = jnp.where(front, re[:, :h], half_roll(im[:, :h]))
    high = jnp.where(front, half_roll(im[:, h:]), re[:, h:])
    return low, high


def copy_all(sources, places, sems):
    copies = [
        pltpu.make_async_copy(a, b, sems.at[i]) for i, (a, b) in enumerate(zip(sources, places))
    ]
    for copy in copies:
        copy.start()
    return copies


def row_start(which, n, margin):
    even = lax.axis_index("row") % 2 == 0
    last = even if which == 0 else jnp.logical_not(even)
    return pl.multiple_of(jnp.where(last, n - margin, 0), 8)


def pack_kernel(margin, obj_hbm, obj, *refs):
    evens, odds, rows, sems = refs[:2], refs[2], refs[3:-1], refs[-1]
    n = obj.shape[1]
    copies = copy_all((obj_hbm.at[0:2], obj_hbm.at[2:4]), (obj.at[0:2], obj.at[2:4]), sems)
    even = lax.axis_index("col") % 2 == 0
    for s in range(2):
        copies[s].wait()
        low, high = pack_cols(obj[2 * s], obj[2 * s + 1])
        strip = jnp.where(even, high, low)
        if s == 0:
            evens[0][:n] = strip
        else:
            evens[0][n:], evens[1][...] = strip[: n // 2], strip[n // 2 :]
        odds[s] = jnp.where(even, low, high)
    for which, out in enumerate(rows):
        out[...] = obj[:, pl.ds(row_start(which, n, margin), margin), :]


def corner_kernel(s, margin, *refs):
    evens, o, outs = refs[: s + 1], refs[s + 1], refs[s + 3 :]
    n = o.shape[1]
    for which, out in enumerate(outs):
        start = row_start(which, n, margin)
        if s == 0:
            out[0] = evens[0][pl.ds(start, margin), :]
        else:
            top, bottom = evens[0][n : n + margin], evens[1][n // 2 - margin :]
            out[0] = jnp.where(start == 0, top, bottom)
        out[1] = o[s, pl.ds(start, margin), :]


def even_odd(n, axis):
    h = n // 2
    natural, sorted_ = iota((n, n), axis), iota((n, n), 1 - axis)
    source = jnp.where(sorted_ < h, 2 * sorted_, 2 * (sorted_ - h) + 1)
    return (natural == source).astype(F32).astype(BF16)


def reorder(x, order):
    def thirds(y):
        a = y.astype(BF16)
        return (a,) + split(y - a.astype(F32))

    a, b, c = thirds(x)
    a, b, c = thirds(dot(order[1], a) + (dot(order[1], b) + dot(order[1], c)))
    return dot(a, order[0]) + (dot(b, order[0]) + dot(c, order[0]))


def prep_kernel(margin, *refs):
    hbm, (offs, limits, kr, ki, mats, *loaded) = refs[:6], refs[6:13]
    phase, table, sems = refs[13:]
    n = phase.shape[0]
    h = n // 2
    first = pltpu.make_async_copy(hbm[0], phase, sems.at[0])
    first.start()
    order = [even_odd(n, axis) for axis in range(2)]
    first.wait()
    copies = copy_all(hbm[1:], (table, mats.at[4:8], *loaded, offs), sems)
    angle = reorder(phase[...], order)
    kr[...], ki[...] = cos_sin(angle)
    copies[0].wait()
    for i in range(2):
        mats[i] = table[i]
        mats[2 + i, :h, :h] = table[i, :h, :h]
        mats[2 + i, :h, h:] = -table[i, :h, h:]
        mats[2 + i, h:, :h] = -table[i, h:, :h]
        mats[2 + i, h:, h:] = table[i, h:, h:]
    for copy in copies[1:]:
        copy.wait()
    for i in range(2):
        limits[i] = jnp.full(limits.shape[1:], offs[0, i] - margin, jnp.int32)


def reorder_kernel(x, after, out):
    out[...] = reorder(x[...], [even_odd(x.shape[0], axis) for axis in range(2)])


def roll_kernel(margin, offs, probe, pr):
    n = probe.shape[1]
    sy = (offs[0, 0] - margin + n) % n
    sx = (offs[0, 1] - margin + n) % n
    for i in range(2):
        pr[i] = dyn_roll(dyn_roll(probe[i], sy, 0), sx, 1)


def merge_cols(own, e, o, limits):
    n = own[0].shape[1]
    h = n // 2
    even = lax.axis_index("col") % 2 == 0
    high, low = jnp.where(even, e, o), jnp.where(even, o, e)
    lane = iota((1, h), 1)
    from_high = lane < limits[1, 0:1]
    from_low = lane >= limits[1, 0:1] + h
    out = []
    for i in range(2):
        strip_high = high if i == 0 else half_roll(high)
        strip_low = low if i == 0 else half_roll(low)
        out.append(
            cat(
                [
                    jnp.where(from_high, strip_high, own[i][:, :h]),
                    jnp.where(from_low, strip_low, own[i][:, h:]),
                ],
                1,
            )
        )
    return out


def merge_kernel(s, obj, *refs):
    evens, (o, limits, out) = refs[: s + 1], refs[s + 1 :]
    n = obj.shape[1]
    e = cat([evens[0][n:], evens[1][...]], 0) if s else evens[0][:n]
    own = [obj[2 * s], obj[2 * s + 1]]
    out[0], out[1] = merge_cols(own, e, o[s], limits)


def window_of(main, s, halos, corners, limits, margin):
    n = main.shape[1]
    row_even = lax.axis_index("row") % 2 == 0
    blocks = []
    for halo, corner in zip(halos, corners):
        own = [halo[2 * s], halo[2 * s + 1]]
        blocks.append(merge_cols(own, corner[0], corner[1], limits))
    row = iota((margin, n), 0)
    limit = cat([limits[0, 0:1]] * 2, 1)
    take_high = row < limit
    take_low = row >= limit + margin
    out = []
    for i in range(2):
        e = blocks[0][i]
        o = blocks[1][i] if len(blocks) == 2 else jnp.zeros_like(e)
        high, low = jnp.where(row_even, e, o), jnp.where(row_even, o, e)
        out.append(
            cat(
                [
                    jnp.where(take_high, high, main[i, :margin]),
                    main[i, margin : n - margin],
                    jnp.where(take_low, low, main[i, n - margin :]),
                ],
                0,
            )
        )
    return out


def unpack(n_row, refs):
    return refs[0], refs[1 : 1 + n_row], refs[1 + n_row : 1 + 2 * n_row], refs[1 + 2 * n_row :]


def through(dft, x, re, im):
    return dft.right_inverse(product([re, im], dft.right(x)))


def arrive_kernel(n_row, margin, *refs):
    main, halos, corners, refs = unpack(n_row, refs)
    limits, pr, kr, ki, mats, w1, arrive = refs
    n = main.shape[1]
    dft = Dft(mats, n)
    win = window_of(main, 0, halos, corners, limits, margin)
    w1[0], w1[1] = win
    x = dft.left(product([pr[0], pr[1]], win))
    x = through(dft, x, kr[...], ki[...])
    arrive[0], arrive[1] = dft.left_inverse(x)


def back_kernel(n_row, margin, *refs):
    main, halos, corners, refs = unpack(n_row, refs)
    limits, offs_hbm, pr, kr, ki, am, w1, arrive, mats = refs[:9]
    keep, give, grads, offs, sem = refs[9:]
    scalars = pltpu.make_async_copy(offs_hbm, offs, sem)
    scalars.start()
    n = main.shape[1]
    dft = Dft(mats, n)
    win = window_of(main, 1, halos, corners, limits, margin)
    x = dft.left(product([arrive[0], arrive[1]], win))
    far = dft.right(x)
    modulus = jnp.sqrt(far[0] * far[0] + far[1] * far[1] + EPS_AMP)
    factor = 2.0 * (1.0 - am[...] / modulus)
    x = dft.right_inverse([factor * far[0], factor * far[1]])
    back_far = dft.left_inverse(x)
    grads[2], grads[3] = conj_product([arrive[0], arrive[1]], back_far)
    x = dft.left(conj_product(win, back_far))
    x = through(dft, x, kr[...], -ki[...])
    x = dft.left_inverse(x)
    grads[0], grads[1] = conj_product([pr[0], pr[1]], x)
    grad = conj_product([w1[0], w1[1]], x)
    scalars.wait()
    sy = (margin - offs[0, 0] + n) % n
    sx = (margin - offs[0, 1] + n) % n
    grad = [dyn_roll(dyn_roll(g, sy, 0), sx, 1) for g in grad]
    even = lax.axis_index("row") % 2 == 0
    keep[...] = jnp.where(even, grad[0], grad[1])
    give[...] = jnp.where(even, grad[1], grad[0])


def divide_kernel(margin, grads, limits, own, strip, *sends):
    for s in range(2):
        split_grad([grads[2 * s], grads[2 * s + 1]], s, limits, margin, own, strip, sends)


def split_grad(grad, s, limits, margin, own, strip, sends):
    n = grad[0].shape[0]
    h = n // 2
    row_even = lax.axis_index("row") % 2 == 0
    lane = iota((1, h), 1)
    to_high, to_low = lane < limits[1, 0:1], lane >= limits[1, 0:1] + h
    front = lane < h // 2
    spill = jnp.where(front, to_high.astype(jnp.int32), to_low.astype(jnp.int32)) != 0
    for i in range(2):
        g = grad[i]
        row = iota((n, h), 0)
        high_rows = row < limits[0, 0:1]
        low_rows = row >= limits[0, 0:1] + n
        inner = jnp.logical_not(jnp.logical_or(high_rows, low_rows))
        left = jnp.where(to_high, 0.0, g[:, :h])
        right = jnp.where(to_low, 0.0, g[:, h:])
        side = jnp.where(spill, jnp.where(front, g[:, :h], g[:, h:]), 0.0)
        pieces = [left, right, side]
        own[2 * s + i, :, :h] = jnp.where(inner, left, 0.0)
        own[2 * s + i, :, h:] = jnp.where(inner, right, 0.0)
        strip[2 * s + i] = jnp.where(inner, side, 0.0)
        for j, piece in enumerate(pieces):
            top = jnp.where(high_rows[:margin], piece[:margin], 0.0)
            bottom = jnp.where(low_rows[n - margin :], piece[n - margin :], 0.0)
            for which, send in enumerate(sends):
                first = row_even if which == 0 else jnp.logical_not(row_even)
                send[2 * s + i, :, j * h : (j + 1) * h] = jnp.where(first, top, bottom)


def fold_rows_kernel(n_row, margin, own, strip, *refs):
    got, (total, send_e, send_o) = refs[:n_row], refs[n_row:]
    row_even = lax.axis_index("row") % 2 == 0
    col_even = lax.axis_index("col") % 2 == 0
    n = own.shape[1]
    h = n // 2
    front = iota((n, h), 1) < h // 2
    for s in range(2):
        strips = []
        for i in range(2 * s, 2 * s + 2):
            total[i] = own[i]
            r = got[0][i]
            q = got[1][i] if n_row == 2 else jnp.zeros_like(r)
            top, bottom = jnp.where(row_even, q, r), jnp.where(row_even, r, q)
            total[i, :margin] += top[:, :n]
            total[i, n - margin :] += bottom[:, :n]
            st = strip[i]
            strips.append(
                cat(
                    [
                        st[:margin] + top[:, n:],
                        st[margin : n - margin],
                        st[n - margin :] + bottom[:, n:],
                    ],
                    0,
                )
            )
        moved = half_roll(strips[1])
        to_high = jnp.where(front, strips[0], moved)
        to_low = jnp.where(front, moved, strips[0])
        send_e[s] = jnp.where(col_even, to_high, to_low)
        send_o[s] = jnp.where(col_even, to_low, to_high)


def fold_cols_kernel(total, e, o, out):
    col_even = lax.axis_index("col") % 2 == 0
    n = total.shape[1]
    h = n // 2
    front = iota((n, h), 1) < h // 2
    for s in range(2):
        high = jnp.where(col_even, e[s], o[s])
        low = jnp.where(col_even, o[s], e[s])
        for i in range(2):
            a = low if i == 0 else half_roll(low)
            b = high if i == 0 else half_roll(high)
            at = 2 * s + i
            out[at, :, :h] = total[at, :, :h] + jnp.where(front, a, 0.0)
            out[at, :, h:] = total[at, :, h:] + jnp.where(front, 0.0, b)


def in_hbm(x):
    return pltpu.with_memory_space_constraint(x, pltpu.HBM)


def call(kernel, shapes, in_specs, *args, scratch=(), mib=16):
    shapes = [s if isinstance(s, jax.ShapeDtypeStruct) else jax.ShapeDtypeStruct(s, F32) for s in shapes]
    return pl.pallas_call(
        kernel,
        out_shape=shapes,
        in_specs=in_specs,
        out_specs=[SMEM if s.shape == (1, 2) else VMEM for s in shapes],
        scratch_shapes=list(scratch),
        compiler_params=pltpu.CompilerParams(vmem_limit_bytes=mib << 20),
    )(*args)


def edges(axis):
    count = lax.axis_size(axis)
    rounds = []
    for first in (0, 1):
        pairs = [(i, i + 1) for i in range(first, count - 1, 2)]
        pairs += [(b, a) for a, b in pairs]
        if pairs:
            rounds.append(pairs)
    return rounds


def swap(value, axis, distance):
    count = lax.axis_size(axis)
    return lax.ppermute(value, axis, [(i, i ^ distance) for i in range(count)])


def groups():
    cols = [("col", 1 << b) for b in range(lax.axis_size("col").bit_length() - 1)]
    rows = [("row", 1 << b) for b in range(1, lax.axis_size("row").bit_length() - 1)]
    first, rest = cols[:2], cols[2:]
    pairs = [first]
    for bits in (rest, rows):
        pairs += [bits[i : i + 2] for i in range(0, len(bits), 2)]
    out = []
    for pair in pairs:
        axis, masks = pair[0][0], [m for _, m in pair]
        out.append((axis, [0] + masks + ([sum(masks)] if len(masks) == 2 else [])))
    return out


def pair_sum(parts):
    while len(parts) > 1:
        parts = [parts[i] + parts[i + 1] for i in range(0, len(parts), 2)]
    return parts[0]


def share_kernel(quad, stride, keep, other, *parts):
    place = lax.axis_index("col") // stride % quad
    chunk = keep.shape[0] // quad
    for j, part in enumerate(parts):
        rows = pl.ds(pl.multiple_of((place ^ j) * chunk, 8), chunk)
        part[...] = keep[rows, :] + other[rows, :]


def sum_kernel(*refs):
    refs[-1][...] = pair_sum([r[...] for r in refs[:-1]])


def join_kernel(stride, *refs):
    parts, full = refs[:-1], refs[-1]
    quad, chunk = len(parts), parts[0].shape[0]
    place = lax.axis_index("col") // stride % quad
    for j, part in enumerate(parts):
        full[pl.ds(pl.multiple_of((place ^ j) * chunk, 8), chunk), :] = part[...]


def half_kernel(full, out, sem):
    copy = pltpu.make_async_copy(full, out.at[lax.axis_index("row") % 2], sem)
    copy.start()
    copy.wait()


def other_kernel(started, other, out, sem):
    copy = pltpu.make_async_copy(other, out.at[1 - lax.axis_index("row") % 2], sem)
    copy.start()
    copy.wait()


def reduce_probe(keep, give):
    n = keep.shape[0]
    (_, offsets), *rest = groups()
    quad, stride = len(offsets), offsets[1]
    chunk = n // quad
    other = swap(give, "row", 1)
    parts = call(
        functools.partial(share_kernel, quad, stride),
        [(chunk, n)] * quad,
        [VMEM] * 2,
        keep,
        other,
    )
    sums = [parts[0]]
    for j in range(1, quad):
        sums.append(swap(parts[j], "col", offsets[j]))
    (total,) = call(sum_kernel, [(chunk, n)], [VMEM] * quad, *sums)
    for axis, masks in rest:
        sums = [total]
        for mask in masks[1:]:
            sums.append(swap(total, axis, mask))
        (total,) = call(sum_kernel, [(chunk, n)], [VMEM] * len(sums), *sums)
    parts = [total]
    for j in range(1, quad):
        parts.append(swap(total, "col", offsets[j]))
    (full,) = call(
        functools.partial(join_kernel, stride), [(n, n)], [VMEM] * quad, *parts
    )
    other = swap(full, "row", 1)
    out = dict(
        out_shape=jax.ShapeDtypeStruct((2, n, n), F32),
        out_specs=HBM,
        scratch_shapes=[pltpu.SemaphoreType.DMA(())],
        compiler_params=pltpu.CompilerParams(vmem_limit_bytes=16 << 20),
    )
    grad = pl.pallas_call(half_kernel, in_specs=[VMEM], **out)(full)
    return pl.pallas_call(
        other_kernel, in_specs=[HBM, VMEM], input_output_aliases={0: 0}, **out
    )(grad, other)


def whole(object_field, probe, phase, amplitudes, offsets):
    tile = object_field.shape[2]
    n = probe.shape[1]
    h = n // 2
    margin = n // 4
    even, odd = [jnp.asarray(t) for t in dft_constants(n)]

    row_rounds, col_rounds = edges("row"), edges("col")
    n_row = len(row_rounds)
    obj, even0, even1, odds, *rows = call(
        functools.partial(pack_kernel, margin),
        [(4, n, n)]
        + [(n + n // 2, h), (n // 2, h), (2, n, h)]
        + [(4, margin, n)] * n_row,
        [HBM],
        in_hbm(object_field.reshape(4, tile, tile)),
        scratch=[pltpu.SemaphoreType.DMA((2,))],
    )
    halos, corners = [], [[], []]
    even0 = lax.ppermute(even0, "col", col_rounds[0])
    odds = lax.ppermute(odds, "col", col_rounds[1])
    even1 = lax.ppermute(even1, "col", col_rounds[0])
    for i, pairs in enumerate(row_rounds):
        halos.append(lax.ppermute(rows[i], "row", pairs))
    evens = (even0, even1)

    def cut(s, after):
        parts = call(
            functools.partial(corner_kernel, s, margin),
            [(2, margin, h)] * n_row,
            [VMEM] * (3 + s),
            *evens[: s + 1],
            odds,
            after,
        )
        for i, pairs in enumerate(row_rounds):
            corners[s].append(lax.ppermute(parts[i], "row", pairs))

    def merge(s):
        (main,) = call(
            functools.partial(merge_kernel, s),
            [(2, n, n)],
            [VMEM] * (4 + s),
            obj,
            *evens[: s + 1],
            odds,
            limits,
        )
        return main

    loads = (phase, even, odd, probe, amplitudes.reshape(n, n), offsets.reshape(1, 2))
    offs, limits, kr, ki, mats, pr, am = call(
        functools.partial(prep_kernel, margin),
        [jax.ShapeDtypeStruct((1, 2), jnp.int32), jax.ShapeDtypeStruct((2, 8, h), jnp.int32)]
        + [(n, n)] * 2
        + [jax.ShapeDtypeStruct((8, n, n), BF16)]
        + [jax.ShapeDtypeStruct(x.shape, x.dtype) for x in loads[3:-1]],
        [HBM] * len(loads),
        *[in_hbm(x) for x in loads],
        scratch=[
            pltpu.VMEM((n, n), F32),
            pltpu.VMEM((2, n, n), BF16),
            pltpu.SemaphoreType.DMA((len(loads),)),
        ],
    )
    (pr,) = call(functools.partial(roll_kernel, margin), [(2, n, n)], [SMEM, VMEM], offs, pr)
    (am,) = call(reorder_kernel, [(n, n)], [VMEM] * 2, am, pr)
    cut(0, am)
    main = merge(0)
    cut(1, main)
    w1, arrive = call(
        functools.partial(arrive_kernel, n_row, margin),
        [(2, n, n), (2, n, n)],
        [VMEM] * (6 + 2 * n_row),
        main,
        *halos,
        *corners[0],
        limits,
        pr,
        kr,
        ki,
        mats,
    )
    main = merge(1)
    keep, give, grads = call(
        functools.partial(back_kernel, n_row, margin),
        [(n, n), (n, n), (4, n, n)],
        [VMEM] * (2 + 2 * n_row) + [HBM] + [VMEM] * 7,
        main,
        *halos,
        *corners[1],
        limits,
        in_hbm(offsets.reshape(1, 2)),
        pr,
        kr,
        ki,
        am,
        w1,
        arrive,
        mats,
        scratch=[pltpu.SMEM((1, 2), jnp.int32), pltpu.SemaphoreType.DMA(())],
        mib=40,
    )
    probe_grad = reduce_probe(keep, give)
    own, strip, *sends = call(
        functools.partial(divide_kernel, margin),
        [(4, n, n), (4, n, h)] + [(4, margin, n + h)] * n_row,
        [VMEM, VMEM],
        grads,
        limits,
    )
    got = []
    for i, pairs in enumerate(row_rounds):
        got.append(lax.ppermute(sends[i], "row", pairs))
    total, send_e, send_o = call(
        functools.partial(fold_rows_kernel, n_row, margin),
        [(4, n, n), (2, n, h), (2, n, h)],
        [VMEM] * (2 + n_row),
        own,
        strip,
        *got,
    )
    send_e = lax.ppermute(send_e, "col", col_rounds[0])
    send_o = lax.ppermute(send_o, "col", col_rounds[1])
    (grad,) = call(fold_cols_kernel, [(4, n, n)], [VMEM] * 3, total, send_e, send_o)
    return (grad.reshape(2, 2, tile, tile), probe_grad)


def solution(mesh):
    placed = (
        P(None, None, "row", "col"),
        P(),
        P(),
        P("row", "col", None, None, None),
        P("row", "col", None, None),
    )
    return jax.shard_map(
        whole,
        mesh=mesh,
        in_specs=placed,
        out_specs=(P(None, None, "row", "col"), P()),
        check_vma=False,
    )
```

```python
import functools
import math

import jax
import jax.numpy as jnp
import numpy as np
from jax import lax
from jax.experimental import pallas as pl
from jax.experimental.pallas import tpu as pltpu
from jax.sharding import PartitionSpec as P


EPS_AMP = 0.5
F32 = jnp.float32
BF16 = jnp.bfloat16
VMEM = pl.BlockSpec(memory_space=pltpu.VMEM)
SMEM = pl.BlockSpec(memory_space=pltpu.SMEM)
HBM = pl.BlockSpec(memory_space=pltpu.HBM)


def split_np(table):
    high = table.astype(BF16)
    low = (table - high.astype(np.float64)).astype(BF16)
    return [high, low]


def dft_constants(n):
    h = n // 2
    k = np.arange(h)
    even = np.exp(-2j * np.pi * ((k[:, None] * k[None, :]) % h) / h) / np.sqrt(n)
    odd = even * np.exp(-2j * np.pi * k / n)[None, :]
    real = [np.block([[m.real, -m.imag], [m.imag, m.real]]) for m in (even, odd)]
    return np.stack(split_np(real[0])), np.stack(split_np(real[1]) + split_np(real[1].T))


def split(x):
    high = x.astype(BF16)
    return high, (x - high.astype(F32)).astype(BF16)


def dot(a, b):
    return jnp.dot(a, b, preferred_element_type=F32)


def left_dot(mats, which, x):
    high, low = split(x)
    n = x.shape[0]
    y = dot(mats[which : which + 2].reshape(2 * n, n), high)
    return y[:n] + (y[n:] + dot(mats[which], low))


def right_dot(x, mats, which):
    high, low = split(x)
    m = x.shape[0]
    y = dot(jnp.concatenate([high, low], axis=0), mats[which])
    return y[:m] + (y[m:] + dot(high, mats[which + 1]))


def cat(parts, axis):
    return jnp.concatenate(parts, axis=axis)


def product(a, b):
    return (a[0] * b[0] - a[1] * b[1], a[0] * b[1] + a[1] * b[0])


def conj_product(a, b):
    return (a[0] * b[0] + a[1] * b[1], a[0] * b[1] - a[1] * b[0])


class Dft:
    def __init__(self, mats, n):
        self.mats, self.h = mats, n // 2

    def left(self, x):
        h = self.h
        u = left_dot(self.mats, 0, cat([p[:h] + p[h:] for p in x], 0))
        v = left_dot(self.mats, 4, cat([p[:h] - p[h:] for p in x], 0))
        return [cat([u[:h], v[:h]], 0), cat([u[h:], v[h:]], 0)]

    def right(self, x):
        h = self.h
        u = right_dot(cat([p[:, :h] + p[:, h:] for p in x], 1), self.mats, 2)
        v = right_dot(cat([p[:, :h] - p[:, h:] for p in x], 1), self.mats, 6)
        return [cat([u[:, :h], v[:, :h]], 1), cat([u[:, h:], v[:, h:]], 1)]

    def right_inverse(self, x):
        h = self.h
        u = right_dot(cat([p[:, :h] for p in x], 1), self.mats, 0)
        v = right_dot(cat([p[:, h:] for p in x], 1), self.mats, 4)
        return [cat([e + o, e - o], 1) for e, o in ((u[:, :h], v[:, :h]), (u[:, h:], v[:, h:]))]

    def left_inverse(self, x):
        h = self.h
        u = left_dot(self.mats, 2, cat([p[:h] for p in x], 0))
        v = left_dot(self.mats, 6, cat([p[h:] for p in x], 0))
        return [cat([e + o, e - o], 0) for e, o in ((u[:h], v[:h]), (u[h:], v[h:]))]


SIN = [(-1.0) ** i / math.factorial(2 * i + 1) for i in range(7)]
COS = [(-1.0) ** i / math.factorial(2 * i) for i in range(7)]


def series(coefficients, z):
    total = coefficients[-1]
    for c in coefficients[-2::-1]:
        total = total * z + c
    return total


def cos_sin(x):
    y = 0.5 * x
    z = y * y
    s, c = y * series(SIN, z), series(COS, z)
    return 1.0 - 2.0 * (s * s), 2.0 * (s * c)


def iota(shape, dim):
    return lax.broadcasted_iota(jnp.int32, shape, dim)


def dyn_roll(x, shift, axis):
    return pltpu.roll(x, shift, axis=axis)


def half_roll(x):
    return pltpu.roll(x, x.shape[-1] // 2, axis=x.ndim - 1)


def pack_cols(re, im):
    h = re.shape[1] // 2
    front = iota((re.shape[0], h), 1) < h // 2
    low = jnp.where(front, re[:, :h], half_roll(im[:, :h]))
    high = jnp.where(front, half_roll(im[:, h:]), re[:, h:])
    return low, high


def copy_all(sources, places, sems):
    copies = [
        pltpu.make_async_copy(a, b, sems.at[i]) for i, (a, b) in enumerate(zip(sources, places))
    ]
    for copy in copies:
        copy.start()
    return copies


def row_start(which, n, margin):
    even = lax.axis_index("row") % 2 == 0
    last = even if which == 0 else jnp.logical_not(even)
    return pl.multiple_of(jnp.where(last, n - margin, 0), 8)


def pack_kernel(margin, obj_hbm, obj, *refs):
    evens, odds, rows, sems = refs[:2], refs[2], refs[3:-1], refs[-1]
    n = obj.shape[1]
    copies = copy_all((obj_hbm.at[0:2], obj_hbm.at[2:4]), (obj.at[0:2], obj.at[2:4]), sems)
    even = lax.axis_index("col") % 2 == 0
    for s in range(2):
        copies[s].wait()
        low, high = pack_cols(obj[2 * s], obj[2 * s + 1])
        strip = jnp.where(even, high, low)
        if s == 0:
            evens[0][:n] = strip
        else:
            evens[0][n:], evens[1][...] = strip[: n // 2], strip[n // 2 :]
        odds[s] = jnp.where(even, low, high)
    for which, out in enumerate(rows):
        out[...] = obj[:, pl.ds(row_start(which, n, margin), margin), :]


def corner_kernel(s, margin, *refs):
    evens, o, outs = refs[: s + 1], refs[s + 1], refs[s + 3 :]
    n = o.shape[1]
    for which, out in enumerate(outs):
        start = row_start(which, n, margin)
        if s == 0:
            out[0] = evens[0][pl.ds(start, margin), :]
        else:
            top, bottom = evens[0][n : n + margin], evens[1][n // 2 - margin :]
            out[0] = jnp.where(start == 0, top, bottom)
        out[1] = o[s, pl.ds(start, margin), :]


def even_odd(n, axis):
    h = n // 2
    natural, sorted_ = iota((n, n), axis), iota((n, n), 1 - axis)
    source = jnp.where(sorted_ < h, 2 * sorted_, 2 * (sorted_ - h) + 1)
    return (natural == source).astype(F32).astype(BF16)


def reorder(x, order):
    def thirds(y):
        a = y.astype(BF16)
        return (a,) + split(y - a.astype(F32))

    a, b, c = thirds(x)
    a, b, c = thirds(dot(order[1], a) + (dot(order[1], b) + dot(order[1], c)))
    return dot(a, order[0]) + (dot(b, order[0]) + dot(c, order[0]))


def prep_kernel(margin, *refs):
    hbm, (offs, limits, kr, ki, mats, *loaded) = refs[:6], refs[6:13]
    phase, table, sems = refs[13:]
    n = phase.shape[0]
    h = n // 2
    first = pltpu.make_async_copy(hbm[0], phase, sems.at[0])
    first.start()
    order = [even_odd(n, axis) for axis in range(2)]
    first.wait()
    copies = copy_all(hbm[1:], (table, mats.at[4:8], *loaded, offs), sems)
    angle = reorder(phase[...], order)
    kr[...], ki[...] = cos_sin(angle)
    copies[0].wait()
    for i in range(2):
        mats[i] = table[i]
        mats[2 + i, :h, :h] = table[i, :h, :h]
        mats[2 + i, :h, h:] = -table[i, :h, h:]
        mats[2 + i, h:, :h] = -table[i, h:, :h]
        mats[2 + i, h:, h:] = table[i, h:, h:]
    for copy in copies[1:]:
        copy.wait()
    for i in range(2):
        limits[i] = jnp.full(limits.shape[1:], offs[0, i] - margin, jnp.int32)


def reorder_kernel(x, after, out):
    out[...] = reorder(x[...], [even_odd(x.shape[0], axis) for axis in range(2)])


def roll_kernel(margin, offs, probe, pr):
    n = probe.shape[1]
    sy = (offs[0, 0] - margin + n) % n
    sx = (offs[0, 1] - margin + n) % n
    for i in range(2):
        pr[i] = dyn_roll(dyn_roll(probe[i], sy, 0), sx, 1)


def merge_cols(own, e, o, limits):
    n = own[0].shape[1]
    h = n // 2
    even = lax.axis_index("col") % 2 == 0
    high, low = jnp.where(even, e, o), jnp.where(even, o, e)
    lane = iota((1, h), 1)
    from_high = lane < limits[1, 0:1]
    from_low = lane >= limits[1, 0:1] + h
    out = []
    for i in range(2):
        strip_high = high if i == 0 else half_roll(high)
        strip_low = low if i == 0 else half_roll(low)
        out.append(
            cat(
                [
                    jnp.where(from_high, strip_high, own[i][:, :h]),
                    jnp.where(from_low, strip_low, own[i][:, h:]),
                ],
                1,
            )
        )
    return out


def merge_kernel(s, obj, *refs):
    evens, (o, limits, out) = refs[: s + 1], refs[s + 1 :]
    n = obj.shape[1]
    e = cat([evens[0][n:], evens[1][...]], 0) if s else evens[0][:n]
    own = [obj[2 * s], obj[2 * s + 1]]
    out[0], out[1] = merge_cols(own, e, o[s], limits)


def window_of(main, s, halos, corners, limits, margin):
    n = main.shape[1]
    row_even = lax.axis_index("row") % 2 == 0
    blocks = []
    for halo, corner in zip(halos, corners):
        own = [halo[2 * s], halo[2 * s + 1]]
        blocks.append(merge_cols(own, corner[0], corner[1], limits))
    row = iota((margin, n), 0)
    limit = cat([limits[0, 0:1]] * 2, 1)
    take_high = row < limit
    take_low = row >= limit + margin
    out = []
    for i in range(2):
        e = blocks[0][i]
        o = blocks[1][i] if len(blocks) == 2 else jnp.zeros_like(e)
        high, low = jnp.where(row_even, e, o), jnp.where(row_even, o, e)
        out.append(
            cat(
                [
                    jnp.where(take_high, high, main[i, :margin]),
                    main[i, margin : n - margin],
                    jnp.where(take_low, low, main[i, n - margin :]),
                ],
                0,
            )
        )
    return out


def unpack(n_row, refs):
    return refs[0], refs[1 : 1 + n_row], refs[1 + n_row : 1 + 2 * n_row], refs[1 + 2 * n_row :]


def through(dft, x, re, im):
    return dft.right_inverse(product([re, im], dft.right(x)))


def arrive_kernel(n_row, margin, *refs):
    main, halos, corners, refs = unpack(n_row, refs)
    limits, pr, kr, ki, mats, w1, arrive = refs
    n = main.shape[1]
    dft = Dft(mats, n)
    win = window_of(main, 0, halos, corners, limits, margin)
    w1[0], w1[1] = win
    x = dft.left(product([pr[0], pr[1]], win))
    x = through(dft, x, kr[...], ki[...])
    arrive[0], arrive[1] = dft.left_inverse(x)


def back_kernel(n_row, margin, *refs):
    main, halos, corners, refs = unpack(n_row, refs)
    limits, offs_hbm, pr, kr, ki, am, w1, arrive, mats = refs[:9]
    keep, give, grads, offs, sem = refs[9:]
    scalars = pltpu.make_async_copy(offs_hbm, offs, sem)
    scalars.start()
    n = main.shape[1]
    dft = Dft(mats, n)
    win = window_of(main, 1, halos, corners, limits, margin)
    x = dft.left(product([arrive[0], arrive[1]], win))
    far = dft.right(x)
    modulus = jnp.sqrt(far[0] * far[0] + far[1] * far[1] + EPS_AMP)
    factor = 2.0 * (1.0 - am[...] / modulus)
    x = dft.right_inverse([factor * far[0], factor * far[1]])
    back_far = dft.left_inverse(x)
    grads[2], grads[3] = conj_product([arrive[0], arrive[1]], back_far)
    x = dft.left(conj_product(win, back_far))
    x = through(dft, x, kr[...], -ki[...])
    x = dft.left_inverse(x)
    grads[0], grads[1] = conj_product([pr[0], pr[1]], x)
    grad = conj_product([w1[0], w1[1]], x)
    scalars.wait()
    sy = (margin - offs[0, 0] + n) % n
    sx = (margin - offs[0, 1] + n) % n
    grad = [dyn_roll(dyn_roll(g, sy, 0), sx, 1) for g in grad]
    even = lax.axis_index("row") % 2 == 0
    keep[...] = jnp.where(even, grad[0], grad[1])
    give[...] = jnp.where(even, grad[1], grad[0])


def divide_kernel(margin, grads, limits, own, strip, *sends):
    for s in range(2):
        split_grad([grads[2 * s], grads[2 * s + 1]], s, limits, margin, own, strip, sends)


def split_grad(grad, s, limits, margin, own, strip, sends):
    n = grad[0].shape[0]
    h = n // 2
    row_even = lax.axis_index("row") % 2 == 0
    lane = iota((1, h), 1)
    to_high, to_low = lane < limits[1, 0:1], lane >= limits[1, 0:1] + h
    front = lane < h // 2
    spill = jnp.where(front, to_high.astype(jnp.int32), to_low.astype(jnp.int32)) != 0
    for i in range(2):
        g = grad[i]
        row = iota((n, h), 0)
        high_rows = row < limits[0, 0:1]
        low_rows = row >= limits[0, 0:1] + n
        inner = jnp.logical_not(jnp.logical_or(high_rows, low_rows))
        left = jnp.where(to_high, 0.0, g[:, :h])
        right = jnp.where(to_low, 0.0, g[:, h:])
        side = jnp.where(spill, jnp.where(front, g[:, :h], g[:, h:]), 0.0)
        pieces = [left, right, side]
        own[2 * s + i, :, :h] = jnp.where(inner, left, 0.0)
        own[2 * s + i, :, h:] = jnp.where(inner, right, 0.0)
        strip[2 * s + i] = jnp.where(inner, side, 0.0)
        for j, piece in enumerate(pieces):
            top = jnp.where(high_rows[:margin], piece[:margin], 0.0)
            bottom = jnp.where(low_rows[n - margin :], piece[n - margin :], 0.0)
            for which, send in enumerate(sends):
                first = row_even if which == 0 else jnp.logical_not(row_even)
                send[2 * s + i, :, j * h : (j + 1) * h] = jnp.where(first, top, bottom)


def fold_rows_kernel(n_row, margin, own, strip, *refs):
    got, (total, send_e, send_o) = refs[:n_row], refs[n_row:]
    row_even = lax.axis_index("row") % 2 == 0
    col_even = lax.axis_index("col") % 2 == 0
    n = own.shape[1]
    h = n // 2
    front = iota((n, h), 1) < h // 2
    for s in range(2):
        strips = []
        for i in range(2 * s, 2 * s + 2):
            total[i] = own[i]
            r = got[0][i]
            q = got[1][i] if n_row == 2 else jnp.zeros_like(r)
            top, bottom = jnp.where(row_even, q, r), jnp.where(row_even, r, q)
            total[i, :margin] += top[:, :n]
            total[i, n - margin :] += bottom[:, :n]
            st = strip[i]
            strips.append(
                cat(
                    [
                        st[:margin] + top[:, n:],
                        st[margin : n - margin],
                        st[n - margin :] + bottom[:, n:],
                    ],
                    0,
                )
            )
        moved = half_roll(strips[1])
        to_high = jnp.where(front, strips[0], moved)
        to_low = jnp.where(front, moved, strips[0])
        send_e[s] = jnp.where(col_even, to_high, to_low)
        send_o[s] = jnp.where(col_even, to_low, to_high)


def fold_cols_kernel(total, e, o, out):
    col_even = lax.axis_index("col") % 2 == 0
    n = total.shape[1]
    h = n // 2
    front = iota((n, h), 1) < h // 2
    for s in range(2):
        high = jnp.where(col_even, e[s], o[s])
        low = jnp.where(col_even, o[s], e[s])
        for i in range(2):
            a = low if i == 0 else half_roll(low)
            b = high if i == 0 else half_roll(high)
            at = 2 * s + i
            out[at, :, :h] = total[at, :, :h] + jnp.where(front, a, 0.0)
            out[at, :, h:] = total[at, :, h:] + jnp.where(front, 0.0, b)


def in_hbm(x):
    return pltpu.with_memory_space_constraint(x, pltpu.HBM)


def call(kernel, shapes, in_specs, *args, scratch=(), mib=16):
    shapes = [s if isinstance(s, jax.ShapeDtypeStruct) else jax.ShapeDtypeStruct(s, F32) for s in shapes]
    return pl.pallas_call(
        kernel,
        out_shape=shapes,
        in_specs=in_specs,
        out_specs=[SMEM if s.shape == (1, 2) else VMEM for s in shapes],
        scratch_shapes=list(scratch),
        compiler_params=pltpu.CompilerParams(vmem_limit_bytes=mib << 20),
    )(*args)


def edges(axis):
    count = lax.axis_size(axis)
    rounds = []
    for first in (0, 1):
        pairs = [(i, i + 1) for i in range(first, count - 1, 2)]
        pairs += [(b, a) for a, b in pairs]
        if pairs:
            rounds.append(pairs)
    return rounds


def swap(value, axis, distance):
    count = lax.axis_size(axis)
    return lax.ppermute(value, axis, [(i, i ^ distance) for i in range(count)])


def groups():
    cols = [("col", 1 << b) for b in range(lax.axis_size("col").bit_length() - 1)]
    rows = [("row", 1 << b) for b in range(1, lax.axis_size("row").bit_length() - 1)]
    first, rest = cols[:2], cols[2:]
    pairs = [first]
    for bits in (rest, rows):
        pairs += [bits[i : i + 2] for i in range(0, len(bits), 2)]
    out = []
    for pair in pairs:
        axis, masks = pair[0][0], [m for _, m in pair]
        out.append((axis, [0] + masks + ([sum(masks)] if len(masks) == 2 else [])))
    return out


def pair_sum(parts):
    while len(parts) > 1:
        parts = [parts[i] + parts[i + 1] for i in range(0, len(parts), 2)]
    return parts[0]


def share_kernel(quad, stride, keep, other, *parts):
    place = lax.axis_index("col") // stride % quad
    chunk = keep.shape[0] // quad
    for j, part in enumerate(parts):
        rows = pl.ds(pl.multiple_of((place ^ j) * chunk, 8), chunk)
        part[...] = keep[rows, :] + other[rows, :]


def sum_kernel(*refs):
    refs[-1][...] = pair_sum([r[...] for r in refs[:-1]])


def join_kernel(stride, *refs):
    parts, full = refs[:-1], refs[-1]
    quad, chunk = len(parts), parts[0].shape[0]
    place = lax.axis_index("col") // stride % quad
    for j, part in enumerate(parts):
        full[pl.ds(pl.multiple_of((place ^ j) * chunk, 8), chunk), :] = part[...]


def half_kernel(full, out, sem):
    copy = pltpu.make_async_copy(full, out.at[lax.axis_index("row") % 2], sem)
    copy.start()
    copy.wait()


def other_kernel(started, other, out, sem):
    copy = pltpu.make_async_copy(other, out.at[1 - lax.axis_index("row") % 2], sem)
    copy.start()
    copy.wait()


def reduce_probe(keep, give):
    n = keep.shape[0]
    (_, offsets), *rest = groups()
    quad, stride = len(offsets), offsets[1]
    chunk = n // quad
    other = swap(give, "row", 1)
    parts = call(
        functools.partial(share_kernel, quad, stride),
        [(chunk, n)] * quad,
        [VMEM] * 2,
        keep,
        other,
    )
    sums = [parts[0]]
    for j in range(1, quad):
        sums.append(swap(parts[j], "col", offsets[j]))
    (total,) = call(sum_kernel, [(chunk, n)], [VMEM] * quad, *sums)
    for axis, masks in rest:
        sums = [total]
        for mask in masks[1:]:
            sums.append(swap(total, axis, mask))
        (total,) = call(sum_kernel, [(chunk, n)], [VMEM] * len(sums), *sums)
    parts = [total]
    for j in range(1, quad):
        parts.append(swap(total, "col", offsets[j]))
    (full,) = call(
        functools.partial(join_kernel, stride), [(n, n)], [VMEM] * quad, *parts
    )
    other = swap(full, "row", 1)
    out = dict(
        out_shape=jax.ShapeDtypeStruct((2, n, n), F32),
        out_specs=HBM,
        scratch_shapes=[pltpu.SemaphoreType.DMA(())],
        compiler_params=pltpu.CompilerParams(vmem_limit_bytes=16 << 20),
    )
    grad = pl.pallas_call(half_kernel, in_specs=[VMEM], **out)(full)
    return pl.pallas_call(
        other_kernel, in_specs=[HBM, VMEM], input_output_aliases={0: 0}, **out
    )(grad, other)


def whole(object_field, probe, phase, amplitudes, offsets):
    tile = object_field.shape[2]
    n = probe.shape[1]
    h = n // 2
    margin = n // 4
    even, odd = [jnp.asarray(t) for t in dft_constants(n)]

    row_rounds, col_rounds = edges("row"), edges("col")
    n_row = len(row_rounds)
    obj, even0, even1, odds, *rows = call(
        functools.partial(pack_kernel, margin),
        [(4, n, n)]
        + [(n + n // 2, h), (n // 2, h), (2, n, h)]
        + [(4, margin, n)] * n_row,
        [HBM],
        in_hbm(object_field.reshape(4, tile, tile)),
        scratch=[pltpu.SemaphoreType.DMA((2,))],
    )
    halos, corners = [], [[], []]
    even0 = lax.ppermute(even0, "col", col_rounds[0])
    odds = lax.ppermute(odds, "col", col_rounds[1])
    even1 = lax.ppermute(even1, "col", col_rounds[0])
    for i, pairs in enumerate(row_rounds):
        halos.append(lax.ppermute(rows[i], "row", pairs))
    evens = (even0, even1)

    def cut(s, after):
        parts = call(
            functools.partial(corner_kernel, s, margin),
            [(2, margin, h)] * n_row,
            [VMEM] * (3 + s),
            *evens[: s + 1],
            odds,
            after,
        )
        for i, pairs in enumerate(row_rounds):
            corners[s].append(lax.ppermute(parts[i], "row", pairs))

    def merge(s):
        (main,) = call(
            functools.partial(merge_kernel, s),
            [(2, n, n)],
            [VMEM] * (4 + s),
            obj,
            *evens[: s + 1],
            odds,
            limits,
        )
        return main

    loads = (phase, even, odd, probe, amplitudes.reshape(n, n), offsets.reshape(1, 2))
    offs, limits, kr, ki, mats, pr, am = call(
        functools.partial(prep_kernel, margin),
        [jax.ShapeDtypeStruct((1, 2), jnp.int32), jax.ShapeDtypeStruct((2, 8, h), jnp.int32)]
        + [(n, n)] * 2
        + [jax.ShapeDtypeStruct((8, n, n), BF16)]
        + [jax.ShapeDtypeStruct(x.shape, x.dtype) for x in loads[3:-1]],
        [HBM] * len(loads),
        *[in_hbm(x) for x in loads],
        scratch=[
            pltpu.VMEM((n, n), F32),
            pltpu.VMEM((2, n, n), BF16),
            pltpu.SemaphoreType.DMA((len(loads),)),
        ],
    )
    (pr,) = call(functools.partial(roll_kernel, margin), [(2, n, n)], [SMEM, VMEM], offs, pr)
    (am,) = call(reorder_kernel, [(n, n)], [VMEM] * 2, am, pr)
    cut(0, am)
    main = merge(0)
    cut(1, main)
    w1, arrive = call(
        functools.partial(arrive_kernel, n_row, margin),
        [(2, n, n), (2, n, n)],
        [VMEM] * (6 + 2 * n_row),
        main,
        *halos,
        *corners[0],
        limits,
        pr,
        kr,
        ki,
        mats,
    )
    main = merge(1)
    keep, give, grads = call(
        functools.partial(back_kernel, n_row, margin),
        [(n, n), (n, n), (4, n, n)],
        [VMEM] * (2 + 2 * n_row) + [HBM] + [VMEM] * 7,
        main,
        *halos,
        *corners[1],
        limits,
        in_hbm(offsets.reshape(1, 2)),
        pr,
        kr,
        ki,
        am,
        w1,
        arrive,
        mats,
        scratch=[pltpu.SMEM((1, 2), jnp.int32), pltpu.SemaphoreType.DMA(())],
        mib=40,
    )
    probe_grad = reduce_probe(keep, give)
    own, strip, *sends = call(
        functools.partial(divide_kernel, margin),
        [(4, n, n), (4, n, h)] + [(4, margin, n + h)] * n_row,
        [VMEM, VMEM],
        grads,
        limits,
    )
    got = []
    for i, pairs in enumerate(row_rounds):
        got.append(lax.ppermute(sends[i], "row", pairs))
    total, send_e, send_o = call(
        functools.partial(fold_rows_kernel, n_row, margin),
        [(4, n, n), (2, n, h), (2, n, h)],
        [VMEM] * (2 + n_row),
        own,
        strip,
        *got,
    )
    send_e = lax.ppermute(send_e, "col", col_rounds[0])
    send_o = lax.ppermute(send_o, "col", col_rounds[1])
    (grad,) = call(fold_cols_kernel, [(4, n, n)], [VMEM] * 3, total, send_e, send_o)
    return (grad.reshape(2, 2, tile, tile), probe_grad)


def solution(mesh):
    placed = (
        P(None, None, "row", "col"),
        P(),
        P(),
        P("row", "col", None, None, None),
        P("row", "col", None, None),
    )
    return jax.shard_map(
        whole,
        mesh=mesh,
        in_specs=placed,
        out_specs=(P(None, None, "row", "col"), P()),
        check_vma=False,
    )
```
